32 devices in a mesh: grp: 2 (over x), wide: 16 (over z, y, core).
Axes of the slice: x: 2, y: 2, z: 4, core: 2. Of those that a mesh axis runs over, the one named last changes fastest.
Arguments:
- qkv: bfloat16 [4096, 3456], P(('grp', 'wide')), parts along dimension 0, may hold values from -51.854497 to 51.854497
- grid: int32 [4, 2], P('grp'), parts along dimension 0, may hold values from 2 to 512, as said below
- w_out: bfloat16 [1152, 1152], replicated, may hold values from -0.1875 to 0.1875
- ln_gain: float32 [4608], replicated, may hold values from 0.1 to 1.9
- ln_bias: float32 [4608], replicated, may hold values from -3 to 3
- w_merge: bfloat16 [4608, 2048], P('wide'), may hold values from -0.09375 to 0.09375
- w_router: bfloat16 [2048, 8], replicated, may hold values from -0.125 to 0.125
- expert_ids: int32 [1024, 6], P(('grp', 'wide')), parts along dimension 0, may hold values from 0 to 7, as said below
- slot_pos: int32 [1024, 6], P(('grp', 'wide')), parts along dimension 0, may hold values from 0 to 31, as said below
- w_gate: bfloat16 [16, 2048, 704], P('wide'), may hold values from -0.125 to 0.125
- w_up: bfloat16 [16, 2048, 704], P('wide'), may hold values from -0.125 to 0.125
- w_down: bfloat16 [16, 704, 2048], P('wide'), may hold values from -0.15625 to 0.15625
Outputs:
- moe_out: bfloat16 [1024, 2048], P(('grp', 'wide')), parts along dimension 0
The draws below stay inside these ranges and needn't reach their ends.
There are 2 independent parts, one for each index of `grp`. The reference program is written for one: setup_inputs(seed, part) draws one part's arguments, and reference() takes and returns one part's arrays. A program takes and returns all parts, laid end to end along the dimension named above; an argument that names none is the same for every part. Nothing has to cross between parts.
Inputs may be any that keep to these rules, and one draw needn't show every extreme that they name: `expert_ids`: each row names 6 different experts. Among the rows of one device no expert is named more than 32 times, and one expert is named exactly 32 times by the rows of every device. `slot_pos`: among the rows of one device, the pairs naming expert e take the slots 0, 1, ... up to the number of such pairs minus one, each once. `grid`: both numbers are even; one clip's product equals 1024, and every other clip's product lies between 512 and 768.
All inputs are finite; a program needn't handle non-finite values.
Results may differ from the reference program's by a relative error of at most 0.023.
Values may be sent and summed in bfloat16 or wider, within the bound.
A program may use at most 128 MiB of HBM per device.

```python
import jax
import jax.numpy as jnp
from jax import lax

D_VIT = 1152
HEADS = 16
D_LLM = 2048
FFE = 1408
TOPK = 6
CLIPS = 2
MERGE_W = 4608
PATCHES = 2048
CLIP_LEN = 1024
MT_DEV = 32
EXPERTS = 8
CAP = 32
N_WIDE = 16


def draw_qkv(key, part):
    vit_width = D_VIT
    streams = jax.random.split(key, 2)
    paired = 1.4 * jax.random.truncated_normal(streams[0], -4.0, 4.0, (PATCHES, 2 * vit_width), jnp.float32)
    values = jax.random.truncated_normal(streams[1], -4.0, 4.0, (PATCHES, vit_width), jnp.float32)
    return jnp.concatenate([paired, values], axis=1).astype(jnp.bfloat16)


def draw_grid(key, part):
    streams = jax.random.split(jax.random.fold_in(key, 11), 3)
    quarter = CLIP_LEN // 4
    levels = quarter.bit_length() - 1
    lowest = levels // 3
    highest = levels - levels // 3
    exponent = jax.random.randint(streams[0], (CLIPS,), lowest, highest + 1)
    half_width = jnp.left_shift(jnp.ones((CLIPS,), jnp.int32), exponent)
    most_rows = quarter // half_width
    least_rows = (most_rows + 1) // 2
    upper_rows = 3 * most_rows // 4
    half_height = least_rows + jax.random.randint(streams[1], (CLIPS,), 0, 1 << 20) % (upper_rows - least_rows + 1)
    full_clip = jax.random.randint(streams[2], (), 0, CLIPS)
    is_full = jnp.arange(CLIPS, dtype=jnp.int32) == full_clip
    half_height = jnp.where(is_full, quarter, half_height)
    half_width = jnp.where(is_full, 1, half_width)
    return jnp.stack([2 * half_height, 2 * half_width], axis=1).astype(jnp.int32)


def routing(key):
    streams = jax.random.split(jax.random.fold_in(key, 29), 4)
    fair_load = MT_DEV * TOPK // EXPERTS
    extra_load = CAP - fair_load
    pair_count = EXPERTS // 2
    middle = (1 + jax.random.permutation(streams[0], EXPERTS - 2)).astype(jnp.int32)
    expert_order = jnp.concatenate([jnp.array([EXPERTS - 1], jnp.int32), middle[:1], jnp.array([0], jnp.int32), middle[1:]]).astype(jnp.int32)
    load_shift = jax.random.randint(streams[1], (N_WIDE, pair_count), 0, extra_load + 1)
    load_shift = load_shift.at[:, 0].set(extra_load)
    load_shift = load_shift.at[:, 1].set(extra_load)
    expert_loads = jnp.zeros((N_WIDE, EXPERTS), jnp.int32)
    expert_loads = expert_loads.at[:, expert_order[0::2]].set(fair_load + load_shift)
    expert_loads = expert_loads.at[:, expert_order[1::2]].set(fair_load - load_shift)
    load_ends = jnp.cumsum(expert_loads, axis=1)
    starts = load_ends - expert_loads
    flat_slots = jnp.arange(MT_DEV * TOPK, dtype=jnp.int32)
    owner_ids = jnp.sum((load_ends[:, None, :] <= flat_slots[None, :, None]).astype(jnp.int32), axis=2)
    place_ids = flat_slots[None, :] - jnp.take_along_axis(starts, owner_ids, axis=1)
    owner_ids = owner_ids.reshape(N_WIDE, TOPK, MT_DEV).transpose(0, 2, 1)
    place_ids = place_ids.reshape(N_WIDE, TOPK, MT_DEV).transpose(0, 2, 1)
    row_order = jax.vmap(lambda stream: jax.random.permutation(stream, MT_DEV))(jax.random.split(streams[2], N_WIDE)).astype(jnp.int32)
    owner_ids = jnp.take_along_axis(owner_ids, row_order[:, :, None], axis=1)
    place_ids = jnp.take_along_axis(place_ids, row_order[:, :, None], axis=1)
    column_score = jax.random.randint(streams[3], (N_WIDE, MT_DEV, TOPK), 0, 1 << 20) * TOPK + jnp.arange(TOPK, dtype=jnp.int32)
    column_order = jnp.argsort(column_score, axis=2).astype(jnp.int32)
    owner_ids = jnp.take_along_axis(owner_ids, column_order, axis=2)
    place_ids = jnp.take_along_axis(place_ids, column_order, axis=2)
    return (owner_ids.reshape(N_WIDE * MT_DEV, TOPK).astype(jnp.int32), place_ids.reshape(N_WIDE * MT_DEV, TOPK).astype(jnp.int32))


def draw_expert_ids(key, part):
    return routing(key)[0]


def draw_slot_pos(key, part):
    return routing(key)[1]


def shard_levels(stream_key, shape, pieces, least, largest):
    def one(dim, blocks):
        steps = jax.random.uniform(jax.random.fold_in(jax.random.fold_in(stream_key, 6), dim), (blocks,), jnp.float32, least / len(pieces), largest / len(pieces))
        return jnp.repeat(jnp.exp(steps), shape[dim] // blocks).reshape((-1,) + (1,) * (len(shape) - dim - 1))

    level = one(*pieces[0])
    for cut in pieces[1:]:
        level = level * one(*cut)
    return level


def gaussian(own_key, extent, width, bound, shards=(), kind=jnp.bfloat16):
    result = width * jax.random.normal(own_key, extent, jnp.float32)
    if shards:
        result = result * shard_levels(own_key, extent, shards, -0.22, 0.18)
    return jnp.clip(result, -bound, bound).astype(kind)


def setup_inputs(seed: int = 0, part: int = 0) -> dict:
    seeds = jax.random.split(jax.random.key(seed), 13)
    part_keys = jax.random.split(jax.random.fold_in(seeds[12], part), 13)
    qkv = draw_qkv(jax.random.fold_in(jax.random.fold_in(seeds[12], part), 71), part)
    grid = draw_grid(jax.random.fold_in(jax.random.fold_in(seeds[12], part), 71), part)
    w_out = gaussian(seeds[2], (D_VIT, D_VIT), D_VIT ** -0.5, 0.1875)
    ln_gain = jnp.clip(1.0 + 0.18 * jax.random.normal(seeds[3], (MERGE_W,), jnp.float32), 0.1, 1.9)
    ln_bias = gaussian(seeds[4], (MERGE_W,), 0.5, 3.0, (), jnp.float32)
    w_merge = gaussian(seeds[5], (MERGE_W, D_LLM), MERGE_W ** -0.5, 0.09375, ((0, 16),))
    w_router = gaussian(seeds[6], (D_LLM, EXPERTS), D_LLM ** -0.5, 0.125)
    expert_ids = draw_expert_ids(jax.random.fold_in(jax.random.fold_in(seeds[12], part), 71), part)
    slot_pos = draw_slot_pos(jax.random.fold_in(jax.random.fold_in(seeds[12], part), 71), part)
    w_gate = gaussian(seeds[9], (2 * EXPERTS, D_LLM, FFE // 2), D_LLM ** -0.5, 0.125, ((0, 16),))
    w_up = gaussian(seeds[10], (2 * EXPERTS, D_LLM, FFE // 2), D_LLM ** -0.5, 0.125, ((0, 16),))
    w_down = gaussian(seeds[11], (2 * EXPERTS, FFE // 2, D_LLM), FFE ** -0.5, 0.15625, ((0, 16),))
    return {"qkv": qkv, "grid": grid, "w_out": w_out, "ln_gain": ln_gain, "ln_bias": ln_bias, "w_merge": w_merge, "w_router": w_router, "expert_ids": expert_ids, "slot_pos": slot_pos, "w_gate": w_gate, "w_up": w_up, "w_down": w_down}


route_scale = 2.446
norm_eps = 1e-05

def attend(operands):
    query_rows, key_rows, value_rows, patch_count = operands
    head_dim = query_rows.shape[1]
    visible = jnp.arange(key_rows.shape[0], dtype=jnp.int32) < patch_count
    block_size = min(1024, query_rows.shape[0])

    def one_block(query_block):
        scores = jnp.dot(query_block, key_rows.T, preferred_element_type=jnp.float32) * head_dim ** (-0.5)
        scores = jnp.where(visible[None, :], scores, -jnp.inf)
        highest = lax.optimization_barrier(jnp.max(scores, axis=1, keepdims=True))
        weights = jnp.exp(scores - highest)
        running = lax.optimization_barrier(jnp.sum(weights, axis=1, keepdims=True))
        mixture = jnp.dot(weights.astype(jnp.bfloat16), value_rows, preferred_element_type=jnp.float32)
        return (mixture / running).astype(jnp.bfloat16)
    blocks = query_rows.reshape(-1, block_size, head_dim)
    return lax.map(one_block, blocks).reshape(query_rows.shape[0], head_dim)

def reference(qkv, grid, w_out, ln_gain, ln_bias, w_merge, w_router, expert_ids, slot_pos, w_gate, w_up, w_down):
    vit_width = w_out.shape[0]
    head_dim = vit_width // HEADS
    patch_total = qkv.shape[0]

    def heads_of(columns):
        return columns.reshape(CLIPS, CLIP_LEN, HEADS, head_dim).transpose(0, 2, 1, 3).reshape(CLIPS * HEADS, CLIP_LEN, head_dim)
    patch_counts = jnp.repeat((grid[:, 0] * grid[:, 1]).astype(jnp.int32), HEADS)
    attended = lax.map(attend, (heads_of(qkv[:, :vit_width]), heads_of(qkv[:, vit_width:2 * vit_width]), heads_of(qkv[:, 2 * vit_width:]), patch_counts))
    attention = attended.reshape(CLIPS, HEADS, CLIP_LEN, head_dim).transpose(0, 2, 1, 3).reshape(patch_total, vit_width)
    projected = jnp.dot(attention, w_out, preferred_element_type=jnp.float32).astype(jnp.bfloat16)
    merged = projected.reshape(patch_total // 4, 4 * vit_width).astype(jnp.float32)
    centre = lax.optimization_barrier(jnp.mean(merged, axis=1, keepdims=True))
    centered = merged - centre
    spread = lax.optimization_barrier(jnp.mean(centered * centered, axis=1, keepdims=True))
    normed = (centered * lax.rsqrt(spread + norm_eps) * ln_gain + ln_bias).astype(jnp.bfloat16)
    tokens = jnp.dot(normed, w_merge, preferred_element_type=jnp.float32).astype(jnp.bfloat16)
    logits = jnp.dot(tokens, w_router, preferred_element_type=jnp.float32)
    chosen = jnp.take_along_axis(logits, expert_ids, axis=1)
    gate_values = jax.nn.sigmoid(chosen)
    route_weight = route_scale * gate_values / lax.optimization_barrier(jnp.sum(gate_values, axis=1, keepdims=True))
    token_count = tokens.shape[0]
    llm_width = tokens.shape[1]
    row_ids = jnp.arange(token_count, dtype=jnp.int32)
    block_ids = jnp.broadcast_to((row_ids // MT_DEV)[:, None], expert_ids.shape)
    owners = jnp.broadcast_to(row_ids[:, None], expert_ids.shape)
    slot_table = jnp.full((EXPERTS, N_WIDE, CAP), token_count, jnp.int32).at[expert_ids, block_ids, slot_pos].set(owners)
    slot_weight = jnp.zeros((EXPERTS, N_WIDE, CAP), jnp.float32).at[expert_ids, block_ids, slot_pos].set(route_weight)
    padded = jnp.concatenate([tokens, jnp.zeros((1, llm_width), jnp.bfloat16)], axis=0)
    half_width = w_gate.shape[2]
    gate_all = w_gate.reshape(EXPERTS, 2, llm_width, half_width)
    up_all = w_up.reshape(EXPERTS, 2, llm_width, half_width)
    down_all = w_down.reshape(EXPERTS, 2, half_width, llm_width)

    def add_expert(running, operands):
        index_table, weight_table, gate_pair, up_pair, down_pair = operands
        flat_index = index_table.reshape(-1)
        inputs = padded[flat_index]
        combined = jnp.zeros((flat_index.shape[0], llm_width), jnp.float32)
        for half_index in range(2):
            gate_part = jnp.dot(inputs, gate_pair[half_index], preferred_element_type=jnp.float32)
            up_part = jnp.dot(inputs, up_pair[half_index], preferred_element_type=jnp.float32)
            hidden = (jax.nn.silu(gate_part) * up_part).astype(jnp.bfloat16)
            product = jnp.dot(hidden, down_pair[half_index], preferred_element_type=jnp.float32).astype(jnp.bfloat16)
            combined = combined + lax.optimization_barrier(product).astype(jnp.float32)
        joined = lax.optimization_barrier(combined.astype(jnp.bfloat16)).astype(jnp.float32)
        return (running.at[flat_index].add(weight_table.reshape(-1, 1) * joined), None)
    running = jnp.zeros((token_count + 1, llm_width), jnp.float32)
    running = lax.scan(add_expert, running, (slot_table, slot_weight, gate_all, up_all, down_all))[0]
    return running[:token_count].astype(jnp.bfloat16)
```

```python
import functools

import jax
import jax.numpy as jnp
from jax import lax
from jax.experimental import pallas as pl
from jax.experimental.pallas import tpu as pltpu
from jax.sharding import PartitionSpec as P

HEADS = 16
CLIPS = 2


route_scale = 2.446
norm_eps = 1e-05


def swapped(value, axis, stride):
    mask = 2**stride
    pairs = [(source, source ^ mask) for source in range(lax.axis_size(axis))]
    return lax.ppermute(value, axis, pairs)


def ordered_pair(own_part, partner, upper_bit):
    return jnp.where(
        upper_bit == 1,
        jnp.concatenate([partner, own_part], 0),
        jnp.concatenate([own_part, partner], 0),
    )


def local(
    qkv,
    grid,
    w_out,
    ln_gain,
    ln_bias,
    w_merge,
    w_router,
    expert_ids,
    slot_pos,
    w_gate,
    w_up,
    w_down,
):
    devices = lax.axis_size("wide")
    position_self = lax.axis_index("wide")
    vit_width = w_out.shape[0]
    head_dim = vit_width // HEADS
    groups = devices // HEADS
    local_rows = qkv.shape[0]
    sub_rows = local_rows // groups
    per_clip = devices // CLIPS
    query_send = (
        qkv[:, :vit_width]
        .reshape(groups, sub_rows, HEADS, head_dim)
        .transpose(2, 0, 1, 3)
        .reshape(devices, sub_rows, head_dim)
    )
    key_value = jnp.concatenate(
        [
            qkv[:, vit_width : 2 * vit_width].reshape(local_rows, HEADS, head_dim),
            qkv[:, 2 * vit_width :].reshape(local_rows, HEADS, head_dim),
        ],
        axis=2,
    )
    spread_send = jnp.broadcast_to(
        key_value.transpose(1, 0, 2)[:, None], (HEADS, groups, local_rows, 2 * head_dim)
    ).reshape(devices, local_rows, 2 * head_dim)
    queries, key_rows = (
        lax.all_to_all(query_send, "wide", split_axis=0, concat_axis=0, tiled=True),
        lax.all_to_all(spread_send, "wide", split_axis=0, concat_axis=0, tiled=True),
    )
    key_rows = key_rows[None]
    key_groups = key_rows.shape[0]
    key_count = key_rows.shape[2]
    key_place = (
        jnp.arange(per_clip, dtype=jnp.int32)[None, :, None] * local_rows
        + jnp.arange(key_groups, dtype=jnp.int32)[:, None, None] * local_rows
        + jnp.arange(key_count, dtype=jnp.int32)[None, None, :]
    ).reshape(-1)
    patch_counts = grid[:, 0] * grid[:, 1]
    clip_queries = queries.reshape(CLIPS, per_clip * sub_rows, head_dim)
    query_block_rows = min(512, per_clip * sub_rows)
    score_scale = head_dim ** (-0.5)

    def attend(clip_index):
        key_block = lax.dynamic_slice_in_dim(key_rows, clip_index * per_clip, per_clip, 1).reshape(
            -1, 2 * head_dim
        )
        visible = key_place < lax.dynamic_index_in_dim(patch_counts, clip_index, 0, keepdims=False)
        query_all = lax.dynamic_index_in_dim(clip_queries, clip_index, 0, keepdims=False)

        def one_block(query_block):
            scores = (
                lax.dot_general(
                    query_block,
                    key_block[:, :head_dim],
                    (((1,), (1,)), ((), ())),
                    preferred_element_type=jnp.float32,
                )
                * score_scale
            )
            scores = jnp.where(visible[None, :], scores, -jnp.inf)
            highest = jnp.max(scores, axis=1, keepdims=True)
            weights = jnp.exp(scores - highest)
            running = jnp.sum(weights, axis=1, keepdims=True)
            mixture = jnp.dot(
                weights.astype(jnp.bfloat16),
                key_block[:, head_dim:],
                preferred_element_type=jnp.float32,
            )
            return (mixture / running).astype(jnp.bfloat16)

        return lax.map(one_block, query_all.reshape(-1, query_block_rows, head_dim)).reshape(
            -1, head_dim
        )

    attended = lax.map(attend, jnp.arange(CLIPS, dtype=jnp.int32))
    returned = lax.all_to_all(
        attended.reshape(devices, sub_rows, head_dim),
        "wide",
        split_axis=0,
        concat_axis=0,
        tiled=True,
    )
    attention = (
        returned.reshape(HEADS, groups, sub_rows, head_dim)
        .transpose(1, 2, 0, 3)
        .reshape(local_rows, vit_width)
    )
    projected = jnp.dot(attention, w_out, preferred_element_type=jnp.float32).astype(jnp.bfloat16)
    merged = projected.reshape(local_rows // 4, 4 * vit_width).astype(jnp.float32)
    centre = jnp.mean(merged, axis=1, keepdims=True)
    centered = merged - centre
    spread = jnp.mean(centered * centered, axis=1, keepdims=True)
    normed = (centered * lax.rsqrt(spread + norm_eps) * ln_gain + ln_bias).astype(jnp.bfloat16)
    tok_groups = min(8, devices)
    feat_groups = devices // tok_groups
    merge_rows = w_merge
    for bit_index in range(tok_groups.bit_length() - 1):
        partner = swapped(merge_rows, "wide", bit_index)
        upper_bit = position_self // (1 << bit_index) % 2
        merge_rows = ordered_pair(merge_rows, partner, upper_bit)
    token_count = normed.shape[0]
    part_rows = token_count // tok_groups
    feat_width = normed.shape[1] // feat_groups
    out_width = w_merge.shape[1]
    merge_send = (
        normed.reshape(tok_groups, part_rows, feat_groups, feat_width)
        .transpose(2, 0, 1, 3)
        .reshape(devices, part_rows, feat_width)
    )
    flat_rows = lax.all_to_all(merge_send, "wide", split_axis=0, concat_axis=0, tiled=True).reshape(
        -1, feat_width
    )
    partial_value = jnp.dot(flat_rows, merge_rows, preferred_element_type=jnp.float32).reshape(
        devices, -1, out_width
    )
    summed = lax.all_to_all(partial_value, "wide", split_axis=0, concat_axis=0, tiled=True)
    tokens = (
        jnp.sum(summed.reshape(feat_groups, tok_groups, part_rows, out_width), axis=0)
        .reshape(token_count, out_width)
        .astype(jnp.bfloat16)
    )
    logits = jnp.dot(tokens, w_router, preferred_element_type=jnp.float32)
    experts = w_router.shape[1]
    top_count = expert_ids.shape[1]
    matches = expert_ids[:, :, None] == jnp.arange(experts, dtype=jnp.int32)[None, None, :]
    chosen = jnp.sum(jnp.where(matches, logits[:, None, :], 0.0), axis=2)
    gate_values = jax.nn.sigmoid(chosen)
    route_weight = route_scale * gate_values / jnp.sum(gate_values, axis=1, keepdims=True)
    capacity = min(token_count, 2 * token_count * top_count // experts)
    slot_count = experts * capacity
    target = expert_ids * capacity + slot_pos
    one_hot = jnp.any(
        target[None, :, :] == jnp.arange(slot_count, dtype=jnp.int32)[:, None, None], axis=2
    ).astype(jnp.bfloat16)
    buffer = jnp.dot(one_hot, tokens, preferred_element_type=jnp.float32).astype(jnp.bfloat16)
    gate_half = w_gate[0]
    up_half = w_up[0]
    down_half = w_down[0]
    half_cap = capacity // 2
    dispatch = buffer.reshape(devices, half_cap, out_width)
    portion = lax.all_to_all(dispatch, "wide", split_axis=0, concat_axis=0, tiled=True)
    item_count = portion.shape[1]
    partner_rows = swapped(portion, "wide", 0)
    both_rows = jnp.concatenate([portion, partner_rows], axis=1)
    flat_rows = both_rows.reshape(-1, out_width)
    gate_part = jnp.dot(flat_rows, gate_half, preferred_element_type=jnp.float32)
    up_part = jnp.dot(flat_rows, up_half, preferred_element_type=jnp.float32)
    hidden = (jax.nn.silu(gate_part) * up_part).astype(jnp.bfloat16)
    product = (
        jnp.dot(hidden, down_half, preferred_element_type=jnp.float32)
        .astype(jnp.bfloat16)
        .reshape(devices, 2 * item_count, out_width)
    )
    from_partner = swapped(product[:, item_count:], "wide", 0)
    joined = (
        product[:, :item_count].astype(jnp.float32) + from_partner.astype(jnp.float32)
    ).astype(jnp.bfloat16)
    answers = lax.all_to_all(joined, "wide", split_axis=0, concat_axis=0, tiled=True)
    slot_result = answers.reshape(slot_count, out_width)
    slot_result = lax.optimization_barrier(slot_result)
    picked = jnp.take(slot_result, target.reshape(-1), axis=0).reshape(
        token_count, top_count, out_width
    )
    return jnp.sum(picked.astype(jnp.float32) * route_weight[:, :, None], axis=1).astype(
        jnp.bfloat16
    )


def remote(source, target, send_sem, recv_sem, place):
    return pltpu.make_async_remote_copy(
        src_ref=source,
        dst_ref=target,
        send_sem=send_sem,
        recv_sem=recv_sem,
        device_id={"wide": place},
        device_id_type=pl.DeviceIdType.MESH,
    )


def by_rows(left, right):
    return lax.dot_general(
        left, right, (((1,), (1,)), ((), ())), preferred_element_type=jnp.float32
    )


def greet(places):
    barrier = pltpu.get_barrier_semaphore()
    for place in places:
        pl.semaphore_signal(
            barrier, inc=1, device_id={"wide": place}, device_id_type=pl.DeviceIdType.MESH
        )
    return barrier


def vision_part(
    peers,
    head_dim,
    barrier,
    grid_ref,
    qkv_hbm,
    w_out_hbm,
    gain_ref,
    bias_ref,
    out_ref,
    qkv_ref,
    send,
    recv,
    keys,
    values,
    mixed_send,
    mixed_recv,
    attention,
    mixed,
    w_out_ref,
    send_sem,
    recv_sem,
    back_send_sem,
    back_recv_sem,
    local_sem,
    start_rest,
):
    place = lax.axis_index("wide")
    base = place // peers * peers
    me = place - base
    rows = qkv_ref.shape[0]
    width = w_out_hbm.shape[0]
    heads = HEADS // peers
    span = heads * head_dim
    devices = lax.axis_size("wide")
    qkv_copy = pltpu.make_async_copy(qkv_hbm, qkv_ref, local_sem.at[3])
    qkv_copy.start()
    weight_copy = pltpu.make_async_copy(w_out_hbm, w_out_ref, local_sem.at[0])
    weight_copy.start()
    qkv_copy.wait()
    for peer in range(peers):
        for part in range(3):
            start = part * width + peer * span
            send[peer, :, part * span : (part + 1) * span] = qkv_ref[:, start : start + span]
    pl.semaphore_wait(barrier, devices - 1)
    own = pltpu.make_async_copy(send.at[me], recv.at[me], local_sem.at[1])
    own.start()
    sends = []
    for step in range(1, peers):
        peer = lax.rem(me + step, peers)
        copy = remote(
            send.at[peer], recv.at[me], send_sem.at[peer], recv_sem.at[me], base + peer
        )
        copy.start()
        sends.append(copy)
    start_rest()
    own.wait()
    for step in range(1, peers):
        peer = lax.rem(me + step, peers)
        remote(
            send.at[peer], recv.at[peer], send_sem.at[peer], recv_sem.at[peer], base + peer
        ).wait_recv()
    for head in range(heads):
        low = span + head * head_dim
        keys[head] = recv[:, :, low : low + head_dim].reshape(peers * rows, head_dim)
        low = 2 * span + head * head_dim
        values[head] = recv[:, :, low : low + head_dim].reshape(peers * rows, head_dim)
    factor = head_dim ** (-0.5) * 1.4426950408889634
    clip = place // peers
    count = grid_ref[clip, 0] * grid_ref[clip, 1]
    visible = lax.broadcasted_iota(jnp.int32, (1, peers * rows), 1) < count
    hide = jnp.where(visible, 0.0, -jnp.inf)
    group = 2 if peers % 2 == 0 else 1
    blocks = peers // group

    def one_block(step, carry):
        block = lax.rem(me // group + 1 + step, blocks)
        outcomes = []
        for head in range(heads):
            low = head * head_dim
            query = recv[pl.ds(block * group, group), :, low : low + head_dim].reshape(
                group * rows, head_dim
            )
            scores = lax.dot_general(
                query, keys[head], (((1,), (1,)), ((), ())), preferred_element_type=jnp.float32
            )
            scores = scores + hide
            highest = jnp.max(scores, axis=1, keepdims=True)
            weights = jnp.exp2((scores - highest) * factor)
            running = jnp.sum(weights, axis=1, keepdims=True)
            mixture = jnp.dot(
                weights.astype(jnp.bfloat16), values[head], preferred_element_type=jnp.float32
            )
            outcomes.append((mixture / running).astype(jnp.bfloat16))
        joined = jnp.concatenate([piece.astype(jnp.float32) for piece in outcomes], axis=1)
        for part in range(group):
            peer = block * group + part
            mine = joined[part * rows : (part + 1) * rows]
            mixed_send[peer, :rows, :] = mine[:, :128].astype(jnp.bfloat16)
            tail = jnp.concatenate(
                [mine[:, 128:], jnp.zeros((rows, 256 - span), jnp.float32)], axis=1
            )
            mixed_send[peer, rows:, :] = tail.T[: span - 128].astype(jnp.bfloat16)

            @pl.when(peer != me)
            def _():
                remote(
                    mixed_send.at[peer],
                    mixed_recv.at[me],
                    back_send_sem.at[peer],
                    back_recv_sem.at[me],
                    base + peer,
                ).start()

            @pl.when(peer == me)
            def _():
                pltpu.make_async_copy(
                    mixed_send.at[me], mixed_recv.at[me], local_sem.at[2]
                ).start()

        return carry

    lax.fori_loop(0, blocks, one_block, 0)
    pltpu.make_async_copy(mixed_send.at[me], mixed_recv.at[me], local_sem.at[2]).wait()
    for step in range(1, peers):
        peer = lax.rem(me + step, peers)
        copy = remote(
            mixed_send.at[peer],
            mixed_recv.at[peer],
            back_send_sem.at[peer],
            back_recv_sem.at[peer],
            base + peer,
        )
        copy.wait_recv()
        copy.wait_send()
    for copy in sends:
        copy.wait_send()
    for peer in range(peers):
        start = peer * span
        attention[:, start : start + 128] = mixed_recv[peer, :rows, :]
        tail = mixed_recv[peer, rows:, :].astype(jnp.float32).T
        attention[:, start + 128 : start + span] = tail.astype(jnp.bfloat16)
    weight_copy.wait()
    projected = (
        jnp.dot(attention[...], w_out_ref[...], preferred_element_type=jnp.float32)
        .astype(jnp.bfloat16)
        .astype(jnp.float32)
    )
    tiles = width // 128
    for tile in range(tiles):
        mixed[tile] = projected[:, tile * 128 : (tile + 1) * 128]
    pieces = [
        [mixed[tile, pl.ds(part, rows // 4, stride=4), :] for tile in range(tiles)]
        for part in range(4)
    ]
    total_width = 4 * width
    flat = [piece for row in pieces for piece in row]
    centre = jnp.sum(sum(flat), axis=1, keepdims=True) / total_width
    spread = (
        jnp.sum(sum((piece - centre) * (piece - centre) for piece in flat), axis=1, keepdims=True)
        / total_width
    )
    inverse = lax.rsqrt(spread + norm_eps)
    for index, piece in enumerate(flat):
        out_ref[:, index * 128 : (index + 1) * 128] = (
            (piece - centre) * inverse * gain_ref[index : index + 1, :]
            + bias_ref[index : index + 1, :]
        ).astype(jnp.bfloat16)


def language_part(
    far,
    near,
    run_vision,
    normed_ref,
    ids_ref,
    router_hbm,
    w_merge_hbm,
    w_gate_hbm,
    w_up_hbm,
    w_down_hbm,
    out_ref,
    router_ref,
    merge_rows,
    w_gate,
    w_up,
    w_down,
    norm_send,
    norm_recv,
    part_send,
    y_recv,
    z_send,
    z_recv,
    token_sum,
    gathered,
    hidden_rows,
    expert_part,
    core_recv,
    core_sum,
    y2_recv,
    z2_send,
    z2_recv,
    local_sem,
    w_send_sem,
    w_recv_sem,
    n_send_sem,
    n_recv_sem,
    y_send_sem,
    y_recv_sem,
    z_send_sem,
    z_recv_sem,
    g_recv_sem,
    gz_send_sem,
    gy_send_sem,
    gc_send_sem,
    c_send_sem,
    c_recv_sem,
    y2_send_sem,
    y2_recv_sem,
    z2_send_sem,
    z2_recv_sem,
):
    place = lax.axis_index("wide")
    chips = far * near
    core = lax.rem(place, 2)
    chip = place // 2
    a = chip // near
    b = lax.rem(chip, near)
    other = place + 1 - 2 * core
    tokens_here = normed_ref.shape[0]
    depth = w_merge_hbm.shape[0]
    out_width = w_merge_hbm.shape[1]
    experts = chips
    f32 = jnp.float32
    half = jnp.bfloat16

    def at(a_index, b_index, c_index):
        return (a_index * near + b_index) * 2 + c_index

    other_chips = [lax.rem(chip + step, chips) for step in range(1, chips)]
    weight_copies = [
        pltpu.make_async_copy(w_gate_hbm.at[0], w_gate, local_sem.at[0]),
        pltpu.make_async_copy(w_up_hbm.at[0], w_up, local_sem.at[1]),
        pltpu.make_async_copy(w_down_hbm.at[0], w_down, local_sem.at[2]),
    ]
    own_rows = merge_rows.at[pl.ds(core * depth, depth)]
    merge_copy = pltpu.make_async_copy(w_merge_hbm, own_rows, local_sem.at[3])
    merge_swap = remote(w_merge_hbm, own_rows, w_send_sem.at[0], w_recv_sem.at[0], other)

    def start_rest():
        merge_swap.start()
        merge_copy.start()
        for copy in weight_copies:
            copy.start()
        named_rows = router_hbm[...].astype(f32)
        router_ref[...] = jnp.concatenate(
            [
                named_rows,
                named_rows,
                jnp.zeros((router_ref.shape[0] - 2 * experts, out_width), f32),
            ],
            axis=0,
        ).astype(half)

    run_vision(start_rest)
    for q in range(chips):
        norm_send[q] = normed_ref[:, 2 * depth * q : 2 * depth * (q + 1)]
    own_norm = pltpu.make_async_copy(norm_send.at[chip], norm_recv.at[chip], local_sem.at[4])
    own_norm.start()
    for q in other_chips:
        remote(
            norm_send.at[q], norm_recv.at[chip], n_send_sem.at[q], n_recv_sem.at[chip], q * 2 + core
        ).start()
    merge_copy.wait()
    merge_swap.wait_send()
    remote(
        w_merge_hbm,
        merge_rows.at[pl.ds((1 - core) * depth, depth)],
        w_send_sem.at[0],
        w_recv_sem.at[0],
        other,
    ).wait_recv()
    own_norm.wait()
    for q in other_chips:
        copy = remote(
            norm_send.at[q], norm_recv.at[q], n_send_sem.at[q], n_recv_sem.at[q], q * 2 + core
        )
        copy.wait_recv()
        copy.wait_send()
    column_block = min(512, out_width)
    flat = norm_recv[...].reshape(chips * tokens_here, 2 * depth)

    def merge_columns(index, carry):
        columns = pl.ds(pl.multiple_of(index * column_block, column_block), column_block)
        part_send[:, :, columns] = (
            jnp.dot(flat, merge_rows[:, columns], preferred_element_type=f32)
            .astype(half)
            .reshape(chips, tokens_here, column_block)
        )
        return carry

    lax.fori_loop(0, out_width // column_block, merge_columns, 0)

    near_order = [lax.rem(b + step, near) for step in range(1, near)]
    pieces = out_width // column_block
    flip = a // (far // 2)
    mirrored = a + flip * (far - 1 - 2 * a)

    def columns_of(piece):
        return pl.ds(piece * column_block, column_block)

    def far_first(step):
        value = far - 1 - step
        value = value - (mirrored - value + far) // far
        return value + flip * (far - 1 - 2 * value)

    def y_copy(a_index, b_index, slot, piece):
        columns = columns_of(piece)
        return remote(
            part_send.at[a_index * near + b_index, :, columns],
            y_recv.at[slot, a_index, :, columns],
            y_send_sem.at[b_index, a_index, piece],
            y_recv_sem.at[slot, a_index, piece],
            at(a, b_index, core),
        )

    def y_total(a_index, piece):
        columns = columns_of(piece)
        value = part_send[a_index * near + b, :, columns].astype(f32)
        for b_index in near_order:
            y_copy(a_index, b_index, b_index, piece).wait_recv()
            value = value + y_recv[b_index, a_index, :, columns].astype(f32)
        return value

    def z_copy(a_index, rightward, target, piece):
        columns = columns_of(piece)
        return remote(
            z_send.at[a_index, :, columns],
            z_recv.at[rightward, a_index, :, columns],
            z_send_sem.at[a_index, piece],
            z_recv_sem.at[rightward, a_index, piece],
            at(target, b, core),
        )

    far_targets = [far_first(step) for step in range(far - 1)]
    for a_index in far_targets + [a]:
        for piece in range(pieces):
            for b_index in near_order:
                y_copy(a_index, b_index, b, piece).start()
    z_sends = []
    for a_index in far_targets:
        rightward = (a_index - a + far) // far
        following = a + 2 * rightward - 1
        behind = rightward * a + (1 - rightward) * (far - 1 - a)
        for piece in range(pieces):
            columns = columns_of(piece)
            value = y_total(a_index, piece)
            copy = z_copy(a_index, rightward, following, piece)
            z_sends.append(copy)

            @pl.when(behind == 0)
            def _():
                z_send[a_index, :, columns] = value.astype(half)

            @pl.when(behind > 0)
            def _():
                copy.wait_recv()
                z_send[a_index, :, columns] = (
                    value + z_recv[rightward, a_index, :, columns].astype(f32)
                ).astype(half)

            copy.start()
    for piece in range(pieces):
        columns = columns_of(piece)
        token_sum[:, columns] = y_total(a, piece)

        @pl.when(a > 0)
        def _():
            z_copy(a, 1, a, piece).wait_recv()
            token_sum[:, columns] = token_sum[:, columns] + z_recv[1, a, :, columns].astype(f32)

        @pl.when(a < far - 1)
        def _():
            z_copy(a, 0, a, piece).wait_recv()
            token_sum[:, columns] = token_sum[:, columns] + z_recv[0, a, :, columns].astype(f32)

    tokens = token_sum[...].astype(half)

    lane_count = router_ref.shape[0]
    logits = by_rows(tokens, router_ref[...])
    lane = lax.broadcasted_iota(jnp.int32, (tokens_here, lane_count), 1)
    line = lax.broadcasted_iota(jnp.int32, (lane_count, tokens_here), 0)
    line = jnp.where(line < experts, line, line - experts)
    marks = jnp.zeros((lane_count, tokens_here), f32)
    for k in range(ids_ref.shape[0]):
        marks = jnp.where(line == ids_ref[k : k + 1, :], 1.0, marks)
    same = (
        lax.broadcasted_iota(jnp.int32, (tokens_here, tokens_here), 0)
        == lax.broadcasted_iota(jnp.int32, (tokens_here, tokens_here), 1)
    )
    chosen = by_rows(jnp.where(same, 1.0, 0.0).astype(half), marks.astype(half))
    gates = chosen / (1.0 + jnp.exp(-logits))
    gate_sum = jnp.sum(jnp.where(lane < experts, gates, 0.0), axis=1, keepdims=True)
    route = route_scale * gates / gate_sum
    route_high = route.astype(half)
    route_low = (route - route_high.astype(f32)).astype(half)
    gathered[place, :, :out_width] = tokens
    gathered[place, :, out_width:] = jnp.where(lane < experts, route_high.astype(f32), route_low.astype(f32)).astype(half)

    def share(slot, send_sem, target):
        return remote(gathered.at[slot], gathered.at[slot], send_sem, g_recv_sem.at[slot], target)

    def arrived(slot):
        share(slot, gc_send_sem.at[0], other).wait_recv()

    def to_far(a_index):
        return share(place, gz_send_sem.at[a_index], at(a_index, b, core))

    def to_near(a_index, b_index):
        return share(
            at(a_index, b, core), gy_send_sem.at[a_index, b_index], at(a, b_index, core)
        )

    def to_core(a_index, b_index):
        return share(
            at(a_index, b_index, core), gc_send_sem.at[a_index * near + b_index], other
        )

    def pass_on(a_index):
        for b_index in near_order:
            to_near(a_index, b_index).start()
        to_core(a_index, b).start()

    def paired(step):
        value, bit = 0, 1
        while bit < far:
            mine, theirs = a // bit % 2, step // bit % 2
            value = value + bit * (mine + theirs - 2 * mine * theirs)
            bit *= 2
        return value

    pass_on(a)
    for step in range(1, far):
        to_far(paired(step)).start()
    for copy in weight_copies:
        copy.wait()

    def core_copy(a_index, side, piece):
        columns = columns_of(piece)
        return remote(
            expert_part.at[a_index, side, :, :, columns],
            core_recv.at[a_index, :, :, columns],
            c_send_sem.at[a_index, piece],
            c_recv_sem.at[a_index, piece],
            other,
        )

    def y2_copy(a_index, b_index, slot, piece):
        columns = columns_of(piece)
        return remote(
            core_sum.at[a_index, b_index, :, columns],
            y2_recv.at[slot, a_index, :, columns],
            y2_send_sem.at[b_index, a_index, piece],
            y2_recv_sem.at[slot, a_index, piece],
            at(a, b_index, core),
        )

    def z2_copy(a_index, slot, piece):
        columns = columns_of(piece)
        return remote(
            z2_send.at[a_index, :, columns],
            z2_recv.at[slot, :, columns],
            z2_send_sem.at[a_index, piece],
            z2_recv_sem.at[slot, piece],
            at(a_index, b, core),
        )

    chunk = near * 2
    expert = place // 2

    def y2_start(a_index, piece):
        for b_index in near_order:
            y2_copy(a_index, b_index, b, piece).start()

    def join_cores(a_index, piece):
        columns = columns_of(piece)
        core_copy(a_index, 1 - core, piece).wait_recv()
        core_sum[a_index, :, :, columns] = (
            expert_part[a_index, core, :, :, columns].astype(f32)
            + core_recv[a_index, :, :, columns].astype(f32)
        ).astype(half)

    def y2_total(a_index, piece):
        columns = columns_of(piece)
        value = core_sum[a_index, b, :, columns].astype(f32)
        for b_index in near_order:
            y2_copy(a_index, b_index, b_index, piece).wait_recv()
            value = value + y2_recv[b_index, a_index, :, columns].astype(f32)
        return value

    def join_near(a_index):
        for piece in range(pieces):
            z2_send[a_index, :, columns_of(piece)] = y2_total(a_index, piece).astype(half)
            z2_copy(a_index, a, piece).start()

    def chunks(step, carry):
        a_index = paired(step)

        @pl.when(step < far - 1)
        def _():
            upcoming = paired(step + 1)
            arrived(at(upcoming, b, core))
            pass_on(upcoming)

        for b_index in near_order:
            arrived(at(a_index, b_index, core))
            to_core(a_index, b_index).start()
        for b_index in range(near):
            arrived(at(a_index, b_index, 1 - core))
        slots = pl.ds(a_index * chunk, chunk)
        rows = gathered[slots, :, :out_width].reshape(chunk * tokens_here, out_width)
        table = gathered[slots, :, out_width:].reshape(chunk * tokens_here, lane_count).astype(f32)
        table_lane = lax.broadcasted_iota(jnp.int32, table.shape, 1)
        mine = jnp.logical_or(table_lane == expert, table_lane == expert + experts)
        scale = jnp.sum(jnp.where(mine, table, 0.0), axis=1, keepdims=True)
        gate_part = by_rows(rows, w_gate[...])
        up_part = by_rows(rows, w_up[...])
        hidden_rows[...] = (gate_part / (1.0 + jnp.exp(-gate_part)) * up_part).astype(half)

        @pl.when(step == 1)
        def _():
            for piece in range(pieces):
                join_cores(a, piece)

        @pl.when(step > 1)
        def _():
            previous = paired(step - 1)
            for piece in range(pieces):
                join_cores(previous, piece)
                y2_start(previous, piece)

        hidden = hidden_rows[...]
        for piece in range(pieces):
            columns = columns_of(piece)
            product = jnp.dot(hidden, w_down[:, columns], preferred_element_type=f32).astype(half)
            scaled = (product.astype(f32) * scale).astype(half)
            for b_index in range(near):
                for side in range(2):
                    start = (b_index * 2 + side) * tokens_here
                    expert_part[a_index, side, b_index, :, columns] = scaled[
                        start : start + tokens_here
                    ]
            core_copy(a_index, 1 - core, piece).start()

        @pl.when(step > 2)
        def _():
            join_near(paired(step - 2))

        return carry

    lax.fori_loop(0, far, chunks, 0)
    final = paired(far - 1)
    for piece in range(pieces):
        join_cores(final, piece)
        y2_start(final, piece)
    for piece in range(pieces):
        y2_start(a, piece)
    for step in range(max(1, far - 2), far):
        join_near(paired(step))
    for piece in range(pieces):
        columns = columns_of(piece)
        value = y2_total(a, piece)
        for step in range(1, far):
            z2_copy(paired(step), paired(step), piece).wait_recv()
            value = value + z2_recv[paired(step), :, columns].astype(f32)
        out_ref[:, columns] = value.astype(half)

    for copy in z_sends:
        copy.wait_send()
    for step in range(1, far):
        to_far(paired(step)).wait_send()
        for piece in range(pieces):
            z2_copy(paired(step), a, piece).wait_send()
    for a_index in range(far):
        for piece in range(pieces):
            core_copy(a_index, 1 - core, piece).wait_send()
        for b_index in range(near):
            to_core(a_index, b_index).wait_send()
        for b_index in near_order:
            to_near(a_index, b_index).wait_send()
            for piece in range(pieces):
                y_copy(a_index, b_index, b, piece).wait_send()
                y2_copy(a_index, b_index, b, piece).wait_send()


def layer_kernel(far, near, peers, head_dim, *refs):
    operands, out_ref, normed = refs[:11], refs[11], refs[12]
    grid_ref, qkv_hbm, w_out_hbm, gain_ref, bias_ref = operands[:5]
    scratch = refs[13:]
    vision_scratch, language_scratch = scratch[:15], scratch[15:]
    place = lax.axis_index("wide")
    devices = lax.axis_size("wide")
    barrier = greet([lax.rem(place + step, devices) for step in range(1, devices)])

    def run_vision(start_rest):
        vision_part(
            peers,
            head_dim,
            barrier,
            grid_ref,
            qkv_hbm,
            w_out_hbm,
            gain_ref,
            bias_ref,
            normed,
            *vision_scratch,
            start_rest,
        )

    language_part(far, near, run_vision, normed, *operands[5:], out_ref, *language_scratch)


def fast_local(
    qkv,
    grid,
    w_out,
    ln_gain,
    ln_bias,
    w_merge,
    w_router,
    expert_ids,
    slot_pos,
    w_gate,
    w_up,
    w_down,
):
    devices = lax.axis_size("wide")
    peers = devices // CLIPS
    patch_rows = qkv.shape[0]
    width = w_out.shape[0]
    head_dim = width // HEADS
    heads = HEADS // peers
    span = heads * head_dim
    chips = devices // 2
    near = 1
    while 4 * near * near <= chips:
        near *= 2
    far = chips // near
    rows = patch_rows // 4
    depth, out_width = w_merge.shape
    experts = w_router.shape[1]
    lanes = -(-2 * experts // 128) * 128
    hidden = w_gate.shape[2]
    whole = pl.BlockSpec(memory_space=pltpu.VMEM)
    away = pl.BlockSpec(memory_space=pl.ANY)
    half = jnp.bfloat16
    block = (rows, out_width)
    dma = pltpu.SemaphoreType.DMA
    pieces = out_width // min(512, out_width)
    return pl.pallas_call(
        functools.partial(layer_kernel, far, near, peers, head_dim),
        out_shape=jax.ShapeDtypeStruct(block, half),
        in_specs=[
            pl.BlockSpec(memory_space=pltpu.SMEM),
            away,
            away,
            whole,
            whole,
            whole,
            whole,
            away,
            away,
            away,
            away,
        ],
        out_specs=whole,
        scratch_shapes=[
            pltpu.VMEM((rows, 4 * width), half),
            pltpu.VMEM((patch_rows, 3 * width), half),
            pltpu.VMEM((peers, patch_rows, 3 * span), half),
            pltpu.VMEM((peers, patch_rows, 3 * span), half),
            pltpu.VMEM((heads, peers * patch_rows, head_dim), half),
            pltpu.VMEM((heads, peers * patch_rows, head_dim), half),
            pltpu.VMEM((peers, patch_rows + span - 128, 128), half),
            pltpu.VMEM((peers, patch_rows + span - 128, 128), half),
            pltpu.VMEM((patch_rows, width), half),
            pltpu.VMEM((width // 128, patch_rows, 128), jnp.float32),
            pltpu.VMEM((width, width), half),
            dma((peers,)),
            dma((peers,)),
            dma((peers,)),
            dma((peers,)),
            dma((4,)),
            pltpu.VMEM((lanes, out_width), half),
            pltpu.VMEM((2 * depth, out_width), half),
            pltpu.VMEM((hidden, out_width), half),
            pltpu.VMEM((hidden, out_width), half),
            pltpu.VMEM((hidden, out_width), half),
            pltpu.VMEM((chips, rows, 2 * depth), half),
            pltpu.VMEM((chips, rows, 2 * depth), half),
            pltpu.VMEM((chips, *block), half),
            pltpu.VMEM((near, far, *block), half),
            pltpu.VMEM((far, *block), half),
            pltpu.VMEM((2, far, *block), half),
            pltpu.VMEM(block, jnp.float32),
            pltpu.VMEM((devices, rows, out_width + lanes), half),
            pltpu.VMEM((2 * near * rows, hidden), half),
            pltpu.VMEM((far, 2, near, *block), half),
            pltpu.VMEM((far, near, *block), half),
            pltpu.VMEM((far, near, *block), half),
            pltpu.VMEM((near, far, *block), half),
            pltpu.VMEM((far, *block), half),
            pltpu.VMEM((far, *block), half),
            dma((5,)),
            dma((1,)),
            dma((1,)),
            dma((chips,)),
            dma((chips,)),
            dma((near, far, pieces)),
            dma((near, far, pieces)),
            dma((far, pieces)),
            dma((2, far, pieces)),
            dma((devices,)),
            dma((far,)),
            dma((far, near)),
            dma((chips,)),
            dma((far, pieces)),
            dma((far, pieces)),
            dma((near, far, pieces)),
            dma((near, far, pieces)),
            dma((far, pieces)),
            dma((far, pieces)),
        ],
        compiler_params=pltpu.CompilerParams(
            collective_id=0, has_side_effects=True, vmem_limit_bytes=62 * 2**20
        ),
        name="layer",
    )(
        grid,
        qkv,
        w_out,
        ln_gain.reshape(-1, 128),
        ln_bias.reshape(-1, 128),
        expert_ids.T,
        w_router.T,
        w_merge,
        w_gate.swapaxes(1, 2),
        w_up.swapaxes(1, 2),
        w_down,
    )


def either(*operands):
    devices = lax.axis_size("wide")
    qkv, w_router, expert_ids = operands[0], operands[6], operands[7]
    token_count = qkv.shape[0] // 4
    experts = w_router.shape[1]
    dense = 2 * token_count * expert_ids.shape[1] >= experts * token_count
    whole_heads = HEADS % (devices // CLIPS) == 0 and devices == 2 * experts
    if not (dense and whole_heads):
        return local(*operands)
    span = HEADS // (devices // CLIPS) * (operands[2].shape[0] // HEADS)
    packs = qkv.shape[0] == 128 and 128 < span < 256 and span % 16 == 0
    return fast_local(*operands) if packs else local(*operands)


def solution(mesh):
    placed = (
        P(("grp", "wide"), None),
        P("grp", None),
        P(),
        P(),
        P(),
        P("wide", None),
        P(),
        P(("grp", "wide"), None),
        P(("grp", "wide"), None),
        P("wide", None, None),
        P("wide", None, None),
        P("wide", None, None),
    )
    return jax.shard_map(
        either, mesh=mesh, in_specs=placed, out_specs=P(("grp", "wide"), None), check_vma=False
    )
```

```python
import functools

import jax
import jax.numpy as jnp
from jax import lax
from jax.experimental import pallas as pl
from jax.experimental.pallas import tpu as pltpu
from jax.sharding import PartitionSpec as P

HEADS = 16
CLIPS = 2


route_scale = 2.446
norm_eps = 1e-05
column_parts = 2


def swapped(value, axis, stride):
    mask = 2**stride
    pairs = [(source, source ^ mask) for source in range(lax.axis_size(axis))]
    return lax.ppermute(value, axis, pairs)


def ordered_pair(own_part, partner, upper_bit):
    return jnp.where(
        upper_bit == 1,
        jnp.concatenate([partner, own_part], 0),
        jnp.concatenate([own_part, partner], 0),
    )


def local(
    qkv,
    grid,
    w_out,
    ln_gain,
    ln_bias,
    w_merge,
    w_router,
    expert_ids,
    slot_pos,
    w_gate,
    w_up,
    w_down,
):
    devices = lax.axis_size("wide")
    position_self = lax.axis_index("wide")
    vit_width = w_out.shape[0]
    head_dim = vit_width // HEADS
    groups = devices // HEADS
    local_rows = qkv.shape[0]
    sub_rows = local_rows // groups
    per_clip = devices // CLIPS
    query_send = (
        qkv[:, :vit_width]
        .reshape(groups, sub_rows, HEADS, head_dim)
        .transpose(2, 0, 1, 3)
        .reshape(devices, sub_rows, head_dim)
    )
    key_value = jnp.concatenate(
        [
            qkv[:, vit_width : 2 * vit_width].reshape(local_rows, HEADS, head_dim),
            qkv[:, 2 * vit_width :].reshape(local_rows, HEADS, head_dim),
        ],
        axis=2,
    )
    spread_send = jnp.broadcast_to(
        key_value.transpose(1, 0, 2)[:, None], (HEADS, groups, local_rows, 2 * head_dim)
    ).reshape(devices, local_rows, 2 * head_dim)
    queries, key_rows = (
        lax.all_to_all(query_send, "wide", split_axis=0, concat_axis=0, tiled=True),
        lax.all_to_all(spread_send, "wide", split_axis=0, concat_axis=0, tiled=True),
    )
    key_rows = key_rows[None]
    key_groups = key_rows.shape[0]
    key_count = key_rows.shape[2]
    key_place = (
        jnp.arange(per_clip, dtype=jnp.int32)[None, :, None] * local_rows
        + jnp.arange(key_groups, dtype=jnp.int32)[:, None, None] * local_rows
        + jnp.arange(key_count, dtype=jnp.int32)[None, None, :]
    ).reshape(-1)
    patch_counts = grid[:, 0] * grid[:, 1]
    clip_queries = queries.reshape(CLIPS, per_clip * sub_rows, head_dim)
    query_block_rows = min(512, per_clip * sub_rows)
    score_scale = head_dim ** (-0.5)

    def attend(clip_index):
        key_block = lax.dynamic_slice_in_dim(key_rows, clip_index * per_clip, per_clip, 1).reshape(
            -1, 2 * head_dim
        )
        visible = key_place < lax.dynamic_index_in_dim(patch_counts, clip_index, 0, keepdims=False)
        query_all = lax.dynamic_index_in_dim(clip_queries, clip_index, 0, keepdims=False)

        def one_block(query_block):
            scores = (
                lax.dot_general(
                    query_block,
                    key_block[:, :head_dim],
                    (((1,), (1,)), ((), ())),
                    preferred_element_type=jnp.float32,
                )
                * score_scale
            )
            scores = jnp.where(visible[None, :], scores, -jnp.inf)
            highest = jnp.max(scores, axis=1, keepdims=True)
            weights = jnp.exp(scores - highest)
            running = jnp.sum(weights, axis=1, keepdims=True)
            mixture = jnp.dot(
                weights.astype(jnp.bfloat16),
                key_block[:, head_dim:],
                preferred_element_type=jnp.float32,
            )
            return (mixture / running).astype(jnp.bfloat16)

        return lax.map(one_block, query_all.reshape(-1, query_block_rows, head_dim)).reshape(
            -1, head_dim
        )

    attended = lax.map(attend, jnp.arange(CLIPS, dtype=jnp.int32))
    returned = lax.all_to_all(
        attended.reshape(devices, sub_rows, head_dim),
        "wide",
        split_axis=0,
        concat_axis=0,
        tiled=True,
    )
    attention = (
        returned.reshape(HEADS, groups, sub_rows, head_dim)
        .transpose(1, 2, 0, 3)
        .reshape(local_rows, vit_width)
    )
    projected = jnp.dot(attention, w_out, preferred_element_type=jnp.float32).astype(jnp.bfloat16)
    merged = projected.reshape(local_rows // 4, 4 * vit_width).astype(jnp.float32)
    centre = jnp.mean(merged, axis=1, keepdims=True)
    centered = merged - centre
    spread = jnp.mean(centered * centered, axis=1, keepdims=True)
    normed = (centered * lax.rsqrt(spread + norm_eps) * ln_gain + ln_bias).astype(jnp.bfloat16)
    tok_groups = min(8, devices)
    feat_groups = devices // tok_groups
    merge_rows = w_merge
    for bit_index in range(tok_groups.bit_length() - 1):
        partner = swapped(merge_rows, "wide", bit_index)
        upper_bit = position_self // (1 << bit_index) % 2
        merge_rows = ordered_pair(merge_rows, partner, upper_bit)
    token_count = normed.shape[0]
    part_rows = token_count // tok_groups
    feat_width = normed.shape[1] // feat_groups
    out_width = w_merge.shape[1]
    merge_send = (
        normed.reshape(tok_groups, part_rows, feat_groups, feat_width)
        .transpose(2, 0, 1, 3)
        .reshape(devices, part_rows, feat_width)
    )
    flat_rows = lax.all_to_all(merge_send, "wide", split_axis=0, concat_axis=0, tiled=True).reshape(
        -1, feat_width
    )
    partial_value = jnp.dot(flat_rows, merge_rows, preferred_element_type=jnp.float32).reshape(
        devices, -1, out_width
    )
    summed = lax.all_to_all(partial_value, "wide", split_axis=0, concat_axis=0, tiled=True)
    tokens = (
        jnp.sum(summed.reshape(feat_groups, tok_groups, part_rows, out_width), axis=0)
        .reshape(token_count, out_width)
        .astype(jnp.bfloat16)
    )
    logits = jnp.dot(tokens, w_router, preferred_element_type=jnp.float32)
    experts = w_router.shape[1]
    top_count = expert_ids.shape[1]
    matches = expert_ids[:, :, None] == jnp.arange(experts, dtype=jnp.int32)[None, None, :]
    chosen = jnp.sum(jnp.where(matches, logits[:, None, :], 0.0), axis=2)
    gate_values = jax.nn.sigmoid(chosen)
    route_weight = route_scale * gate_values / jnp.sum(gate_values, axis=1, keepdims=True)
    capacity = min(token_count, 2 * token_count * top_count // experts)
    slot_count = experts * capacity
    target = expert_ids * capacity + slot_pos
    one_hot = jnp.any(
        target[None, :, :] == jnp.arange(slot_count, dtype=jnp.int32)[:, None, None], axis=2
    ).astype(jnp.bfloat16)
    buffer = jnp.dot(one_hot, tokens, preferred_element_type=jnp.float32).astype(jnp.bfloat16)
    gate_half = w_gate[0]
    up_half = w_up[0]
    down_half = w_down[0]
    half_cap = capacity // 2
    dispatch = buffer.reshape(devices, half_cap, out_width)
    portion = lax.all_to_all(dispatch, "wide", split_axis=0, concat_axis=0, tiled=True)
    item_count = portion.shape[1]
    partner_rows = swapped(portion, "wide", 0)
    both_rows = jnp.concatenate([portion, partner_rows], axis=1)
    flat_rows = both_rows.reshape(-1, out_width)
    gate_part = jnp.dot(flat_rows, gate_half, preferred_element_type=jnp.float32)
    up_part = jnp.dot(flat_rows, up_half, preferred_element_type=jnp.float32)
    hidden = (jax.nn.silu(gate_part) * up_part).astype(jnp.bfloat16)
    product = (
        jnp.dot(hidden, down_half, preferred_element_type=jnp.float32)
        .astype(jnp.bfloat16)
        .reshape(devices, 2 * item_count, out_width)
    )
    from_partner = swapped(product[:, item_count:], "wide", 0)
    joined = (
        product[:, :item_count].astype(jnp.float32) + from_partner.astype(jnp.float32)
    ).astype(jnp.bfloat16)
    answers = lax.all_to_all(joined, "wide", split_axis=0, concat_axis=0, tiled=True)
    slot_result = answers.reshape(slot_count, out_width)
    slot_result = lax.optimization_barrier(slot_result)
    picked = jnp.take(slot_result, target.reshape(-1), axis=0).reshape(
        token_count, top_count, out_width
    )
    return jnp.sum(picked.astype(jnp.float32) * route_weight[:, :, None], axis=1).astype(
        jnp.bfloat16
    )


def remote(source, target, send_sem, recv_sem, place):
    return pltpu.make_async_remote_copy(
        src_ref=source,
        dst_ref=target,
        send_sem=send_sem,
        recv_sem=recv_sem,
        device_id={"wide": place},
        device_id_type=pl.DeviceIdType.MESH,
    )


def by_rows(left, right):
    return lax.dot_general(
        left, right, (((1,), (1,)), ((), ())), preferred_element_type=jnp.float32
    )


def greet(places):
    barrier = pltpu.get_barrier_semaphore()
    for place in places:
        pl.semaphore_signal(
            barrier, inc=1, device_id={"wide": place}, device_id_type=pl.DeviceIdType.MESH
        )
    return barrier


def vision_part(
    peers,
    head_dim,
    barrier,
    grid_ref,
    qkv_hbm,
    w_out_hbm,
    gain_ref,
    bias_ref,
    out_ref,
    qkv_ref,
    send,
    recv,
    keys,
    values,
    mixed_send,
    mixed_recv,
    attention,
    mixed,
    w_out_ref,
    send_sem,
    recv_sem,
    back_send_sem,
    back_recv_sem,
    local_sem,
    start_rest,
):
    place = lax.axis_index("wide")
    base = place // peers * peers
    me = place - base
    rows = qkv_ref.shape[0]
    width = w_out_hbm.shape[0]
    heads = HEADS // peers
    span = heads * head_dim
    devices = lax.axis_size("wide")
    qkv_copy = pltpu.make_async_copy(qkv_hbm, qkv_ref, local_sem.at[3])
    qkv_copy.start()
    weight_copy = pltpu.make_async_copy(w_out_hbm, w_out_ref, local_sem.at[0])
    weight_copy.start()
    qkv_copy.wait()
    for peer in range(peers):
        for part in range(3):
            start = part * width + peer * span
            send[peer, :, part * span : (part + 1) * span] = qkv_ref[:, start : start + span]
    pl.semaphore_wait(barrier, devices - 1)
    own = pltpu.make_async_copy(send.at[me], recv.at[me], local_sem.at[1])
    own.start()
    sends = []
    for step in range(1, peers):
        peer = lax.rem(me + step, peers)
        copy = remote(
            send.at[peer], recv.at[me], send_sem.at[peer], recv_sem.at[me], base + peer
        )
        copy.start()
        sends.append(copy)
    start_rest()
    own.wait()
    for step in range(1, peers):
        peer = lax.rem(me + step, peers)
        remote(
            send.at[peer], recv.at[peer], send_sem.at[peer], recv_sem.at[peer], base + peer
        ).wait_recv()
    for head in range(heads):
        low = span + head * head_dim
        keys[head] = recv[:, :, low : low + head_dim].reshape(peers * rows, head_dim)
        low = 2 * span + head * head_dim
        values[head] = recv[:, :, low : low + head_dim].reshape(peers * rows, head_dim)
    factor = head_dim ** (-0.5) * 1.4426950408889634
    clip = place // peers
    count = grid_ref[clip, 0] * grid_ref[clip, 1]
    visible = lax.broadcasted_iota(jnp.int32, (1, peers * rows), 1) < count
    hide = jnp.where(visible, 0.0, -jnp.inf)
    group = 2 if peers % 2 == 0 else 1
    blocks = peers // group

    def one_block(step, carry):
        block = lax.rem(me // group + 1 + step, blocks)
        outcomes = []
        for head in range(heads):
            low = head * head_dim
            query = recv[pl.ds(block * group, group), :, low : low + head_dim].reshape(
                group * rows, head_dim
            )
            scores = lax.dot_general(
                query, keys[head], (((1,), (1,)), ((), ())), preferred_element_type=jnp.float32
            )
            scores = scores + hide
            highest = jnp.max(scores, axis=1, keepdims=True)
            weights = jnp.exp2((scores - highest) * factor)
            running = jnp.sum(weights, axis=1, keepdims=True)
            mixture = jnp.dot(
                weights.astype(jnp.bfloat16), values[head], preferred_element_type=jnp.float32
            )
            outcomes.append((mixture / running).astype(jnp.bfloat16))
        joined = jnp.concatenate([piece.astype(jnp.float32) for piece in outcomes], axis=1)
        for part in range(group):
            peer = block * group + part
            mine = joined[part * rows : (part + 1) * rows]
            mixed_send[peer, :rows, :] = mine[:, :128].astype(jnp.bfloat16)
            tail = jnp.concatenate(
                [mine[:, 128:], jnp.zeros((rows, 256 - span), jnp.float32)], axis=1
            )
            mixed_send[peer, rows:, :] = tail.T[: span - 128].astype(jnp.bfloat16)

            @pl.when(peer != me)
            def _():
                remote(
                    mixed_send.at[peer],
                    mixed_recv.at[me],
                    back_send_sem.at[peer],
                    back_recv_sem.at[me],
                    base + peer,
                ).start()

            @pl.when(peer == me)
            def _():
                pltpu.make_async_copy(
                    mixed_send.at[me], mixed_recv.at[me], local_sem.at[2]
                ).start()

        return carry

    lax.fori_loop(0, blocks, one_block, 0)
    pltpu.make_async_copy(mixed_send.at[me], mixed_recv.at[me], local_sem.at[2]).wait()
    for step in range(1, peers):
        peer = lax.rem(me + step, peers)
        copy = remote(
            mixed_send.at[peer],
            mixed_recv.at[peer],
            back_send_sem.at[peer],
            back_recv_sem.at[peer],
            base + peer,
        )
        copy.wait_recv()
        copy.wait_send()
    for copy in sends:
        copy.wait_send()
    for peer in range(peers):
        start = peer * span
        attention[:, start : start + 128] = mixed_recv[peer, :rows, :]
        tail = mixed_recv[peer, rows:, :].astype(jnp.float32).T
        attention[:, start + 128 : start + span] = tail.astype(jnp.bfloat16)
    weight_copy.wait()
    projected = (
        jnp.dot(attention[...], w_out_ref[...], preferred_element_type=jnp.float32)
        .astype(jnp.bfloat16)
        .astype(jnp.float32)
    )
    tiles = width // 128
    for tile in range(tiles):
        mixed[tile] = projected[:, tile * 128 : (tile + 1) * 128]
    pieces = [
        [mixed[tile, pl.ds(part, rows // 4, stride=4), :] for tile in range(tiles)]
        for part in range(4)
    ]
    total_width = 4 * width
    flat = [piece for row in pieces for piece in row]
    centre = jnp.sum(sum(flat), axis=1, keepdims=True) / total_width
    spread = (
        jnp.sum(sum((piece - centre) * (piece - centre) for piece in flat), axis=1, keepdims=True)
        / total_width
    )
    inverse = lax.rsqrt(spread + norm_eps)
    for index, piece in enumerate(flat):
        out_ref[:, index * 128 : (index + 1) * 128] = (
            (piece - centre) * inverse * gain_ref[index : index + 1, :]
            + bias_ref[index : index + 1, :]
        ).astype(jnp.bfloat16)


def language_part(
    far,
    near,
    run_vision,
    normed_ref,
    ids_ref,
    router_hbm,
    w_merge_hbm,
    w_gate_hbm,
    w_up_hbm,
    w_down_hbm,
    out_ref,
    router_ref,
    merge_rows,
    w_gate,
    w_up,
    w_down,
    norm_send,
    norm_recv,
    part_send,
    y_recv,
    z_send,
    z_recv,
    gathered,
    hidden_rows,
    expert_part,
    core_recv,
    core_sum,
    y2_recv,
    z2_send,
    z2_recv,
    local_sem,
    w_send_sem,
    w_recv_sem,
    n_send_sem,
    n_recv_sem,
    y_send_sem,
    y_recv_sem,
    z_send_sem,
    z_recv_sem,
    g_recv_sem,
    gz_send_sem,
    gy_send_sem,
    gc_send_sem,
    c_send_sem,
    c_recv_sem,
    y2_send_sem,
    y2_recv_sem,
    z2_send_sem,
    z2_recv_sem,
):
    place = lax.axis_index("wide")
    chips = far * near
    core = lax.rem(place, 2)
    chip = place // 2
    a = chip // near
    b = lax.rem(chip, near)
    other = place + 1 - 2 * core
    tokens_here = normed_ref.shape[0]
    depth = w_merge_hbm.shape[0]
    out_width = w_merge_hbm.shape[1]
    experts = chips
    f32 = jnp.float32
    half = jnp.bfloat16

    def at(a_index, b_index, c_index):
        return (a_index * near + b_index) * 2 + c_index

    other_chips = [lax.rem(chip + step, chips) for step in range(1, chips)]
    weight_copies = [
        pltpu.make_async_copy(w_gate_hbm.at[0], w_gate, local_sem.at[0]),
        pltpu.make_async_copy(w_up_hbm.at[0], w_up, local_sem.at[1]),
        pltpu.make_async_copy(w_down_hbm.at[0], w_down, local_sem.at[2]),
    ]
    own_rows = merge_rows.at[pl.ds(core * depth, depth)]
    merge_copy = pltpu.make_async_copy(w_merge_hbm, own_rows, local_sem.at[3])
    merge_swap = remote(w_merge_hbm, own_rows, w_send_sem.at[0], w_recv_sem.at[0], other)

    def start_rest():
        merge_swap.start()
        merge_copy.start()
        for copy in weight_copies:
            copy.start()
        named_rows = router_hbm[...].astype(f32)
        router_ref[...] = jnp.concatenate(
            [
                named_rows,
                named_rows,
                jnp.zeros((router_ref.shape[0] - 2 * experts, out_width), f32),
            ],
            axis=0,
        ).astype(half)

    run_vision(start_rest)
    for q in range(chips):
        norm_send[q] = normed_ref[:, 2 * depth * q : 2 * depth * (q + 1)]
    own_norm = pltpu.make_async_copy(norm_send.at[chip], norm_recv.at[chip], local_sem.at[4])
    own_norm.start()
    for q in other_chips:
        remote(
            norm_send.at[q], norm_recv.at[chip], n_send_sem.at[q], n_recv_sem.at[chip], q * 2 + core
        ).start()
    merge_copy.wait()
    merge_swap.wait_send()
    remote(
        w_merge_hbm,
        merge_rows.at[pl.ds((1 - core) * depth, depth)],
        w_send_sem.at[0],
        w_recv_sem.at[0],
        other,
    ).wait_recv()
    own_norm.wait()
    for q in other_chips:
        copy = remote(
            norm_send.at[q], norm_recv.at[q], n_send_sem.at[q], n_recv_sem.at[q], q * 2 + core
        )
        copy.wait_recv()
        copy.wait_send()
    column_block = min(512, out_width)
    flat = norm_recv[...].reshape(chips * tokens_here, 2 * depth)

    def merge_columns(index, carry):
        columns = pl.ds(pl.multiple_of(index * column_block, column_block), column_block)
        part_send[:, :, columns] = (
            jnp.dot(flat, merge_rows[:, columns], preferred_element_type=f32)
            .astype(half)
            .reshape(chips, tokens_here, column_block)
        )
        return carry

    lax.fori_loop(0, out_width // column_block, merge_columns, 0)

    near_steps = range(1, near)
    pieces = out_width // column_block
    parts = column_parts
    part_width = out_width // parts

    def columns_of(piece):
        return pl.ds(piece * column_block, column_block)

    def part_of(part):
        return pl.ds(part * part_width, part_width)

    def paired(step):
        value, bit = 0, 1
        while bit < far:
            mine, theirs = a // bit % 2, step // bit % 2
            value = value + bit * (mine + theirs - 2 * mine * theirs)
            bit *= 2
        return value

    def y_copy(a_index, step, slot, part):
        target = lax.rem(b + step, near)
        columns = part_of(part)
        return remote(
            part_send.at[a_index * near + target, :, columns],
            y_recv.at[slot, a_index, :, columns],
            y_send_sem.at[0],
            y_recv_sem.at[slot, a_index, part],
            at(a, target, core),
        )

    def y_total(a_index, part):
        columns = part_of(part)
        value = part_send[a_index * near + b, :, columns].astype(f32)
        for step in near_steps:
            y_copy(a_index, step, step - 1, part).wait_recv()
            value = value + y_recv[step - 1, a_index, :, columns].astype(f32)
        return value

    def z_copy(a_index, slot, part):
        columns = part_of(part)
        return remote(
            z_send.at[a_index, :, columns],
            z_recv.at[slot, :, columns],
            z_send_sem.at[0],
            z_recv_sem.at[slot, part],
            at(a_index, b, core),
        )

    far_targets = [paired(step) for step in range(far - 1, 0, -1)]
    for part in range(parts):
        for a_index in far_targets + [a]:
            for step in near_steps:
                y_copy(a_index, step, near - step - 1, part).start()

    def merge_far(part):
        for a_index in far_targets:
            z_send[a_index, :, part_of(part)] = y_total(a_index, part).astype(half)
            z_copy(a_index, a, part).start()

    def merge_own(part):
        columns = part_of(part)
        value = y_total(a, part)
        for a_index in far_targets:
            z_copy(a_index, a_index, part).wait_recv()
            value = value + z_recv[a_index, :, columns].astype(f32)
        gathered[place, :, columns] = value.astype(half)

    lane_count = router_ref.shape[0]

    def span_of(part):
        extra = lane_count if part == parts - 1 else 0
        return pl.ds(part * part_width, part_width + extra)

    def share(slot, send_sem, target, part):
        block = gathered.at[slot, :, span_of(part)]
        return remote(block, block, send_sem, g_recv_sem.at[slot, part], target)

    def arrived(slot, part):
        share(slot, gc_send_sem.at[0], other, part).wait_recv()

    def to_far(a_index, part):
        return share(place, gz_send_sem.at[0], at(a_index, b, core), part)

    def to_near(a_index, step, part):
        return share(
            at(a_index, b, core),
            gy_send_sem.at[0],
            at(a, lax.rem(b + step, near), core),
            part,
        )

    def to_core(a_index, b_index, part):
        return share(at(a_index, b_index, core), gc_send_sem.at[0], other, part)

    def pass_on(a_index, part):
        for step in near_steps:
            to_near(a_index, step, part).start()
        to_core(a_index, b, part).start()

    def share_own(part):
        for step in range(1, far):
            to_far(paired(step), part).start()
        pass_on(a, part)

    def forward_far(a_index, part):
        arrived(at(a_index, b, core), part)
        pass_on(a_index, part)

    def forward_near(a_index, part):
        for step in near_steps:
            b_index = lax.rem(b + step, near)
            arrived(at(a_index, b_index, core), part)
            to_core(a_index, b_index, part).start()

    for part in range(parts):
        merge_far(part)
    for part in range(parts - 1):
        merge_own(part)
        share_own(part)
    merge_own(parts - 1)
    tokens = gathered[place, :, :out_width]

    logits = by_rows(tokens, router_ref[...])
    lane = lax.broadcasted_iota(jnp.int32, (tokens_here, lane_count), 1)
    line = lax.broadcasted_iota(jnp.int32, (lane_count, tokens_here), 0)
    line = jnp.where(line < experts, line, line - experts)
    marks = jnp.zeros((lane_count, tokens_here), f32)
    for k in range(ids_ref.shape[0]):
        marks = jnp.where(line == ids_ref[k : k + 1, :], 1.0, marks)
    same = (
        lax.broadcasted_iota(jnp.int32, (tokens_here, tokens_here), 0)
        == lax.broadcasted_iota(jnp.int32, (tokens_here, tokens_here), 1)
    )
    chosen = by_rows(jnp.where(same, 1.0, 0.0).astype(half), marks.astype(half))
    gates = chosen / (1.0 + jnp.exp(-logits))
    gate_sum = jnp.sum(jnp.where(lane < experts, gates, 0.0), axis=1, keepdims=True)
    route = route_scale * gates / gate_sum
    route_high = route.astype(half)
    route_low = (route - route_high.astype(f32)).astype(half)
    gathered[place, :, out_width:] = jnp.where(lane < experts, route_high.astype(f32), route_low.astype(f32)).astype(half)

    share_own(parts - 1)
    for part in range(parts - 1):
        forward_far(paired(1), part)
        forward_near(a, part)
        for step in range(2, far):
            forward_far(paired(step), part)
    for copy in weight_copies:
        copy.wait()

    def core_copy(a_index, side, piece):
        columns = columns_of(piece)
        return remote(
            expert_part.at[a_index, side, :, :, columns],
            core_recv.at[a_index, :, :, columns],
            c_send_sem.at[0],
            c_recv_sem.at[a_index, piece],
            other,
        )

    def y2_copy(a_index, step, slot, piece):
        target = lax.rem(b + step, near)
        columns = columns_of(piece)
        return remote(
            core_sum.at[a_index, target, :, columns],
            y2_recv.at[slot, a_index, :, columns],
            y2_send_sem.at[0],
            y2_recv_sem.at[slot, a_index, piece],
            at(a, target, core),
        )

    def z2_copy(a_index, slot, piece):
        columns = columns_of(piece)
        return remote(
            z2_send.at[a_index, :, columns],
            z2_recv.at[slot, :, columns],
            z2_send_sem.at[0],
            z2_recv_sem.at[slot, piece],
            at(a_index, b, core),
        )

    chunk = near * 2
    expert = place // 2

    def y2_start(a_index, piece):
        for step in near_steps:
            y2_copy(a_index, step, near - step - 1, piece).start()

    def join_cores(a_index, piece):
        columns = columns_of(piece)
        core_copy(a_index, 1 - core, piece).wait_recv()
        core_sum[a_index, :, :, columns] = (
            expert_part[a_index, core, :, :, columns].astype(f32)
            + core_recv[a_index, :, :, columns].astype(f32)
        ).astype(half)

    def y2_total(a_index, piece):
        columns = columns_of(piece)
        value = core_sum[a_index, b, :, columns].astype(f32)
        for step in near_steps:
            y2_copy(a_index, step, step - 1, piece).wait_recv()
            value = value + y2_recv[step - 1, a_index, :, columns].astype(f32)
        return value

    def join_near(a_index):
        for piece in range(pieces):
            z2_send[a_index, :, columns_of(piece)] = y2_total(a_index, piece).astype(half)
            z2_copy(a_index, a, piece).start()

    def chunks(step, carry):
        a_index = paired(step)

        @pl.when(step < far - 1)
        def _():
            forward_far(paired(step + 1), parts - 1)

        forward_near(a_index, parts - 1)

        @pl.when(step < far - 1)
        def _():
            for part in range(parts - 1):
                forward_near(paired(step + 1), part)

        @pl.when(step == 1)
        def _():
            for piece in range(pieces):
                join_cores(a, piece)

        @pl.when(step > 1)
        def _():
            previous = paired(step - 1)
            for piece in range(pieces):
                join_cores(previous, piece)
                y2_start(previous, piece)

        for part in range(parts):
            for b_index in range(near):
                arrived(at(a_index, b_index, 1 - core), part)
        slots = pl.ds(a_index * chunk, chunk)
        rows = gathered[slots, :, :out_width].reshape(chunk * tokens_here, out_width)
        table = gathered[slots, :, out_width:].reshape(chunk * tokens_here, lane_count).astype(f32)
        table_lane = lax.broadcasted_iota(jnp.int32, table.shape, 1)
        mine = jnp.logical_or(table_lane == expert, table_lane == expert + experts)
        scale = jnp.sum(jnp.where(mine, table, 0.0), axis=1, keepdims=True)
        gate_part = by_rows(rows, w_gate[...])
        up_part = by_rows(rows, w_up[...])
        hidden_rows[...] = (gate_part / (1.0 + jnp.exp(-gate_part)) * up_part).astype(half)

        hidden = hidden_rows[...]
        for piece in range(pieces):
            columns = columns_of(piece)
            product = jnp.dot(hidden, w_down[:, columns], preferred_element_type=f32).astype(half)
            scaled = (product.astype(f32) * scale).astype(half)
            for b_index in range(near):
                for side in range(2):
                    start = (b_index * 2 + side) * tokens_here
                    expert_part[a_index, side, b_index, :, columns] = scaled[
                        start : start + tokens_here
                    ]
            core_copy(a_index, 1 - core, piece).start()

        @pl.when(step > 2)
        def _():
            join_near(paired(step - 2))

        return carry

    lax.fori_loop(0, far, chunks, 0)
    final = paired(far - 1)
    for piece in range(pieces):
        join_cores(final, piece)
        y2_start(final, piece)
    for piece in range(pieces):
        y2_start(a, piece)
    for step in range(max(1, far - 2), far):
        join_near(paired(step))
    for piece in range(pieces):
        columns = columns_of(piece)
        value = y2_total(a, piece)
        for step in range(1, far):
            z2_copy(paired(step), paired(step), piece).wait_recv()
            value = value + z2_recv[paired(step), :, columns].astype(f32)
        out_ref[:, columns] = value.astype(half)

    def sent(block, sem):
        remote(block, block, sem, w_recv_sem.at[0], other).wait_send()

    sent(part_send.at[pl.ds(0, far * (near - 1))], y_send_sem.at[0])
    sent(z_send.at[pl.ds(0, far - 1)], z_send_sem.at[0])
    sent(gathered.at[pl.ds(0, far - 1)], gz_send_sem.at[0])
    sent(gathered.at[pl.ds(0, far * (near - 1))], gy_send_sem.at[0])
    sent(gathered.at[pl.ds(0, chips)], gc_send_sem.at[0])
    sent(core_sum, c_send_sem.at[0])
    sent(y2_recv, y2_send_sem.at[0])
    sent(z2_send.at[pl.ds(0, far - 1)], z2_send_sem.at[0])


def layer_kernel(far, near, peers, head_dim, *refs):
    operands, out_ref, normed = refs[:11], refs[11], refs[12]
    grid_ref, qkv_hbm, w_out_hbm, gain_ref, bias_ref = operands[:5]
    scratch = refs[13:]
    vision_scratch, language_scratch = scratch[:15], scratch[15:]
    place = lax.axis_index("wide")
    devices = lax.axis_size("wide")
    barrier = greet([lax.rem(place + step, devices) for step in range(1, devices)])

    def run_vision(start_rest):
        vision_part(
            peers,
            head_dim,
            barrier,
            grid_ref,
            qkv_hbm,
            w_out_hbm,
            gain_ref,
            bias_ref,
            normed,
            *vision_scratch,
            start_rest,
        )

    language_part(far, near, run_vision, normed, *operands[5:], out_ref, *language_scratch)


def fast_local(
    qkv,
    grid,
    w_out,
    ln_gain,
    ln_bias,
    w_merge,
    w_router,
    expert_ids,
    slot_pos,
    w_gate,
    w_up,
    w_down,
):
    devices = lax.axis_size("wide")
    peers = devices // CLIPS
    patch_rows = qkv.shape[0]
    width = w_out.shape[0]
    head_dim = width // HEADS
    heads = HEADS // peers
    span = heads * head_dim
    chips = devices // 2
    near = 1
    while 4 * near * near <= chips:
        near *= 2
    far = chips // near
    rows = patch_rows // 4
    depth, out_width = w_merge.shape
    experts = w_router.shape[1]
    lanes = -(-2 * experts // 128) * 128
    hidden = w_gate.shape[2]
    whole = pl.BlockSpec(memory_space=pltpu.VMEM)
    away = pl.BlockSpec(memory_space=pl.ANY)
    half = jnp.bfloat16
    block = (rows, out_width)
    dma = pltpu.SemaphoreType.DMA
    pieces = out_width // min(512, out_width)
    return pl.pallas_call(
        functools.partial(layer_kernel, far, near, peers, head_dim),
        out_shape=jax.ShapeDtypeStruct(block, half),
        in_specs=[
            pl.BlockSpec(memory_space=pltpu.SMEM),
            away,
            away,
            whole,
            whole,
            whole,
            whole,
            away,
            away,
            away,
            away,
        ],
        out_specs=whole,
        scratch_shapes=[
            pltpu.VMEM((rows, 4 * width), half),
            pltpu.VMEM((patch_rows, 3 * width), half),
            pltpu.VMEM((peers, patch_rows, 3 * span), half),
            pltpu.VMEM((peers, patch_rows, 3 * span), half),
            pltpu.VMEM((heads, peers * patch_rows, head_dim), half),
            pltpu.VMEM((heads, peers * patch_rows, head_dim), half),
            pltpu.VMEM((peers, patch_rows + span - 128, 128), half),
            pltpu.VMEM((peers, patch_rows + span - 128, 128), half),
            pltpu.VMEM((patch_rows, width), half),
            pltpu.VMEM((width // 128, patch_rows, 128), jnp.float32),
            pltpu.VMEM((width, width), half),
            dma((peers,)),
            dma((peers,)),
            dma((peers,)),
            dma((peers,)),
            dma((4,)),
            pltpu.VMEM((lanes, out_width), half),
            pltpu.VMEM((2 * depth, out_width), half),
            pltpu.VMEM((hidden, out_width), half),
            pltpu.VMEM((hidden, out_width), half),
            pltpu.VMEM((hidden, out_width), half),
            pltpu.VMEM((chips, rows, 2 * depth), half),
            pltpu.VMEM((chips, rows, 2 * depth), half),
            pltpu.VMEM((chips, *block), half),
            pltpu.VMEM((near - 1, far, *block), half),
            pltpu.VMEM((far, *block), half),
            pltpu.VMEM((far, *block), half),
            pltpu.VMEM((devices, rows, out_width + lanes), half),
            pltpu.VMEM((2 * near * rows, hidden), half),
            pltpu.VMEM((far, 2, near, *block), half),
            pltpu.VMEM((far, near, *block), half),
            pltpu.VMEM((far, near, *block), half),
            pltpu.VMEM((near - 1, far, *block), half),
            pltpu.VMEM((far, *block), half),
            pltpu.VMEM((far, *block), half),
            dma((5,)),
            dma((1,)),
            dma((1,)),
            dma((chips,)),
            dma((chips,)),
            dma((1,)),
            dma((near - 1, far, column_parts)),
            dma((1,)),
            dma((far, column_parts)),
            dma((devices, column_parts)),
            dma((1,)),
            dma((1,)),
            dma((1,)),
            dma((1,)),
            dma((far, pieces)),
            dma((1,)),
            dma((near - 1, far, pieces)),
            dma((1,)),
            dma((far, pieces)),
        ],
        compiler_params=pltpu.CompilerParams(
            collective_id=0, has_side_effects=True, vmem_limit_bytes=62 * 2**20
        ),
        name="layer",
    )(
        grid,
        qkv,
        w_out,
        ln_gain.reshape(-1, 128),
        ln_bias.reshape(-1, 128),
        expert_ids.T,
        w_router.T,
        w_merge,
        w_gate.swapaxes(1, 2),
        w_up.swapaxes(1, 2),
        w_down,
    )


def either(*operands):
    devices = lax.axis_size("wide")
    qkv, w_router, expert_ids = operands[0], operands[6], operands[7]
    token_count = qkv.shape[0] // 4
    experts = w_router.shape[1]
    dense = 2 * token_count * expert_ids.shape[1] >= experts * token_count
    whole_heads = HEADS % (devices // CLIPS) == 0 and devices == 2 * experts
    if not (dense and whole_heads):
        return local(*operands)
    span = HEADS // (devices // CLIPS) * (operands[2].shape[0] // HEADS)
    packs = qkv.shape[0] == 128 and 128 < span < 256 and span % 16 == 0
    return fast_local(*operands) if packs else local(*operands)


def solution(mesh):
    placed = (
        P(("grp", "wide"), None),
        P("grp", None),
        P(),
        P(),
        P(),
        P("wide", None),
        P(),
        P(("grp", "wide"), None),
        P(("grp", "wide"), None),
        P("wide", None, None),
        P("wide", None, None),
        P("wide", None, None),
    )
    return jax.shard_map(
        either, mesh=mesh, in_specs=placed, out_specs=P(("grp", "wide"), None), check_vma=False
    )
```

```python
import functools

import jax
import jax.numpy as jnp
from jax import lax
from jax.experimental import pallas as pl
from jax.experimental.pallas import tpu as pltpu
from jax.sharding import PartitionSpec as P

HEADS = 16
CLIPS = 2


route_scale = 2.446
norm_eps = 1e-05
column_parts = 2


def swapped(value, axis, stride):
    mask = 2**stride
    pairs = [(source, source ^ mask) for source in range(lax.axis_size(axis))]
    return lax.ppermute(value, axis, pairs)


def ordered_pair(own_part, partner, upper_bit):
    return jnp.where(
        upper_bit == 1,
        jnp.concatenate([partner, own_part], 0),
        jnp.concatenate([own_part, partner], 0),
    )


def local(
    qkv,
    grid,
    w_out,
    ln_gain,
    ln_bias,
    w_merge,
    w_router,
    expert_ids,
    slot_pos,
    w_gate,
    w_up,
    w_down,
):
    devices = lax.axis_size("wide")
    position_self = lax.axis_index("wide")
    vit_width = w_out.shape[0]
    head_dim = vit_width // HEADS
    groups = devices // HEADS
    local_rows = qkv.shape[0]
    sub_rows = local_rows // groups
    per_clip = devices // CLIPS
    query_send = (
        qkv[:, :vit_width]
        .reshape(groups, sub_rows, HEADS, head_dim)
        .transpose(2, 0, 1, 3)
        .reshape(devices, sub_rows, head_dim)
    )
    key_value = jnp.concatenate(
        [
            qkv[:, vit_width : 2 * vit_width].reshape(local_rows, HEADS, head_dim),
            qkv[:, 2 * vit_width :].reshape(local_rows, HEADS, head_dim),
        ],
        axis=2,
    )
    spread_send = jnp.broadcast_to(
        key_value.transpose(1, 0, 2)[:, None], (HEADS, groups, local_rows, 2 * head_dim)
    ).reshape(devices, local_rows, 2 * head_dim)
    queries, key_rows = (
        lax.all_to_all(query_send, "wide", split_axis=0, concat_axis=0, tiled=True),
        lax.all_to_all(spread_send, "wide", split_axis=0, concat_axis=0, tiled=True),
    )
    key_rows = key_rows[None]
    key_groups = key_rows.shape[0]
    key_count = key_rows.shape[2]
    key_place = (
        jnp.arange(per_clip, dtype=jnp.int32)[None, :, None] * local_rows
        + jnp.arange(key_groups, dtype=jnp.int32)[:, None, None] * local_rows
        + jnp.arange(key_count, dtype=jnp.int32)[None, None, :]
    ).reshape(-1)
    patch_counts = grid[:, 0] * grid[:, 1]
    clip_queries = queries.reshape(CLIPS, per_clip * sub_rows, head_dim)
    query_block_rows = min(512, per_clip * sub_rows)
    score_scale = head_dim ** (-0.5)

    def attend(clip_index):
        key_block = lax.dynamic_slice_in_dim(key_rows, clip_index * per_clip, per_clip, 1).reshape(
            -1, 2 * head_dim
        )
        visible = key_place < lax.dynamic_index_in_dim(patch_counts, clip_index, 0, keepdims=False)
        query_all = lax.dynamic_index_in_dim(clip_queries, clip_index, 0, keepdims=False)

        def one_block(query_block):
            scores = (
                lax.dot_general(
                    query_block,
                    key_block[:, :head_dim],
                    (((1,), (1,)), ((), ())),
                    preferred_element_type=jnp.float32,
                )
                * score_scale
            )
            scores = jnp.where(visible[None, :], scores, -jnp.inf)
            highest = jnp.max(scores, axis=1, keepdims=True)
            weights = jnp.exp(scores - highest)
            running = jnp.sum(weights, axis=1, keepdims=True)
            mixture = jnp.dot(
                weights.astype(jnp.bfloat16),
                key_block[:, head_dim:],
                preferred_element_type=jnp.float32,
            )
            return (mixture / running).astype(jnp.bfloat16)

        return lax.map(one_block, query_all.reshape(-1, query_block_rows, head_dim)).reshape(
            -1, head_dim
        )

    attended = lax.map(attend, jnp.arange(CLIPS, dtype=jnp.int32))
    returned = lax.all_to_all(
        attended.reshape(devices, sub_rows, head_dim),
        "wide",
        split_axis=0,
        concat_axis=0,
        tiled=True,
    )
    attention = (
        returned.reshape(HEADS, groups, sub_rows, head_dim)
        .transpose(1, 2, 0, 3)
        .reshape(local_rows, vit_width)
    )
    projected = jnp.dot(attention, w_out, preferred_element_type=jnp.float32).astype(jnp.bfloat16)
    merged = projected.reshape(local_rows // 4, 4 * vit_width).astype(jnp.float32)
    centre = jnp.mean(merged, axis=1, keepdims=True)
    centered = merged - centre
    spread = jnp.mean(centered * centered, axis=1, keepdims=True)
    normed = (centered * lax.rsqrt(spread + norm_eps) * ln_gain + ln_bias).astype(jnp.bfloat16)
    tok_groups = min(8, devices)
    feat_groups = devices // tok_groups
    merge_rows = w_merge
    for bit_index in range(tok_groups.bit_length() - 1):
        partner = swapped(merge_rows, "wide", bit_index)
        upper_bit = position_self // (1 << bit_index) % 2
        merge_rows = ordered_pair(merge_rows, partner, upper_bit)
    token_count = normed.shape[0]
    part_rows = token_count // tok_groups
    feat_width = normed.shape[1] // feat_groups
    out_width = w_merge.shape[1]
    merge_send = (
        normed.reshape(tok_groups, part_rows, feat_groups, feat_width)
        .transpose(2, 0, 1, 3)
        .reshape(devices, part_rows, feat_width)
    )
    flat_rows = lax.all_to_all(merge_send, "wide", split_axis=0, concat_axis=0, tiled=True).reshape(
        -1, feat_width
    )
    partial_value = jnp.dot(flat_rows, merge_rows, preferred_element_type=jnp.float32).reshape(
        devices, -1, out_width
    )
    summed = lax.all_to_all(partial_value, "wide", split_axis=0, concat_axis=0, tiled=True)
    tokens = (
        jnp.sum(summed.reshape(feat_groups, tok_groups, part_rows, out_width), axis=0)
        .reshape(token_count, out_width)
        .astype(jnp.bfloat16)
    )
    logits = jnp.dot(tokens, w_router, preferred_element_type=jnp.float32)
    experts = w_router.shape[1]
    top_count = expert_ids.shape[1]
    matches = expert_ids[:, :, None] == jnp.arange(experts, dtype=jnp.int32)[None, None, :]
    chosen = jnp.sum(jnp.where(matches, logits[:, None, :], 0.0), axis=2)
    gate_values = jax.nn.sigmoid(chosen)
    route_weight = route_scale * gate_values / jnp.sum(gate_values, axis=1, keepdims=True)
    capacity = min(token_count, 2 * token_count * top_count // experts)
    slot_count = experts * capacity
    target = expert_ids * capacity + slot_pos
    one_hot = jnp.any(
        target[None, :, :] == jnp.arange(slot_count, dtype=jnp.int32)[:, None, None], axis=2
    ).astype(jnp.bfloat16)
    buffer = jnp.dot(one_hot, tokens, preferred_element_type=jnp.float32).astype(jnp.bfloat16)
    gate_half = w_gate[0]
    up_half = w_up[0]
    down_half = w_down[0]
    half_cap = capacity // 2
    dispatch = buffer.reshape(devices, half_cap, out_width)
    portion = lax.all_to_all(dispatch, "wide", split_axis=0, concat_axis=0, tiled=True)
    item_count = portion.shape[1]
    partner_rows = swapped(portion, "wide", 0)
    both_rows = jnp.concatenate([portion, partner_rows], axis=1)
    flat_rows = both_rows.reshape(-1, out_width)
    gate_part = jnp.dot(flat_rows, gate_half, preferred_element_type=jnp.float32)
    up_part = jnp.dot(flat_rows, up_half, preferred_element_type=jnp.float32)
    hidden = (jax.nn.silu(gate_part) * up_part).astype(jnp.bfloat16)
    product = (
        jnp.dot(hidden, down_half, preferred_element_type=jnp.float32)
        .astype(jnp.bfloat16)
        .reshape(devices, 2 * item_count, out_width)
    )
    from_partner = swapped(product[:, item_count:], "wide", 0)
    joined = (
        product[:, :item_count].astype(jnp.float32) + from_partner.astype(jnp.float32)
    ).astype(jnp.bfloat16)
    answers = lax.all_to_all(joined, "wide", split_axis=0, concat_axis=0, tiled=True)
    slot_result = answers.reshape(slot_count, out_width)
    slot_result = lax.optimization_barrier(slot_result)
    picked = jnp.take(slot_result, target.reshape(-1), axis=0).reshape(
        token_count, top_count, out_width
    )
    return jnp.sum(picked.astype(jnp.float32) * route_weight[:, :, None], axis=1).astype(
        jnp.bfloat16
    )


def remote(source, target, send_sem, recv_sem, place):
    return pltpu.make_async_remote_copy(
        src_ref=source,
        dst_ref=target,
        send_sem=send_sem,
        recv_sem=recv_sem,
        device_id={"wide": place},
        device_id_type=pl.DeviceIdType.MESH,
    )


def by_rows(left, right):
    return lax.dot_general(
        left, right, (((1,), (1,)), ((), ())), preferred_element_type=jnp.float32
    )


def greet(places):
    barrier = pltpu.get_barrier_semaphore()
    for place in places:
        pl.semaphore_signal(
            barrier, inc=1, device_id={"wide": place}, device_id_type=pl.DeviceIdType.MESH
        )
    return barrier


def vision_part(
    peers,
    head_dim,
    barrier,
    grid_ref,
    qkv_hbm,
    w_out_hbm,
    gain_ref,
    bias_ref,
    out_ref,
    qkv_ref,
    pair_send,
    pair_recv,
    value_send,
    value_recv,
    queries,
    keys,
    values,
    weights_kept,
    sums_kept,
    mixed_send,
    mixed_recv,
    attention,
    mixed,
    w_out_ref,
    send_sem,
    recv_sem,
    back_send_sem,
    back_recv_sem,
    local_sem,
    start_rest,
):
    place = lax.axis_index("wide")
    base = place // peers * peers
    me = place - base
    rows = qkv_ref.shape[0]
    width = w_out_hbm.shape[0]
    heads = HEADS // peers
    span = heads * head_dim
    devices = lax.axis_size("wide")
    qkv_copy = pltpu.make_async_copy(qkv_hbm, qkv_ref, local_sem.at[3])
    qkv_copy.start()
    weight_copy = pltpu.make_async_copy(w_out_hbm, w_out_ref, local_sem.at[0])
    weight_copy.start()
    qkv_copy.wait()
    tail = span - 128
    for part, (packed, first, last) in enumerate(
        [
            (pair_send, 0, 2 * rows),
            (pair_send, rows, 2 * rows + tail),
            (value_send, 0, rows),
        ]
    ):
        ends = [part * width + (peer + 1) * span for peer in range(peers)]
        tails = jnp.concatenate([qkv_ref[:, end - tail : end] for end in ends], axis=1)
        turned = tails.astype(jnp.float32).T
        for peer, end in enumerate(ends):
            packed[peer, first : first + rows, :] = qkv_ref[:, end - span : end - tail]
            packed[peer, last : last + tail, :] = turned[
                peer * tail : (peer + 1) * tail
            ].astype(jnp.bfloat16)
    pl.semaphore_wait(barrier, devices - 1)
    own_pair = pltpu.make_async_copy(pair_send.at[me], pair_recv.at[me], local_sem.at[1])
    own_value = pltpu.make_async_copy(value_send.at[me], value_recv.at[me], local_sem.at[4])
    own_pair.start()
    own_value.start()
    for kind, (source, target) in enumerate(
        [(pair_send, pair_recv), (value_send, value_recv)]
    ):
        for step in range(1, peers):
            peer = lax.rem(me + step, peers)
            remote(
                source.at[peer], target.at[me], send_sem.at[kind], recv_sem.at[kind], base + peer
            ).start()
    start_rest()

    def whole(block, kind):
        block = block.at[pl.ds(0, peers - 1)]
        return remote(
            block, block, send_sem.at[kind], recv_sem.at[kind], base + lax.rem(me + 1, peers)
        )

    own_pair.wait()
    whole(pair_recv, 0).wait_recv()

    def unpack(packed, first, last, target):
        turned = (
            packed[:, last : last + tail, :].astype(jnp.float32).reshape(peers * tail, rows).T
        )
        for peer in range(peers):
            joined = jnp.concatenate(
                [
                    packed[peer, first : first + rows, :],
                    turned[:, peer * tail : (peer + 1) * tail].astype(jnp.bfloat16),
                ],
                axis=1,
            )
            for head in range(heads):
                target[head, peer * rows : (peer + 1) * rows, :] = joined[
                    :, head * head_dim : (head + 1) * head_dim
                ]

    unpack(pair_recv, 0, 2 * rows, queries)
    unpack(pair_recv, rows, 2 * rows + tail, keys)
    factor = head_dim ** (-0.5) * 1.4426950408889634
    clip = place // peers
    count = grid_ref[clip, 0] * grid_ref[clip, 1]
    visible = lax.broadcasted_iota(jnp.int32, (1, peers * rows), 1) < count
    hide = jnp.where(visible, 0.0, -jnp.inf)
    group = 2 if peers % 2 == 0 else 1
    blocks = peers // group

    def score_block(block, carry):
        lines = pl.ds(pl.multiple_of(block * group * rows, group * rows), group * rows)
        for head in range(heads):
            scores = lax.dot_general(
                queries[head, lines, :], keys[head], (((1,), (1,)), ((), ())), preferred_element_type=jnp.float32
            )
            scores = scores + hide
            highest = jnp.max(scores, axis=1, keepdims=True)
            weights = jnp.exp2((scores - highest) * factor)
            sums_kept[head, lines, :] = jnp.sum(weights, axis=1, keepdims=True)
            weights_kept[head, lines, :] = weights.astype(jnp.bfloat16)
        return carry

    lax.fori_loop(0, blocks, score_block, 0)
    own_value.wait()
    whole(value_recv, 1).wait_recv()
    unpack(value_recv, 0, rows, values)

    def one_block(step, carry):
        block = lax.rem(me // group + 1 + step, blocks)
        lines = pl.ds(pl.multiple_of(block * group * rows, group * rows), group * rows)
        outcomes = []
        for head in range(heads):
            mixture = jnp.dot(
                weights_kept[head, lines, :], values[head], preferred_element_type=jnp.float32
            )
            outcomes.append((mixture / sums_kept[head, lines, :]).astype(jnp.bfloat16))
        joined = jnp.concatenate([piece.astype(jnp.float32) for piece in outcomes], axis=1)
        for part in range(group):
            peer = block * group + part
            mine = joined[part * rows : (part + 1) * rows]
            mixed_send[peer, :rows, :] = mine[:, :128].astype(jnp.bfloat16)
            tail = jnp.concatenate(
                [mine[:, 128:], jnp.zeros((rows, 256 - span), jnp.float32)], axis=1
            )
            mixed_send[peer, rows:, :] = tail.T[: span - 128].astype(jnp.bfloat16)

            @pl.when(peer != me)
            def _():
                remote(
                    mixed_send.at[peer],
                    mixed_recv.at[me],
                    back_send_sem.at[0],
                    back_recv_sem.at[0],
                    base + peer,
                ).start()

            @pl.when(peer == me)
            def _():
                pltpu.make_async_copy(
                    mixed_send.at[me], mixed_recv.at[me], local_sem.at[2]
                ).start()

        return carry

    lax.fori_loop(0, blocks, one_block, 0)
    pltpu.make_async_copy(mixed_send.at[me], mixed_recv.at[me], local_sem.at[2]).wait()
    returned = mixed_recv.at[pl.ds(0, peers - 1)]
    back = remote(
        returned,
        returned,
        back_send_sem.at[0],
        back_recv_sem.at[0],
        base + lax.rem(me + 1, peers),
    )
    back.wait_recv()
    back.wait_send()
    whole(pair_send, 0).wait_send()
    whole(value_send, 1).wait_send()
    for peer in range(peers):
        start = peer * span
        attention[:, start : start + 128] = mixed_recv[peer, :rows, :]
        tail = mixed_recv[peer, rows:, :].astype(jnp.float32).T
        attention[:, start + 128 : start + span] = tail.astype(jnp.bfloat16)
    weight_copy.wait()
    projected = (
        jnp.dot(attention[...], w_out_ref[...], preferred_element_type=jnp.float32)
        .astype(jnp.bfloat16)
        .astype(jnp.float32)
    )
    tiles = width // 128
    for tile in range(tiles):
        mixed[tile] = projected[:, tile * 128 : (tile + 1) * 128]
    pieces = [
        [mixed[tile, pl.ds(part, rows // 4, stride=4), :] for tile in range(tiles)]
        for part in range(4)
    ]
    total_width = 4 * width
    flat = [piece for row in pieces for piece in row]
    centre = jnp.sum(sum(flat), axis=1, keepdims=True) / total_width
    spread = (
        jnp.sum(sum((piece - centre) * (piece - centre) for piece in flat), axis=1, keepdims=True)
        / total_width
    )
    inverse = lax.rsqrt(spread + norm_eps)
    for index, piece in enumerate(flat):
        out_ref[:, index * 128 : (index + 1) * 128] = (
            (piece - centre) * inverse * gain_ref[index : index + 1, :]
            + bias_ref[index : index + 1, :]
        ).astype(jnp.bfloat16)


def language_part(
    far,
    near,
    run_vision,
    normed_ref,
    ids_ref,
    router_hbm,
    w_merge_hbm,
    w_gate_hbm,
    w_up_hbm,
    w_down_hbm,
    out_ref,
    router_ref,
    merge_rows,
    w_gate,
    w_up,
    w_down,
    norm_send,
    norm_recv,
    part_send,
    y_recv,
    z_send,
    z_recv,
    gathered,
    gate_rows,
    expert_part,
    core_recv,
    core_sum,
    y2_recv,
    z2_send,
    z2_recv,
    local_sem,
    w_send_sem,
    w_recv_sem,
    n_send_sem,
    n_recv_sem,
    y_send_sem,
    y_recv_sem,
    z_send_sem,
    z_recv_sem,
    g_recv_sem,
    gz_send_sem,
    gy_send_sem,
    gc_send_sem,
    c_send_sem,
    c_recv_sem,
    y2_send_sem,
    y2_recv_sem,
    z2_send_sem,
    z2_recv_sem,
):
    place = lax.axis_index("wide")
    chips = far * near
    core = lax.rem(place, 2)
    chip = place // 2
    a = chip // near
    b = lax.rem(chip, near)
    other = place + 1 - 2 * core
    tokens_here = normed_ref.shape[0]
    depth = w_merge_hbm.shape[0]
    out_width = w_merge_hbm.shape[1]
    experts = chips
    f32 = jnp.float32
    half = jnp.bfloat16

    def at(a_index, b_index, c_index):
        return (a_index * near + b_index) * 2 + c_index

    other_chips = [lax.rem(chip + step, chips) for step in range(1, chips)]
    weight_copies = [
        pltpu.make_async_copy(w_gate_hbm.at[0], w_gate, local_sem.at[0]),
        pltpu.make_async_copy(w_up_hbm.at[0], w_up, local_sem.at[1]),
        pltpu.make_async_copy(w_down_hbm.at[0], w_down, local_sem.at[2]),
    ]
    own_rows = merge_rows.at[pl.ds(core * depth, depth)]
    merge_copy = pltpu.make_async_copy(w_merge_hbm, own_rows, local_sem.at[3])
    merge_swap = remote(w_merge_hbm, own_rows, w_send_sem.at[0], w_recv_sem.at[0], other)

    def start_rest():
        merge_swap.start()
        merge_copy.start()
        for copy in weight_copies:
            copy.start()
        named_rows = router_hbm[...].astype(f32)
        router_ref[...] = jnp.concatenate(
            [
                named_rows,
                named_rows,
                jnp.zeros((router_ref.shape[0] - 2 * experts, out_width), f32),
            ],
            axis=0,
        ).astype(half)

    run_vision(start_rest)
    for q in range(chips):
        norm_send[q] = normed_ref[:, 2 * depth * q : 2 * depth * (q + 1)]
    own_norm = pltpu.make_async_copy(norm_send.at[chip], norm_recv.at[chip], local_sem.at[4])
    own_norm.start()
    for q in other_chips:
        remote(
            norm_send.at[q], norm_recv.at[chip], n_send_sem.at[0], n_recv_sem.at[0], q * 2 + core
        ).start()
    merge_copy.wait()
    merge_swap.wait_send()
    remote(
        w_merge_hbm,
        merge_rows.at[pl.ds((1 - core) * depth, depth)],
        w_send_sem.at[0],
        w_recv_sem.at[0],
        other,
    ).wait_recv()
    own_norm.wait()
    arrivals = norm_recv.at[pl.ds(0, chips - 1)]
    normed_copies = remote(arrivals, arrivals, n_send_sem.at[0], n_recv_sem.at[0], other)
    normed_copies.wait_recv()
    normed_copies.wait_send()
    column_block = min(512, out_width)
    flat = norm_recv[...].reshape(chips * tokens_here, 2 * depth)

    def merge_columns(index, carry):
        columns = pl.ds(pl.multiple_of(index * column_block, column_block), column_block)
        part_send[:, :, columns] = (
            jnp.dot(flat, merge_rows[:, columns], preferred_element_type=f32)
            .astype(half)
            .reshape(chips, tokens_here, column_block)
        )
        return carry

    lax.fori_loop(0, out_width // column_block, merge_columns, 0)

    near_steps = range(1, near)
    pieces = out_width // column_block
    parts = column_parts
    part_width = out_width // parts

    def columns_of(piece):
        return pl.ds(piece * column_block, column_block)

    def part_of(part):
        return pl.ds(part * part_width, part_width)

    def paired(step):
        value, bit = 0, 1
        while bit < far:
            mine, theirs = a // bit % 2, step // bit % 2
            value = value + bit * (mine + theirs - 2 * mine * theirs)
            bit *= 2
        return value

    def y_copy(a_index, step, slot, part):
        target = lax.rem(b + step, near)
        columns = part_of(part)
        return remote(
            part_send.at[a_index * near + target, :, columns],
            y_recv.at[slot, a_index, :, columns],
            y_send_sem.at[0],
            y_recv_sem.at[slot, a_index, part],
            at(a, target, core),
        )

    def y_total(a_index, part):
        columns = part_of(part)
        value = part_send[a_index * near + b, :, columns].astype(f32)
        for step in near_steps:
            y_copy(a_index, step, step - 1, part).wait_recv()
            value = value + y_recv[step - 1, a_index, :, columns].astype(f32)
        return value

    def z_copy(a_index, slot, part):
        columns = part_of(part)
        return remote(
            z_send.at[a_index, :, columns],
            z_recv.at[slot, :, columns],
            z_send_sem.at[0],
            z_recv_sem.at[slot, part],
            at(a_index, b, core),
        )

    far_targets = [paired(step) for step in range(far - 1, 0, -1)]
    for part in range(parts):
        for a_index in far_targets + [a]:
            for step in near_steps:
                y_copy(a_index, step, near - step - 1, part).start()

    def merge_far(part):
        for a_index in far_targets:
            z_send[a_index, :, part_of(part)] = y_total(a_index, part).astype(half)
            z_copy(a_index, a, part).start()

    def merge_own(part):
        columns = part_of(part)
        value = y_total(a, part)
        for a_index in far_targets:
            z_copy(a_index, a_index, part).wait_recv()
            value = value + z_recv[a_index, :, columns].astype(f32)
        gathered[place, :, columns] = value.astype(half)

    lane_count = router_ref.shape[0]

    def span_of(part):
        extra = lane_count if part == parts - 1 else 0
        return pl.ds(part * part_width, part_width + extra)

    def share(slot, send_sem, target, part):
        block = gathered.at[slot, :, span_of(part)]
        return remote(block, block, send_sem, g_recv_sem.at[slot, part], target)

    def arrived(slot, part):
        share(slot, gc_send_sem.at[0], other, part).wait_recv()

    def to_far(a_index, part):
        return share(place, gz_send_sem.at[0], at(a_index, b, core), part)

    def to_near(a_index, step, part):
        return share(
            at(a_index, b, core),
            gy_send_sem.at[0],
            at(a, lax.rem(b + step, near), core),
            part,
        )

    def to_core(a_index, b_index, part):
        return share(at(a_index, b_index, core), gc_send_sem.at[0], other, part)

    def pass_on(a_index, part):
        for step in near_steps:
            to_near(a_index, step, part).start()
        to_core(a_index, b, part).start()

    def turn(step):
        value, bit = 0, 1
        while bit < far:
            wide_bit, next_bit = far // (2 * bit), far // bit
            value = value + bit * ((step // wide_bit + step // next_bit) % 2)
            bit *= 2
        return paired(value)

    def share_own(part):
        for step in range(1, far):
            to_far(turn(step), part).start()
        pass_on(a, part)

    def forward_far(a_index, part):
        arrived(at(a_index, b, core), part)
        pass_on(a_index, part)

    def forward_near(a_index, part):
        for step in near_steps:
            b_index = lax.rem(b + step, near)
            arrived(at(a_index, b_index, core), part)
            to_core(a_index, b_index, part).start()

    for part in range(parts):
        merge_far(part)
    for part in range(parts - 1):
        merge_own(part)
        share_own(part)
    merge_own(parts - 1)
    tokens = gathered[place, :, :out_width]

    logits = by_rows(tokens, router_ref[...])
    lane = lax.broadcasted_iota(jnp.int32, (tokens_here, lane_count), 1)
    line = lax.broadcasted_iota(jnp.int32, (lane_count, tokens_here), 0)
    line = jnp.where(line < experts, line, line - experts)
    marks = jnp.zeros((lane_count, tokens_here), f32)
    for k in range(ids_ref.shape[0]):
        marks = jnp.where(line == ids_ref[k : k + 1, :], 1.0, marks)
    same = (
        lax.broadcasted_iota(jnp.int32, (tokens_here, tokens_here), 0)
        == lax.broadcasted_iota(jnp.int32, (tokens_here, tokens_here), 1)
    )
    chosen = by_rows(jnp.where(same, 1.0, 0.0).astype(half), marks.astype(half))
    gates = chosen / (1.0 + jnp.exp(-logits))
    gate_sum = jnp.sum(jnp.where(lane < experts, gates, 0.0), axis=1, keepdims=True)
    route = route_scale * gates / gate_sum
    route_high = route.astype(half)
    route_low = (route - route_high.astype(f32)).astype(half)
    gathered[place, :, out_width:] = jnp.where(lane < experts, route_high.astype(f32), route_low.astype(f32)).astype(half)

    share_own(parts - 1)
    for part in range(parts - 1):
        forward_far(turn(1), part)
        forward_near(a, part)
        for step in range(2, far):
            forward_far(turn(step), part)
    for copy in weight_copies:
        copy.wait()

    def core_copy(a_index, side, piece):
        columns = columns_of(piece)
        return remote(
            expert_part.at[a_index, side, :, :, columns],
            core_recv.at[a_index, :, :, columns],
            c_send_sem.at[0],
            c_recv_sem.at[a_index, piece],
            other,
        )

    def y2_copy(a_index, step, slot, piece):
        target = lax.rem(b + step, near)
        columns = columns_of(piece)
        return remote(
            core_sum.at[a_index, target, :, columns],
            y2_recv.at[slot, a_index, :, columns],
            y2_send_sem.at[0],
            y2_recv_sem.at[slot, a_index, piece],
            at(a, target, core),
        )

    def z2_copy(a_index, slot, piece):
        columns = columns_of(piece)
        return remote(
            z2_send.at[a_index, :, columns],
            z2_recv.at[slot, :, columns],
            z2_send_sem.at[0],
            z2_recv_sem.at[slot, piece],
            at(a_index, b, core),
        )

    chunk = near * 2
    expert = place // 2

    def y2_start(a_index, piece):
        for step in near_steps:
            y2_copy(a_index, step, near - step - 1, piece).start()

    def join_cores(a_index, piece):
        columns = columns_of(piece)
        core_copy(a_index, 1 - core, piece).wait_recv()
        core_sum[a_index, :, :, columns] = (
            expert_part[a_index, core, :, :, columns].astype(f32)
            + core_recv[a_index, :, :, columns].astype(f32)
        ).astype(half)

    def y2_total(a_index, piece):
        columns = columns_of(piece)
        value = core_sum[a_index, b, :, columns].astype(f32)
        for step in near_steps:
            y2_copy(a_index, step, step - 1, piece).wait_recv()
            value = value + y2_recv[step - 1, a_index, :, columns].astype(f32)
        return value

    def join_near(a_index):
        for piece in range(pieces):
            z2_send[a_index, :, columns_of(piece)] = y2_total(a_index, piece).astype(half)
            z2_copy(a_index, a, piece).start()

    def chunks(step, carry):
        a_index = turn(step)

        @pl.when(step < far - 1)
        def _():
            forward_far(turn(step + 1), parts - 1)

        forward_near(a_index, parts - 1)

        @pl.when(step < far - 1)
        def _():
            for part in range(parts - 1):
                forward_near(turn(step + 1), part)

        @pl.when(step == 1)
        def _():
            for piece in range(pieces):
                join_cores(a, piece)

        @pl.when(step > 1)
        def _():
            previous = turn(step - 1)
            for piece in range(pieces):
                join_cores(previous, piece)
                y2_start(previous, piece)

        for part in range(parts):
            for b_index in range(near):
                arrived(at(a_index, b_index, 1 - core), part)
        slots = pl.ds(a_index * chunk, chunk)
        rows = gathered[slots, :, :out_width].reshape(chunk * tokens_here, out_width)
        table = gathered[slots, :, out_width:].reshape(chunk * tokens_here, lane_count).astype(f32)
        table_lane = lax.broadcasted_iota(jnp.int32, table.shape, 1)
        mine = jnp.logical_or(table_lane == expert, table_lane == expert + experts)
        scale = jnp.sum(jnp.where(mine, table, 0.0), axis=1, keepdims=True)
        gate_rows[...] = by_rows(rows, w_gate[...])
        gate_part = gate_rows[...]
        up_part = by_rows(rows, w_up[...])
        hidden = (gate_part / (1.0 + jnp.exp(-gate_part)) * up_part).astype(half)

        for piece in range(pieces):
            columns = columns_of(piece)
            product = jnp.dot(hidden, w_down[:, columns], preferred_element_type=f32).astype(half)
            scaled = (product.astype(f32) * scale).astype(half)
            for b_index in range(near):
                for side in range(2):
                    start = (b_index * 2 + side) * tokens_here
                    expert_part[a_index, side, b_index, :, columns] = scaled[
                        start : start + tokens_here
                    ]
            core_copy(a_index, 1 - core, piece).start()

        @pl.when(step > 2)
        def _():
            join_near(turn(step - 2))

        return carry

    lax.fori_loop(0, far, chunks, 0)
    final = turn(far - 1)
    for piece in range(pieces):
        join_cores(final, piece)
        y2_start(final, piece)
    for piece in range(pieces):
        y2_start(a, piece)
    for step in range(max(1, far - 2), far):
        join_near(turn(step))
    for piece in range(pieces):
        columns = columns_of(piece)
        value = y2_total(a, piece)
        for step in range(1, far):
            z2_copy(turn(step), turn(step), piece).wait_recv()
            value = value + z2_recv[turn(step), :, columns].astype(f32)
        out_ref[:, columns] = value.astype(half)

    def sent(block, sem):
        remote(block, block, sem, w_recv_sem.at[0], other).wait_send()

    sent(part_send.at[pl.ds(0, far * (near - 1))], y_send_sem.at[0])
    sent(z_send.at[pl.ds(0, far - 1)], z_send_sem.at[0])
    sent(gathered.at[pl.ds(0, far - 1)], gz_send_sem.at[0])
    sent(gathered.at[pl.ds(0, far * (near - 1))], gy_send_sem.at[0])
    sent(gathered.at[pl.ds(0, chips)], gc_send_sem.at[0])
    sent(core_sum, c_send_sem.at[0])
    sent(y2_recv, y2_send_sem.at[0])
    sent(z2_send.at[pl.ds(0, far - 1)], z2_send_sem.at[0])


def layer_kernel(far, near, peers, head_dim, *refs):
    operands, out_ref, normed = refs[:11], refs[11], refs[12]
    grid_ref, qkv_hbm, w_out_hbm, gain_ref, bias_ref = operands[:5]
    scratch = refs[13:]
    vision_scratch, language_scratch = scratch[:20], scratch[20:]
    place = lax.axis_index("wide")
    devices = lax.axis_size("wide")
    barrier = greet([lax.rem(place + step, devices) for step in range(1, devices)])

    def run_vision(start_rest):
        vision_part(
            peers,
            head_dim,
            barrier,
            grid_ref,
            qkv_hbm,
            w_out_hbm,
            gain_ref,
            bias_ref,
            normed,
            *vision_scratch,
            start_rest,
        )

    language_part(far, near, run_vision, normed, *operands[5:], out_ref, *language_scratch)


def fast_local(
    qkv,
    grid,
    w_out,
    ln_gain,
    ln_bias,
    w_merge,
    w_router,
    expert_ids,
    slot_pos,
    w_gate,
    w_up,
    w_down,
):
    devices = lax.axis_size("wide")
    peers = devices // CLIPS
    patch_rows = qkv.shape[0]
    width = w_out.shape[0]
    head_dim = width // HEADS
    heads = HEADS // peers
    span = heads * head_dim
    chips = devices // 2
    near = 1
    while 4 * near * near <= chips:
        near *= 2
    far = chips // near
    rows = patch_rows // 4
    depth, out_width = w_merge.shape
    experts = w_router.shape[1]
    lanes = -(-2 * experts // 128) * 128
    hidden = w_gate.shape[2]
    whole = pl.BlockSpec(memory_space=pltpu.VMEM)
    away = pl.BlockSpec(memory_space=pl.ANY)
    half = jnp.bfloat16
    block = (rows, out_width)
    dma = pltpu.SemaphoreType.DMA
    pieces = out_width // min(512, out_width)
    return pl.pallas_call(
        functools.partial(layer_kernel, far, near, peers, head_dim),
        out_shape=jax.ShapeDtypeStruct(block, half),
        in_specs=[
            pl.BlockSpec(memory_space=pltpu.SMEM),
            away,
            away,
            whole,
            whole,
            whole,
            whole,
            away,
            away,
            away,
            away,
        ],
        out_specs=whole,
        scratch_shapes=[
            pltpu.VMEM((rows, 4 * width), half),
            pltpu.VMEM((patch_rows, 3 * width), half),
            pltpu.VMEM((peers, 2 * (patch_rows + span - 128), 128), half),
            pltpu.VMEM((peers, 2 * (patch_rows + span - 128), 128), half),
            pltpu.VMEM((peers, patch_rows + span - 128, 128), half),
            pltpu.VMEM((peers, patch_rows + span - 128, 128), half),
            pltpu.VMEM((heads, peers * patch_rows, head_dim), half),
            pltpu.VMEM((heads, peers * patch_rows, head_dim), half),
            pltpu.VMEM((heads, peers * patch_rows, head_dim), half),
            pltpu.VMEM((heads, peers * patch_rows, peers * patch_rows), half),
            pltpu.VMEM((heads, peers * patch_rows, 1), jnp.float32),
            pltpu.VMEM((peers, patch_rows + span - 128, 128), half),
            pltpu.VMEM((peers, patch_rows + span - 128, 128), half),
            pltpu.VMEM((patch_rows, width), half),
            pltpu.VMEM((width // 128, patch_rows, 128), jnp.float32),
            pltpu.VMEM((width, width), half),
            dma((2,)),
            dma((2,)),
            dma((1,)),
            dma((1,)),
            dma((5,)),
            pltpu.VMEM((lanes, out_width), half),
            pltpu.VMEM((2 * depth, out_width), half),
            pltpu.VMEM((hidden, out_width), half),
            pltpu.VMEM((hidden, out_width), half),
            pltpu.VMEM((hidden, out_width), half),
            pltpu.VMEM((chips, rows, 2 * depth), half),
            pltpu.VMEM((chips, rows, 2 * depth), half),
            pltpu.VMEM((chips, *block), half),
            pltpu.VMEM((near - 1, far, *block), half),
            pltpu.VMEM((far, *block), half),
            pltpu.VMEM((far, *block), half),
            pltpu.VMEM((devices, rows, out_width + lanes), half),
            pltpu.VMEM((2 * near * rows, hidden), jnp.float32),
            pltpu.VMEM((far, 2, near, *block), half),
            pltpu.VMEM((far, near, *block), half),
            pltpu.VMEM((far, near, *block), half),
            pltpu.VMEM((near - 1, far, *block), half),
            pltpu.VMEM((far, *block), half),
            pltpu.VMEM((far, *block), half),
            dma((5,)),
            dma((1,)),
            dma((1,)),
            dma((1,)),
            dma((1,)),
            dma((1,)),
            dma((near - 1, far, column_parts)),
            dma((1,)),
            dma((far, column_parts)),
            dma((devices, column_parts)),
            dma((1,)),
            dma((1,)),
            dma((1,)),
            dma((1,)),
            dma((far, pieces)),
            dma((1,)),
            dma((near - 1, far, pieces)),
            dma((1,)),
            dma((far, pieces)),
        ],
        compiler_params=pltpu.CompilerParams(
            collective_id=0, has_side_effects=True, vmem_limit_bytes=62 * 2**20
        ),
        name="layer",
    )(
        grid,
        qkv,
        w_out,
        ln_gain.reshape(-1, 128),
        ln_bias.reshape(-1, 128),
        expert_ids.T,
        w_router.T,
        w_merge,
        w_gate.swapaxes(1, 2),
        w_up.swapaxes(1, 2),
        w_down,
    )


def either(*operands):
    devices = lax.axis_size("wide")
    qkv, w_router, expert_ids = operands[0], operands[6], operands[7]
    token_count = qkv.shape[0] // 4
    experts = w_router.shape[1]
    dense = 2 * token_count * expert_ids.shape[1] >= experts * token_count
    whole_heads = HEADS % (devices // CLIPS) == 0 and devices == 2 * experts
    if not (dense and whole_heads):
        return local(*operands)
    span = HEADS // (devices // CLIPS) * (operands[2].shape[0] // HEADS)
    packs = qkv.shape[0] == 128 and 128 < span < 256 and span % 16 == 0
    return fast_local(*operands) if packs else local(*operands)


def solution(mesh):
    placed = (
        P(("grp", "wide"), None),
        P("grp", None),
        P(),
        P(),
        P(),
        P("wide", None),
        P(),
        P(("grp", "wide"), None),
        P(("grp", "wide"), None),
        P("wide", None, None),
        P("wide", None, None),
        P("wide", None, None),
    )
    return jax.shard_map(
        either, mesh=mesh, in_specs=placed, out_specs=P(("grp", "wide"), None), check_vma=False
    )
```

```python
import functools

import jax
import jax.numpy as jnp
from jax import lax
from jax.experimental import pallas as pl
from jax.experimental.pallas import tpu as pltpu
from jax.sharding import PartitionSpec as P

HEADS = 16
CLIPS = 2


route_scale = 2.446
norm_eps = 1e-05
column_parts = 2


def swapped(value, axis, stride):
    mask = 2**stride
    pairs = [(source, source ^ mask) for source in range(lax.axis_size(axis))]
    return lax.ppermute(value, axis, pairs)


def ordered_pair(own_part, partner, upper_bit):
    return jnp.where(
        upper_bit == 1,
        jnp.concatenate([partner, own_part], 0),
        jnp.concatenate([own_part, partner], 0),
    )


def local(
    qkv,
    grid,
    w_out,
    ln_gain,
    ln_bias,
    w_merge,
    w_router,
    expert_ids,
    slot_pos,
    w_gate,
    w_up,
    w_down,
):
    devices = lax.axis_size("wide")
    position_self = lax.axis_index("wide")
    vit_width = w_out.shape[0]
    head_dim = vit_width // HEADS
    groups = devices // HEADS
    local_rows = qkv.shape[0]
    sub_rows = local_rows // groups
    per_clip = devices // CLIPS
    query_send = (
        qkv[:, :vit_width]
        .reshape(groups, sub_rows, HEADS, head_dim)
        .transpose(2, 0, 1, 3)
        .reshape(devices, sub_rows, head_dim)
    )
    key_value = jnp.concatenate(
        [
            qkv[:, vit_width : 2 * vit_width].reshape(local_rows, HEADS, head_dim),
            qkv[:, 2 * vit_width :].reshape(local_rows, HEADS, head_dim),
        ],
        axis=2,
    )
    spread_send = jnp.broadcast_to(
        key_value.transpose(1, 0, 2)[:, None], (HEADS, groups, local_rows, 2 * head_dim)
    ).reshape(devices, local_rows, 2 * head_dim)
    queries, key_rows = (
        lax.all_to_all(query_send, "wide", split_axis=0, concat_axis=0, tiled=True),
        lax.all_to_all(spread_send, "wide", split_axis=0, concat_axis=0, tiled=True),
    )
    key_rows = key_rows[None]
    key_groups = key_rows.shape[0]
    key_count = key_rows.shape[2]
    key_place = (
        jnp.arange(per_clip, dtype=jnp.int32)[None, :, None] * local_rows
        + jnp.arange(key_groups, dtype=jnp.int32)[:, None, None] * local_rows
        + jnp.arange(key_count, dtype=jnp.int32)[None, None, :]
    ).reshape(-1)
    patch_counts = grid[:, 0] * grid[:, 1]
    clip_queries = queries.reshape(CLIPS, per_clip * sub_rows, head_dim)
    query_block_rows = min(512, per_clip * sub_rows)
    score_scale = head_dim ** (-0.5)

    def attend(clip_index):
        key_block = lax.dynamic_slice_in_dim(key_rows, clip_index * per_clip, per_clip, 1).reshape(
            -1, 2 * head_dim
        )
        visible = key_place < lax.dynamic_index_in_dim(patch_counts, clip_index, 0, keepdims=False)
        query_all = lax.dynamic_index_in_dim(clip_queries, clip_index, 0, keepdims=False)

        def one_block(query_block):
            scores = (
                lax.dot_general(
                    query_block,
                    key_block[:, :head_dim],
                    (((1,), (1,)), ((), ())),
                    preferred_element_type=jnp.float32,
                )
                * score_scale
            )
            scores = jnp.where(visible[None, :], scores, -jnp.inf)
            highest = jnp.max(scores, axis=1, keepdims=True)
            weights = jnp.exp(scores - highest)
            running = jnp.sum(weights, axis=1, keepdims=True)
            mixture = jnp.dot(
                weights.astype(jnp.bfloat16),
                key_block[:, head_dim:],
                preferred_element_type=jnp.float32,
            )
            return (mixture / running).astype(jnp.bfloat16)

        return lax.map(one_block, query_all.reshape(-1, query_block_rows, head_dim)).reshape(
            -1, head_dim
        )

    attended = lax.map(attend, jnp.arange(CLIPS, dtype=jnp.int32))
    returned = lax.all_to_all(
        attended.reshape(devices, sub_rows, head_dim),
        "wide",
        split_axis=0,
        concat_axis=0,
        tiled=True,
    )
    attention = (
        returned.reshape(HEADS, groups, sub_rows, head_dim)
        .transpose(1, 2, 0, 3)
        .reshape(local_rows, vit_width)
    )
    projected = jnp.dot(attention, w_out, preferred_element_type=jnp.float32).astype(jnp.bfloat16)
    merged = projected.reshape(local_rows // 4, 4 * vit_width).astype(jnp.float32)
    centre = jnp.mean(merged, axis=1, keepdims=True)
    centered = merged - centre
    spread = jnp.mean(centered * centered, axis=1, keepdims=True)
    normed = (centered * lax.rsqrt(spread + norm_eps) * ln_gain + ln_bias).astype(jnp.bfloat16)
    tok_groups = min(8, devices)
    feat_groups = devices // tok_groups
    merge_rows = w_merge
    for bit_index in range(tok_groups.bit_length() - 1):
        partner = swapped(merge_rows, "wide", bit_index)
        upper_bit = position_self // (1 << bit_index) % 2
        merge_rows = ordered_pair(merge_rows, partner, upper_bit)
    token_count = normed.shape[0]
    part_rows = token_count // tok_groups
    feat_width = normed.shape[1] // feat_groups
    out_width = w_merge.shape[1]
    merge_send = (
        normed.reshape(tok_groups, part_rows, feat_groups, feat_width)
        .transpose(2, 0, 1, 3)
        .reshape(devices, part_rows, feat_width)
    )
    flat_rows = lax.all_to_all(merge_send, "wide", split_axis=0, concat_axis=0, tiled=True).reshape(
        -1, feat_width
    )
    partial_value = jnp.dot(flat_rows, merge_rows, preferred_element_type=jnp.float32).reshape(
        devices, -1, out_width
    )
    summed = lax.all_to_all(partial_value, "wide", split_axis=0, concat_axis=0, tiled=True)
    tokens = (
        jnp.sum(summed.reshape(feat_groups, tok_groups, part_rows, out_width), axis=0)
        .reshape(token_count, out_width)
        .astype(jnp.bfloat16)
    )
    logits = jnp.dot(tokens, w_router, preferred_element_type=jnp.float32)
    experts = w_router.shape[1]
    top_count = expert_ids.shape[1]
    matches = expert_ids[:, :, None] == jnp.arange(experts, dtype=jnp.int32)[None, None, :]
    chosen = jnp.sum(jnp.where(matches, logits[:, None, :], 0.0), axis=2)
    gate_values = jax.nn.sigmoid(chosen)
    route_weight = route_scale * gate_values / jnp.sum(gate_values, axis=1, keepdims=True)
    capacity = min(token_count, 2 * token_count * top_count // experts)
    slot_count = experts * capacity
    target = expert_ids * capacity + slot_pos
    one_hot = jnp.any(
        target[None, :, :] == jnp.arange(slot_count, dtype=jnp.int32)[:, None, None], axis=2
    ).astype(jnp.bfloat16)
    buffer = jnp.dot(one_hot, tokens, preferred_element_type=jnp.float32).astype(jnp.bfloat16)
    gate_half = w_gate[0]
    up_half = w_up[0]
    down_half = w_down[0]
    half_cap = capacity // 2
    dispatch = buffer.reshape(devices, half_cap, out_width)
    portion = lax.all_to_all(dispatch, "wide", split_axis=0, concat_axis=0, tiled=True)
    item_count = portion.shape[1]
    partner_rows = swapped(portion, "wide", 0)
    both_rows = jnp.concatenate([portion, partner_rows], axis=1)
    flat_rows = both_rows.reshape(-1, out_width)
    gate_part = jnp.dot(flat_rows, gate_half, preferred_element_type=jnp.float32)
    up_part = jnp.dot(flat_rows, up_half, preferred_element_type=jnp.float32)
    hidden = (jax.nn.silu(gate_part) * up_part).astype(jnp.bfloat16)
    product = (
        jnp.dot(hidden, down_half, preferred_element_type=jnp.float32)
        .astype(jnp.bfloat16)
        .reshape(devices, 2 * item_count, out_width)
    )
    from_partner = swapped(product[:, item_count:], "wide", 0)
    joined = (
        product[:, :item_count].astype(jnp.float32) + from_partner.astype(jnp.float32)
    ).astype(jnp.bfloat16)
    answers = lax.all_to_all(joined, "wide", split_axis=0, concat_axis=0, tiled=True)
    slot_result = answers.reshape(slot_count, out_width)
    slot_result = lax.optimization_barrier(slot_result)
    picked = jnp.take(slot_result, target.reshape(-1), axis=0).reshape(
        token_count, top_count, out_width
    )
    return jnp.sum(picked.astype(jnp.float32) * route_weight[:, :, None], axis=1).astype(
        jnp.bfloat16
    )


def remote(source, target, send_sem, recv_sem, place):
    return pltpu.make_async_remote_copy(
        src_ref=source,
        dst_ref=target,
        send_sem=send_sem,
        recv_sem=recv_sem,
        device_id={"wide": place},
        device_id_type=pl.DeviceIdType.MESH,
    )


def by_rows(left, right):
    return lax.dot_general(
        left, right, (((1,), (1,)), ((), ())), preferred_element_type=jnp.float32
    )


def greet(places):
    barrier = pltpu.get_barrier_semaphore()
    for place in places:
        pl.semaphore_signal(
            barrier, inc=1, device_id={"wide": place}, device_id_type=pl.DeviceIdType.MESH
        )
    return barrier


def vision_part(
    peers,
    head_dim,
    barrier,
    grid_ref,
    qkv_hbm,
    w_out_hbm,
    gain_ref,
    bias_ref,
    out_ref,
    qkv_ref,
    pair_send,
    pair_recv,
    value_send,
    value_recv,
    queries,
    keys,
    values,
    weights_kept,
    sums_kept,
    mixed_send,
    mixed_recv,
    attention,
    mixed,
    w_out_ref,
    send_sem,
    recv_sem,
    back_send_sem,
    back_recv_sem,
    local_sem,
    start_rest,
    fetches,
):
    place = lax.axis_index("wide")
    base = place // peers * peers
    me = place - base
    rows = qkv_ref.shape[0]
    width = w_out_hbm.shape[0]
    heads = HEADS // peers
    span = heads * head_dim
    devices = lax.axis_size("wide")
    qkv_copy = pltpu.make_async_copy(qkv_hbm, qkv_ref, local_sem.at[3])
    qkv_copy.start()
    weight_copy = pltpu.make_async_copy(w_out_hbm, w_out_ref, local_sem.at[0])
    weight_copy.start()
    for fetch in fetches:
        fetch.start()
    qkv_copy.wait()
    tail = span - 128
    for part, (packed, first, last) in enumerate(
        [
            (pair_send, 0, 2 * rows),
            (pair_send, rows, 2 * rows + tail),
            (value_send, 0, rows),
        ]
    ):
        ends = [part * width + (peer + 1) * span for peer in range(peers)]
        tails = jnp.concatenate([qkv_ref[:, end - tail : end] for end in ends], axis=1)
        turned = tails.astype(jnp.float32).T
        for peer, end in enumerate(ends):
            packed[peer, first : first + rows, :] = qkv_ref[:, end - span : end - tail]
            packed[peer, last : last + tail, :] = turned[
                peer * tail : (peer + 1) * tail
            ].astype(jnp.bfloat16)
    pl.semaphore_wait(barrier, devices - 1)
    own_pair = pltpu.make_async_copy(pair_send.at[me], pair_recv.at[me], local_sem.at[1])
    own_value = pltpu.make_async_copy(value_send.at[me], value_recv.at[me], local_sem.at[4])
    own_pair.start()
    own_value.start()
    for kind, (source, target) in enumerate(
        [(pair_send, pair_recv), (value_send, value_recv)]
    ):
        for step in range(1, peers):
            peer = lax.rem(me + step, peers)
            remote(
                source.at[peer], target.at[me], send_sem.at[kind], recv_sem.at[kind], base + peer
            ).start()
    for fetch in fetches:
        fetch.wait()
    start_rest()

    def whole(block, kind):
        block = block.at[pl.ds(0, peers - 1)]
        return remote(
            block, block, send_sem.at[kind], recv_sem.at[kind], base + lax.rem(me + 1, peers)
        )

    own_pair.wait()
    whole(pair_recv, 0).wait_recv()

    def unpack(packed, first, last, target):
        turned = (
            packed[:, last : last + tail, :].astype(jnp.float32).reshape(peers * tail, rows).T
        )
        for peer in range(peers):
            joined = jnp.concatenate(
                [
                    packed[peer, first : first + rows, :],
                    turned[:, peer * tail : (peer + 1) * tail].astype(jnp.bfloat16),
                ],
                axis=1,
            )
            for head in range(heads):
                target[head, peer * rows : (peer + 1) * rows, :] = joined[
                    :, head * head_dim : (head + 1) * head_dim
                ]

    unpack(pair_recv, 0, 2 * rows, queries)
    unpack(pair_recv, rows, 2 * rows + tail, keys)
    factor = head_dim ** (-0.5) * 1.4426950408889634
    clip = place // peers
    count = grid_ref[clip, 0] * grid_ref[clip, 1]
    visible = lax.broadcasted_iota(jnp.int32, (1, peers * rows), 1) < count
    hide = jnp.where(visible, 0.0, -jnp.inf)
    group = 2 if peers % 2 == 0 else 1
    blocks = peers // group

    def score_block(block, carry):
        lines = pl.ds(pl.multiple_of(block * group * rows, group * rows), group * rows)
        for head in range(heads):
            scores = lax.dot_general(
                queries[head, lines, :], keys[head], (((1,), (1,)), ((), ())), preferred_element_type=jnp.float32
            )
            scores = scores + hide
            highest = jnp.max(scores, axis=1, keepdims=True)
            weights = jnp.exp2((scores - highest) * factor)
            sums_kept[head, lines, :] = jnp.sum(weights, axis=1, keepdims=True)
            weights_kept[head, lines, :] = weights.astype(jnp.bfloat16)
        return carry

    lax.fori_loop(0, blocks, score_block, 0)
    own_value.wait()
    whole(value_recv, 1).wait_recv()
    unpack(value_recv, 0, rows, values)

    def one_block(step, carry):
        block, bit = 0, 1
        while bit < blocks:
            block = block + bit * ((me // group // bit + (blocks - 1 - step) // bit) % 2)
            bit *= 2
        lines = pl.ds(pl.multiple_of(block * group * rows, group * rows), group * rows)
        outcomes = []
        for head in range(heads):
            mixture = jnp.dot(
                weights_kept[head, lines, :], values[head], preferred_element_type=jnp.float32
            )
            outcomes.append((mixture / sums_kept[head, lines, :]).astype(jnp.bfloat16))
        joined = jnp.concatenate([piece.astype(jnp.float32) for piece in outcomes], axis=1)
        for part in range(group):
            peer = block * group + part
            mine = joined[part * rows : (part + 1) * rows]
            mixed_send[peer, :rows, :] = mine[:, :128].astype(jnp.bfloat16)
            tail = jnp.concatenate(
                [mine[:, 128:], jnp.zeros((rows, 256 - span), jnp.float32)], axis=1
            )
            mixed_send[peer, rows:, :] = tail.T[: span - 128].astype(jnp.bfloat16)

            @pl.when(peer != me)
            def _():
                remote(
                    mixed_send.at[peer],
                    mixed_recv.at[me],
                    back_send_sem.at[0],
                    back_recv_sem.at[0],
                    base + peer,
                ).start()

            @pl.when(peer == me)
            def _():
                pltpu.make_async_copy(
                    mixed_send.at[me], mixed_recv.at[me], local_sem.at[2]
                ).start()

        return carry

    lax.fori_loop(0, blocks, one_block, 0)
    pltpu.make_async_copy(mixed_send.at[me], mixed_recv.at[me], local_sem.at[2]).wait()
    returned = mixed_recv.at[pl.ds(0, peers - 1)]
    back = remote(
        returned,
        returned,
        back_send_sem.at[0],
        back_recv_sem.at[0],
        base + lax.rem(me + 1, peers),
    )
    back.wait_recv()
    back.wait_send()
    whole(pair_send, 0).wait_send()
    whole(value_send, 1).wait_send()
    for peer in range(peers):
        start = peer * span
        attention[:, start : start + 128] = mixed_recv[peer, :rows, :]
        tail = mixed_recv[peer, rows:, :].astype(jnp.float32).T
        attention[:, start + 128 : start + span] = tail.astype(jnp.bfloat16)
    weight_copy.wait()
    projected = (
        jnp.dot(attention[...], w_out_ref[...], preferred_element_type=jnp.float32)
        .astype(jnp.bfloat16)
        .astype(jnp.float32)
    )
    tiles = width // 128
    for tile in range(tiles):
        mixed[tile] = projected[:, tile * 128 : (tile + 1) * 128]
    pieces = [
        [mixed[tile, pl.ds(part, rows // 4, stride=4), :] for tile in range(tiles)]
        for part in range(4)
    ]
    total_width = 4 * width
    flat = [piece for row in pieces for piece in row]
    centre = jnp.sum(sum(flat), axis=1, keepdims=True) / total_width
    spread = (
        jnp.sum(sum((piece - centre) * (piece - centre) for piece in flat), axis=1, keepdims=True)
        / total_width
    )
    inverse = lax.rsqrt(spread + norm_eps)
    for index, piece in enumerate(flat):
        out_ref[:, index * 128 : (index + 1) * 128] = (
            (piece - centre) * inverse * gain_ref[index : index + 1, :]
            + bias_ref[index : index + 1, :]
        ).astype(jnp.bfloat16)


def language_part(
    far,
    near,
    run_vision,
    normed_ref,
    ids_ref,
    router_hbm,
    w_merge_hbm,
    w_gate_hbm,
    w_up_hbm,
    w_down_hbm,
    out_ref,
    router_ref,
    merge_rows,
    w_gate,
    w_up,
    w_down,
    norm_send,
    norm_recv,
    part_send,
    y_recv,
    z_send,
    z_recv,
    gathered,
    gate_rows,
    expert_part,
    core_recv,
    core_sum,
    y2_recv,
    z2_send,
    z2_recv,
    local_sem,
    w_send_sem,
    w_recv_sem,
    n_send_sem,
    n_recv_sem,
    y_send_sem,
    y_recv_sem,
    z_send_sem,
    z_recv_sem,
    g_recv_sem,
    gz_send_sem,
    gy_send_sem,
    gc_send_sem,
    c_send_sem,
    c_recv_sem,
    y2_send_sem,
    y2_recv_sem,
    z2_send_sem,
    z2_recv_sem,
):
    place = lax.axis_index("wide")
    chips = far * near
    core = lax.rem(place, 2)
    chip = place // 2
    a = chip // near
    b = lax.rem(chip, near)
    other = place + 1 - 2 * core
    tokens_here = normed_ref.shape[0]
    depth = w_merge_hbm.shape[0]
    out_width = w_merge_hbm.shape[1]
    experts = chips
    f32 = jnp.float32
    half = jnp.bfloat16

    def at(a_index, b_index, c_index):
        return (a_index * near + b_index) * 2 + c_index

    other_chips = [lax.rem(chip + step, chips) for step in range(1, chips)]
    weight_copies = [
        pltpu.make_async_copy(w_gate_hbm.at[0], w_gate, local_sem.at[0]),
        pltpu.make_async_copy(w_up_hbm.at[0], w_up, local_sem.at[1]),
        pltpu.make_async_copy(w_down_hbm.at[0], w_down, local_sem.at[2]),
    ]
    own_rows = merge_rows.at[pl.ds(core * depth, depth)]
    merge_copy = pltpu.make_async_copy(w_merge_hbm, own_rows, local_sem.at[3])
    merge_swap = remote(w_merge_hbm, own_rows, w_send_sem.at[0], w_recv_sem.at[0], other)

    def start_rest():
        merge_swap.start()
        merge_copy.start()
        for copy in weight_copies:
            copy.start()
        named_rows = router_hbm[...].astype(f32)
        router_ref[...] = jnp.concatenate(
            [
                named_rows,
                named_rows,
                jnp.zeros((router_ref.shape[0] - 2 * experts, out_width), f32),
            ],
            axis=0,
        ).astype(half)

    run_vision(start_rest)
    for q in range(chips):
        norm_send[q] = normed_ref[:, 2 * depth * q : 2 * depth * (q + 1)]
    own_norm = pltpu.make_async_copy(norm_send.at[chip], norm_recv.at[chip], local_sem.at[4])
    own_norm.start()
    for q in other_chips:
        remote(
            norm_send.at[q], norm_recv.at[chip], n_send_sem.at[0], n_recv_sem.at[0], q * 2 + core
        ).start()
    merge_copy.wait()
    merge_swap.wait_send()
    remote(
        w_merge_hbm,
        merge_rows.at[pl.ds((1 - core) * depth, depth)],
        w_send_sem.at[0],
        w_recv_sem.at[0],
        other,
    ).wait_recv()
    own_norm.wait()
    arrivals = norm_recv.at[pl.ds(0, chips - 1)]
    normed_copies = remote(arrivals, arrivals, n_send_sem.at[0], n_recv_sem.at[0], other)
    normed_copies.wait_recv()
    normed_copies.wait_send()
    column_block = min(512, out_width)
    flat = norm_recv[...].reshape(chips * tokens_here, 2 * depth)

    def merge_columns(index, carry):
        columns = pl.ds(pl.multiple_of(index * column_block, column_block), column_block)
        part_send[:, :, columns] = (
            jnp.dot(flat, merge_rows[:, columns], preferred_element_type=f32)
            .astype(half)
            .reshape(chips, tokens_here, column_block)
        )
        return carry

    lax.fori_loop(0, out_width // column_block, merge_columns, 0)

    near_steps = range(1, near)
    pieces = out_width // column_block
    parts = column_parts
    part_width = out_width // parts

    def columns_of(piece):
        return pl.ds(piece * column_block, column_block)

    def part_of(part):
        return pl.ds(part * part_width, part_width)

    def paired(step):
        value, bit = 0, 1
        while bit < far:
            mine, theirs = a // bit % 2, step // bit % 2
            value = value + bit * (mine + theirs - 2 * mine * theirs)
            bit *= 2
        return value

    def y_copy(a_index, step, slot, part):
        target = lax.rem(b + step, near)
        columns = part_of(part)
        return remote(
            part_send.at[a_index * near + target, :, columns],
            y_recv.at[slot, a_index, :, columns],
            y_send_sem.at[0],
            y_recv_sem.at[slot, a_index, part],
            at(a, target, core),
        )

    def y_total(a_index, part):
        columns = part_of(part)
        value = part_send[a_index * near + b, :, columns].astype(f32)
        for step in near_steps:
            y_copy(a_index, step, step - 1, part).wait_recv()
            value = value + y_recv[step - 1, a_index, :, columns].astype(f32)
        return value

    def z_copy(a_index, slot, part):
        columns = part_of(part)
        return remote(
            z_send.at[a_index, :, columns],
            z_recv.at[slot, :, columns],
            z_send_sem.at[0],
            z_recv_sem.at[slot, part],
            at(a_index, b, core),
        )

    far_targets = [paired(step) for step in range(far - 1, 0, -1)]
    for part in range(parts):
        for a_index in far_targets + [a]:
            for step in near_steps:
                y_copy(a_index, step, near - step - 1, part).start()

    def merge_far(part):
        for a_index in far_targets:
            z_send[a_index, :, part_of(part)] = y_total(a_index, part).astype(half)
            z_copy(a_index, a, part).start()

    def merge_own(part):
        columns = part_of(part)
        value = y_total(a, part)
        for a_index in far_targets:
            z_copy(a_index, a_index, part).wait_recv()
            value = value + z_recv[a_index, :, columns].astype(f32)
        gathered[place, :, columns] = value.astype(half)

    lane_count = router_ref.shape[0]

    def span_of(part):
        extra = lane_count if part == parts - 1 else 0
        return pl.ds(part * part_width, part_width + extra)

    def share(slot, send_sem, target, part):
        block = gathered.at[slot, :, span_of(part)]
        return remote(block, block, send_sem, g_recv_sem.at[slot, part], target)

    def arrived(slot, part):
        share(slot, gc_send_sem.at[0], other, part).wait_recv()

    def to_far(a_index, part):
        return share(place, gz_send_sem.at[0], at(a_index, b, core), part)

    def to_near(a_index, step, part):
        return share(
            at(a_index, b, core),
            gy_send_sem.at[0],
            at(a, lax.rem(b + step, near), core),
            part,
        )

    def to_core(a_index, b_index, part):
        return share(at(a_index, b_index, core), gc_send_sem.at[0], other, part)

    def pass_on(a_index, part):
        for step in near_steps:
            to_near(a_index, step, part).start()
        to_core(a_index, b, part).start()

    def turn(step):
        value, bit = 0, 1
        while bit < far:
            wide_bit, next_bit = far // (2 * bit), far // bit
            value = value + bit * ((step // wide_bit + step // next_bit) % 2)
            bit *= 2
        return paired(value)

    def share_own(part):
        for step in range(1, far):
            to_far(turn(step), part).start()
        pass_on(a, part)

    def forward_far(a_index, part):
        arrived(at(a_index, b, core), part)
        pass_on(a_index, part)

    def forward_near(a_index, part):
        for step in near_steps:
            b_index = lax.rem(b + step, near)
            arrived(at(a_index, b_index, core), part)
            to_core(a_index, b_index, part).start()

    for part in range(parts):
        merge_far(part)
    for part in range(parts - 1):
        merge_own(part)
        share_own(part)
    merge_own(parts - 1)
    tokens = gathered[place, :, :out_width]

    logits = by_rows(tokens, router_ref[...])
    lane = lax.broadcasted_iota(jnp.int32, (tokens_here, lane_count), 1)
    line = lax.broadcasted_iota(jnp.int32, (lane_count, tokens_here), 0)
    line = jnp.where(line < experts, line, line - experts)
    marks = jnp.zeros((lane_count, tokens_here), f32)
    for k in range(ids_ref.shape[0]):
        marks = jnp.where(line == ids_ref[k : k + 1, :], 1.0, marks)
    same = (
        lax.broadcasted_iota(jnp.int32, (tokens_here, tokens_here), 0)
        == lax.broadcasted_iota(jnp.int32, (tokens_here, tokens_here), 1)
    )
    chosen = by_rows(jnp.where(same, 1.0, 0.0).astype(half), marks.astype(half))
    gates = chosen / (1.0 + jnp.exp(-logits))
    gate_sum = jnp.sum(jnp.where(lane < experts, gates, 0.0), axis=1, keepdims=True)
    route = route_scale * gates / gate_sum
    route_high = route.astype(half)
    route_low = (route - route_high.astype(f32)).astype(half)
    gathered[place, :, out_width:] = jnp.where(lane < experts, route_high.astype(f32), route_low.astype(f32)).astype(half)

    share_own(parts - 1)
    for part in range(parts - 1):
        forward_far(turn(1), part)
        forward_near(a, part)
        for step in range(2, far):
            forward_far(turn(step), part)
    for copy in weight_copies:
        copy.wait()

    def core_copy(a_index, side, piece):
        columns = columns_of(piece)
        return remote(
            expert_part.at[a_index, side, :, :, columns],
            core_recv.at[a_index, :, :, columns],
            c_send_sem.at[0],
            c_recv_sem.at[a_index, piece],
            other,
        )

    def y2_copy(a_index, step, slot, piece):
        target = lax.rem(b + step, near)
        columns = columns_of(piece)
        return remote(
            core_sum.at[a_index, target, :, columns],
            y2_recv.at[slot, a_index, :, columns],
            y2_send_sem.at[0],
            y2_recv_sem.at[slot, a_index, piece],
            at(a, target, core),
        )

    def z2_copy(a_index, slot, piece):
        columns = columns_of(piece)
        return remote(
            z2_send.at[a_index, :, columns],
            z2_recv.at[slot, :, columns],
            z2_send_sem.at[0],
            z2_recv_sem.at[slot, piece],
            at(a_index, b, core),
        )

    chunk = near * 2
    expert = place // 2

    def y2_start(a_index, piece):
        for step in near_steps:
            y2_copy(a_index, step, near - step - 1, piece).start()

    def join_cores(a_index, piece):
        columns = columns_of(piece)
        core_copy(a_index, 1 - core, piece).wait_recv()
        core_sum[a_index, :, :, columns] = (
            expert_part[a_index, core, :, :, columns].astype(f32)
            + core_recv[a_index, :, :, columns].astype(f32)
        ).astype(half)

    def y2_total(a_index, piece):
        columns = columns_of(piece)
        value = core_sum[a_index, b, :, columns].astype(f32)
        for step in near_steps:
            y2_copy(a_index, step, step - 1, piece).wait_recv()
            value = value + y2_recv[step - 1, a_index, :, columns].astype(f32)
        return value

    def join_near(a_index):
        for piece in range(pieces):
            z2_send[a_index, :, columns_of(piece)] = y2_total(a_index, piece).astype(half)
            z2_copy(a_index, a, piece).start()

    def chunks(step, carry):
        a_index = turn(step)

        @pl.when(step < far - 1)
        def _():
            forward_far(turn(step + 1), parts - 1)

        forward_near(a_index, parts - 1)

        @pl.when(step < far - 1)
        def _():
            for part in range(parts - 1):
                forward_near(turn(step + 1), part)

        @pl.when(step == 1)
        def _():
            for piece in range(pieces):
                join_cores(a, piece)

        @pl.when(step > 1)
        def _():
            previous = turn(step - 1)
            for piece in range(pieces):
                join_cores(previous, piece)
                y2_start(previous, piece)

        for part in range(parts):
            for b_index in range(near):
                arrived(at(a_index, b_index, 1 - core), part)
        slots = pl.ds(a_index * chunk, chunk)
        rows = gathered[slots, :, :out_width].reshape(chunk * tokens_here, out_width)
        table = gathered[slots, :, out_width:].reshape(chunk * tokens_here, lane_count).astype(f32)
        table_lane = lax.broadcasted_iota(jnp.int32, table.shape, 1)
        mine = jnp.logical_or(table_lane == expert, table_lane == expert + experts)
        scale = jnp.sum(jnp.where(mine, table, 0.0), axis=1, keepdims=True)
        gate_rows[...] = by_rows(rows, w_gate[...])
        gate_part = gate_rows[...]
        up_part = by_rows(rows, w_up[...])
        hidden = (gate_part / (1.0 + jnp.exp(-gate_part)) * up_part).astype(half)

        for piece in range(pieces):
            columns = columns_of(piece)
            product = jnp.dot(hidden, w_down[:, columns], preferred_element_type=f32).astype(half)
            scaled = (product.astype(f32) * scale).astype(half)
            for b_index in range(near):
                for side in range(2):
                    start = (b_index * 2 + side) * tokens_here
                    expert_part[a_index, side, b_index, :, columns] = scaled[
                        start : start + tokens_here
                    ]
            core_copy(a_index, 1 - core, piece).start()

        @pl.when(step > 2)
        def _():
            join_near(turn(step - 2))

        return carry

    lax.fori_loop(0, far, chunks, 0)
    final = turn(far - 1)
    for piece in range(pieces):
        join_cores(final, piece)
        y2_start(final, piece)
    for piece in range(pieces):
        y2_start(a, piece)
    for step in range(max(1, far - 2), far):
        join_near(turn(step))
    for piece in range(pieces):
        columns = columns_of(piece)
        value = y2_total(a, piece)
        for step in range(1, far):
            z2_copy(turn(step), turn(step), piece).wait_recv()
            value = value + z2_recv[turn(step), :, columns].astype(f32)
        out_ref[:, columns] = value.astype(half)

    def sent(block, sem):
        remote(block, block, sem, w_recv_sem.at[0], other).wait_send()

    sent(part_send.at[pl.ds(0, far * (near - 1))], y_send_sem.at[0])
    sent(z_send.at[pl.ds(0, far - 1)], z_send_sem.at[0])
    sent(gathered.at[pl.ds(0, far - 1)], gz_send_sem.at[0])
    sent(gathered.at[pl.ds(0, far * (near - 1))], gy_send_sem.at[0])
    sent(gathered.at[pl.ds(0, chips)], gc_send_sem.at[0])
    sent(core_sum, c_send_sem.at[0])
    sent(y2_recv, y2_send_sem.at[0])
    sent(z2_send.at[pl.ds(0, far - 1)], z2_send_sem.at[0])


def layer_kernel(far, near, peers, head_dim, *refs):
    operands, out_ref, normed = refs[:11], refs[11], refs[12]
    grid_ref, gain_ref, bias_ref, ids_ref, named_ref, small_sem = refs[13:19]
    grid_hbm, qkv_hbm, w_out_hbm, gain_hbm, bias_hbm, ids_hbm, named_hbm = operands[:7]
    scratch = refs[19:]
    vision_scratch, language_scratch = scratch[:20], scratch[20:]
    place = lax.axis_index("wide")
    devices = lax.axis_size("wide")
    barrier = greet([lax.rem(place + step, devices) for step in range(1, devices)])
    fetches = [
        pltpu.make_async_copy(source, target, small_sem.at[index])
        for index, (source, target) in enumerate(
            [
                (named_hbm, named_ref),
                (grid_hbm, grid_ref),
                (gain_hbm, gain_ref),
                (bias_hbm, bias_ref),
                (ids_hbm, ids_ref),
            ]
        )
    ]

    def run_vision(start_rest):
        vision_part(
            peers,
            head_dim,
            barrier,
            grid_ref,
            qkv_hbm,
            w_out_hbm,
            gain_ref,
            bias_ref,
            normed,
            *vision_scratch,
            start_rest,
            fetches,
        )

    language_part(
        far,
        near,
        run_vision,
        normed,
        ids_ref,
        named_ref,
        *operands[7:],
        out_ref,
        *language_scratch,
    )


def fast_local(
    qkv,
    grid,
    w_out,
    ln_gain,
    ln_bias,
    w_merge,
    w_router,
    expert_ids,
    slot_pos,
    w_gate,
    w_up,
    w_down,
):
    devices = lax.axis_size("wide")
    peers = devices // CLIPS
    patch_rows = qkv.shape[0]
    width = w_out.shape[0]
    head_dim = width // HEADS
    heads = HEADS // peers
    span = heads * head_dim
    chips = devices // 2
    near = 1
    while 4 * near * near <= chips:
        near *= 2
    far = chips // near
    rows = patch_rows // 4
    depth, out_width = w_merge.shape
    experts = w_router.shape[1]
    lanes = -(-2 * experts // 128) * 128
    hidden = w_gate.shape[2]
    whole = pl.BlockSpec(memory_space=pltpu.VMEM)
    away = pl.BlockSpec(memory_space=pltpu.MemorySpace.HBM)
    half = jnp.bfloat16
    block = (rows, out_width)
    dma = pltpu.SemaphoreType.DMA
    pieces = out_width // min(512, out_width)
    return pl.pallas_call(
        functools.partial(layer_kernel, far, near, peers, head_dim),
        out_shape=jax.ShapeDtypeStruct(block, half),
        in_specs=[away] * 11,
        out_specs=whole,
        scratch_shapes=[
            pltpu.VMEM((rows, 4 * width), half),
            pltpu.SMEM(grid.shape, jnp.int32),
            pltpu.VMEM((4 * width // 128, 128), jnp.float32),
            pltpu.VMEM((4 * width // 128, 128), jnp.float32),
            pltpu.VMEM(expert_ids.shape[::-1], jnp.int32),
            pltpu.VMEM((experts, out_width), half),
            dma((5,)),
            pltpu.VMEM((patch_rows, 3 * width), half),
            pltpu.VMEM((peers, 2 * (patch_rows + span - 128), 128), half),
            pltpu.VMEM((peers, 2 * (patch_rows + span - 128), 128), half),
            pltpu.VMEM((peers, patch_rows + span - 128, 128), half),
            pltpu.VMEM((peers, patch_rows + span - 128, 128), half),
            pltpu.VMEM((heads, peers * patch_rows, head_dim), half),
            pltpu.VMEM((heads, peers * patch_rows, head_dim), half),
            pltpu.VMEM((heads, peers * patch_rows, head_dim), half),
            pltpu.VMEM((heads, peers * patch_rows, peers * patch_rows), half),
            pltpu.VMEM((heads, peers * patch_rows, 1), jnp.float32),
            pltpu.VMEM((peers, patch_rows + span - 128, 128), half),
            pltpu.VMEM((peers, patch_rows + span - 128, 128), half),
            pltpu.VMEM((patch_rows, width), half),
            pltpu.VMEM((width // 128, patch_rows, 128), jnp.float32),
            pltpu.VMEM((width, width), half),
            dma((2,)),
            dma((2,)),
            dma((1,)),
            dma((1,)),
            dma((5,)),
            pltpu.VMEM((lanes, out_width), half),
            pltpu.VMEM((2 * depth, out_width), half),
            pltpu.VMEM((hidden, out_width), half),
            pltpu.VMEM((hidden, out_width), half),
            pltpu.VMEM((hidden, out_width), half),
            pltpu.VMEM((chips, rows, 2 * depth), half),
            pltpu.VMEM((chips, rows, 2 * depth), half),
            pltpu.VMEM((chips, *block), half),
            pltpu.VMEM((near - 1, far, *block), half),
            pltpu.VMEM((far, *block), half),
            pltpu.VMEM((far, *block), half),
            pltpu.VMEM((devices, rows, out_width + lanes), half),
            pltpu.VMEM((2 * near * rows, hidden), jnp.float32),
            pltpu.VMEM((far, 2, near, *block), half),
            pltpu.VMEM((far, near, *block), half),
            pltpu.VMEM((far, near, *block), half),
            pltpu.VMEM((near - 1, far, *block), half),
            pltpu.VMEM((far, *block), half),
            pltpu.VMEM((far, *block), half),
            dma((5,)),
            dma((1,)),
            dma((1,)),
            dma((1,)),
            dma((1,)),
            dma((1,)),
            dma((near - 1, far, column_parts)),
            dma((1,)),
            dma((far, column_parts)),
            dma((devices, column_parts)),
            dma((1,)),
            dma((1,)),
            dma((1,)),
            dma((1,)),
            dma((far, pieces)),
            dma((1,)),
            dma((near - 1, far, pieces)),
            dma((1,)),
            dma((far, pieces)),
        ],
        compiler_params=pltpu.CompilerParams(
            collective_id=0, has_side_effects=True, vmem_limit_bytes=50 * 2**20
        ),
        name="layer",
    )(
        *[
            pltpu.with_memory_space_constraint(operand, pltpu.MemorySpace.HBM)
            for operand in (
                grid,
                qkv,
                w_out,
                ln_gain.reshape(-1, 128),
                ln_bias.reshape(-1, 128),
                expert_ids.T,
                w_router.T,
                w_merge,
                w_gate.swapaxes(1, 2),
                w_up.swapaxes(1, 2),
                w_down,
            )
        ]
    )


def either(*operands):
    devices = lax.axis_size("wide")
    qkv, w_router, expert_ids = operands[0], operands[6], operands[7]
    token_count = qkv.shape[0] // 4
    experts = w_router.shape[1]
    dense = 2 * token_count * expert_ids.shape[1] >= experts * token_count
    whole_heads = HEADS % (devices // CLIPS) == 0 and devices == 2 * experts
    if not (dense and whole_heads):
        return local(*operands)
    span = HEADS // (devices // CLIPS) * (operands[2].shape[0] // HEADS)
    packs = qkv.shape[0] == 128 and 128 < span < 256 and span % 16 == 0
    return fast_local(*operands) if packs else local(*operands)


def solution(mesh):
    placed = (
        P(("grp", "wide"), None),
        P("grp", None),
        P(),
        P(),
        P(),
        P("wide", None),
        P(),
        P(("grp", "wide"), None),
        P(("grp", "wide"), None),
        P("wide", None, None),
        P("wide", None, None),
        P("wide", None, None),
    )
    return jax.shard_map(
        either, mesh=mesh, in_specs=placed, out_specs=P(("grp", "wide"), None), check_vma=False
    )
```

```python
import functools

import jax
import jax.numpy as jnp
from jax import lax
from jax.experimental import pallas as pl
from jax.experimental.pallas import tpu as pltpu
from jax.sharding import PartitionSpec as P

HEADS = 16
CLIPS = 2


route_scale = 2.446
norm_eps = 1e-05
column_parts = 2


def swapped(value, axis, stride):
    mask = 2**stride
    pairs = [(source, source ^ mask) for source in range(lax.axis_size(axis))]
    return lax.ppermute(value, axis, pairs)


def ordered_pair(own_part, partner, upper_bit):
    return jnp.where(
        upper_bit == 1,
        jnp.concatenate([partner, own_part], 0),
        jnp.concatenate([own_part, partner], 0),
    )


def local(
    qkv,
    grid,
    w_out,
    ln_gain,
    ln_bias,
    w_merge,
    w_router,
    expert_ids,
    slot_pos,
    w_gate,
    w_up,
    w_down,
):
    devices = lax.axis_size("wide")
    position_self = lax.axis_index("wide")
    vit_width = w_out.shape[0]
    head_dim = vit_width // HEADS
    groups = devices // HEADS
    local_rows = qkv.shape[0]
    sub_rows = local_rows // groups
    per_clip = devices // CLIPS
    query_send = (
        qkv[:, :vit_width]
        .reshape(groups, sub_rows, HEADS, head_dim)
        .transpose(2, 0, 1, 3)
        .reshape(devices, sub_rows, head_dim)
    )
    key_value = jnp.concatenate(
        [
            qkv[:, vit_width : 2 * vit_width].reshape(local_rows, HEADS, head_dim),
            qkv[:, 2 * vit_width :].reshape(local_rows, HEADS, head_dim),
        ],
        axis=2,
    )
    spread_send = jnp.broadcast_to(
        key_value.transpose(1, 0, 2)[:, None], (HEADS, groups, local_rows, 2 * head_dim)
    ).reshape(devices, local_rows, 2 * head_dim)
    queries, key_rows = (
        lax.all_to_all(query_send, "wide", split_axis=0, concat_axis=0, tiled=True),
        lax.all_to_all(spread_send, "wide", split_axis=0, concat_axis=0, tiled=True),
    )
    key_rows = key_rows[None]
    key_groups = key_rows.shape[0]
    key_count = key_rows.shape[2]
    key_place = (
        jnp.arange(per_clip, dtype=jnp.int32)[None, :, None] * local_rows
        + jnp.arange(key_groups, dtype=jnp.int32)[:, None, None] * local_rows
        + jnp.arange(key_count, dtype=jnp.int32)[None, None, :]
    ).reshape(-1)
    patch_counts = grid[:, 0] * grid[:, 1]
    clip_queries = queries.reshape(CLIPS, per_clip * sub_rows, head_dim)
    query_block_rows = min(512, per_clip * sub_rows)
    score_scale = head_dim ** (-0.5)

    def attend(clip_index):
        key_block = lax.dynamic_slice_in_dim(key_rows, clip_index * per_clip, per_clip, 1).reshape(
            -1, 2 * head_dim
        )
        visible = key_place < lax.dynamic_index_in_dim(patch_counts, clip_index, 0, keepdims=False)
        query_all = lax.dynamic_index_in_dim(clip_queries, clip_index, 0, keepdims=False)

        def one_block(query_block):
            scores = (
                lax.dot_general(
                    query_block,
                    key_block[:, :head_dim],
                    (((1,), (1,)), ((), ())),
                    preferred_element_type=jnp.float32,
                )
                * score_scale
            )
            scores = jnp.where(visible[None, :], scores, -jnp.inf)
            highest = jnp.max(scores, axis=1, keepdims=True)
            weights = jnp.exp(scores - highest)
            running = jnp.sum(weights, axis=1, keepdims=True)
            mixture = jnp.dot(
                weights.astype(jnp.bfloat16),
                key_block[:, head_dim:],
                preferred_element_type=jnp.float32,
            )
            return (mixture / running).astype(jnp.bfloat16)

        return lax.map(one_block, query_all.reshape(-1, query_block_rows, head_dim)).reshape(
            -1, head_dim
        )

    attended = lax.map(attend, jnp.arange(CLIPS, dtype=jnp.int32))
    returned = lax.all_to_all(
        attended.reshape(devices, sub_rows, head_dim),
        "wide",
        split_axis=0,
        concat_axis=0,
        tiled=True,
    )
    attention = (
        returned.reshape(HEADS, groups, sub_rows, head_dim)
        .transpose(1, 2, 0, 3)
        .reshape(local_rows, vit_width)
    )
    projected = jnp.dot(attention, w_out, preferred_element_type=jnp.float32).astype(jnp.bfloat16)
    merged = projected.reshape(local_rows // 4, 4 * vit_width).astype(jnp.float32)
    centre = jnp.mean(merged, axis=1, keepdims=True)
    centered = merged - centre
    spread = jnp.mean(centered * centered, axis=1, keepdims=True)
    normed = (centered * lax.rsqrt(spread + norm_eps) * ln_gain + ln_bias).astype(jnp.bfloat16)
    tok_groups = min(8, devices)
    feat_groups = devices // tok_groups
    merge_rows = w_merge
    for bit_index in range(tok_groups.bit_length() - 1):
        partner = swapped(merge_rows, "wide", bit_index)
        upper_bit = position_self // (1 << bit_index) % 2
        merge_rows = ordered_pair(merge_rows, partner, upper_bit)
    token_count = normed.shape[0]
    part_rows = token_count // tok_groups
    feat_width = normed.shape[1] // feat_groups
    out_width = w_merge.shape[1]
    merge_send = (
        normed.reshape(tok_groups, part_rows, feat_groups, feat_width)
        .transpose(2, 0, 1, 3)
        .reshape(devices, part_rows, feat_width)
    )
    flat_rows = lax.all_to_all(merge_send, "wide", split_axis=0, concat_axis=0, tiled=True).reshape(
        -1, feat_width
    )
    partial_value = jnp.dot(flat_rows, merge_rows, preferred_element_type=jnp.float32).reshape(
        devices, -1, out_width
    )
    summed = lax.all_to_all(partial_value, "wide", split_axis=0, concat_axis=0, tiled=True)
    tokens = (
        jnp.sum(summed.reshape(feat_groups, tok_groups, part_rows, out_width), axis=0)
        .reshape(token_count, out_width)
        .astype(jnp.bfloat16)
    )
    logits = jnp.dot(tokens, w_router, preferred_element_type=jnp.float32)
    experts = w_router.shape[1]
    top_count = expert_ids.shape[1]
    matches = expert_ids[:, :, None] == jnp.arange(experts, dtype=jnp.int32)[None, None, :]
    chosen = jnp.sum(jnp.where(matches, logits[:, None, :], 0.0), axis=2)
    gate_values = jax.nn.sigmoid(chosen)
    route_weight = route_scale * gate_values / jnp.sum(gate_values, axis=1, keepdims=True)
    capacity = min(token_count, 2 * token_count * top_count // experts)
    slot_count = experts * capacity
    target = expert_ids * capacity + slot_pos
    one_hot = jnp.any(
        target[None, :, :] == jnp.arange(slot_count, dtype=jnp.int32)[:, None, None], axis=2
    ).astype(jnp.bfloat16)
    buffer = jnp.dot(one_hot, tokens, preferred_element_type=jnp.float32).astype(jnp.bfloat16)
    gate_half = w_gate[0]
    up_half = w_up[0]
    down_half = w_down[0]
    half_cap = capacity // 2
    dispatch = buffer.reshape(devices, half_cap, out_width)
    portion = lax.all_to_all(dispatch, "wide", split_axis=0, concat_axis=0, tiled=True)
    item_count = portion.shape[1]
    partner_rows = swapped(portion, "wide", 0)
    both_rows = jnp.concatenate([portion, partner_rows], axis=1)
    flat_rows = both_rows.reshape(-1, out_width)
    gate_part = jnp.dot(flat_rows, gate_half, preferred_element_type=jnp.float32)
    up_part = jnp.dot(flat_rows, up_half, preferred_element_type=jnp.float32)
    hidden = (jax.nn.silu(gate_part) * up_part).astype(jnp.bfloat16)
    product = (
        jnp.dot(hidden, down_half, preferred_element_type=jnp.float32)
        .astype(jnp.bfloat16)
        .reshape(devices, 2 * item_count, out_width)
    )
    from_partner = swapped(product[:, item_count:], "wide", 0)
    joined = (
        product[:, :item_count].astype(jnp.float32) + from_partner.astype(jnp.float32)
    ).astype(jnp.bfloat16)
    answers = lax.all_to_all(joined, "wide", split_axis=0, concat_axis=0, tiled=True)
    slot_result = answers.reshape(slot_count, out_width)
    slot_result = lax.optimization_barrier(slot_result)
    picked = jnp.take(slot_result, target.reshape(-1), axis=0).reshape(
        token_count, top_count, out_width
    )
    return jnp.sum(picked.astype(jnp.float32) * route_weight[:, :, None], axis=1).astype(
        jnp.bfloat16
    )


def remote(source, target, send_sem, recv_sem, place):
    return pltpu.make_async_remote_copy(
        src_ref=source,
        dst_ref=target,
        send_sem=send_sem,
        recv_sem=recv_sem,
        device_id={"wide": place},
        device_id_type=pl.DeviceIdType.MESH,
    )


def by_rows(left, right):
    return lax.dot_general(
        left, right, (((1,), (1,)), ((), ())), preferred_element_type=jnp.float32
    )


def greet(places):
    barrier = pltpu.get_barrier_semaphore()
    for place in places:
        pl.semaphore_signal(
            barrier, inc=1, device_id={"wide": place}, device_id_type=pl.DeviceIdType.MESH
        )
    return barrier


def vision_part(
    peers,
    head_dim,
    barrier,
    grid_ref,
    qkv_hbm,
    w_out_hbm,
    gain_ref,
    bias_ref,
    out_ref,
    qkv_ref,
    pair_send,
    pair_recv,
    value_send,
    value_recv,
    queries,
    keys,
    values,
    weights_kept,
    sums_kept,
    mixed_send,
    mixed_recv,
    attention,
    mixed,
    w_out_ref,
    send_sem,
    recv_sem,
    back_send_sem,
    back_recv_sem,
    local_sem,
    start_rest,
    fetches,
):
    place = lax.axis_index("wide")
    base = place // peers * peers
    me = place - base
    rows = qkv_ref.shape[0]
    width = w_out_hbm.shape[0]
    heads = HEADS // peers
    span = heads * head_dim
    devices = lax.axis_size("wide")
    qkv_copy = pltpu.make_async_copy(qkv_hbm, qkv_ref, local_sem.at[3])
    qkv_copy.start()
    weight_copy = pltpu.make_async_copy(w_out_hbm, w_out_ref, local_sem.at[0])
    weight_copy.start()
    for fetch in fetches:
        fetch.start()
    qkv_copy.wait()
    tail = span - 128
    for part, (packed, first, last) in enumerate(
        [
            (pair_send, 0, 2 * rows),
            (pair_send, rows, 2 * rows + tail),
            (value_send, 0, rows),
        ]
    ):
        ends = [part * width + (peer + 1) * span for peer in range(peers)]
        tails = jnp.concatenate([qkv_ref[:, end - tail : end] for end in ends], axis=1)
        turned = tails.astype(jnp.float32).T
        for peer, end in enumerate(ends):
            packed[peer, first : first + rows, :] = qkv_ref[:, end - span : end - tail]
            packed[peer, last : last + tail, :] = turned[
                peer * tail : (peer + 1) * tail
            ].astype(jnp.bfloat16)
    pl.semaphore_wait(barrier, devices - 1)
    own_pair = pltpu.make_async_copy(pair_send.at[me], pair_recv.at[me], local_sem.at[1])
    own_value = pltpu.make_async_copy(value_send.at[me], value_recv.at[me], local_sem.at[4])
    own_pair.start()
    own_value.start()
    for kind, (source, target) in enumerate(
        [(pair_send, pair_recv), (value_send, value_recv)]
    ):
        for step in range(1, peers):
            peer = lax.rem(me + step, peers)
            remote(
                source.at[peer], target.at[me], send_sem.at[kind], recv_sem.at[kind], base + peer
            ).start()
    for fetch in fetches:
        fetch.wait()
    start_rest()

    def whole(block, kind):
        block = block.at[pl.ds(0, peers - 1)]
        return remote(
            block, block, send_sem.at[kind], recv_sem.at[kind], base + lax.rem(me + 1, peers)
        )

    own_pair.wait()
    whole(pair_recv, 0).wait_recv()

    def unpack(packed, first, last, target):
        turned = (
            packed[:, last : last + tail, :].astype(jnp.float32).reshape(peers * tail, rows).T
        )
        for peer in range(peers):
            joined = jnp.concatenate(
                [
                    packed[peer, first : first + rows, :],
                    turned[:, peer * tail : (peer + 1) * tail].astype(jnp.bfloat16),
                ],
                axis=1,
            )
            for head in range(heads):
                target[head, peer * rows : (peer + 1) * rows, :] = joined[
                    :, head * head_dim : (head + 1) * head_dim
                ]

    unpack(pair_recv, 0, 2 * rows, queries)
    unpack(pair_recv, rows, 2 * rows + tail, keys)
    factor = head_dim ** (-0.5) * 1.4426950408889634
    clip = place // peers
    count = grid_ref[clip, 0] * grid_ref[clip, 1]
    visible = lax.broadcasted_iota(jnp.int32, (1, peers * rows), 1) < count
    hide = jnp.where(visible, 0.0, -jnp.inf)
    group = 2 if peers % 2 == 0 else 1
    blocks = peers // group

    def score_block(block, carry):
        lines = pl.ds(pl.multiple_of(block * group * rows, group * rows), group * rows)
        for head in range(heads):
            scores = lax.dot_general(
                queries[head, lines, :], keys[head], (((1,), (1,)), ((), ())), preferred_element_type=jnp.float32
            )
            scores = scores + hide
            highest = jnp.max(scores, axis=1, keepdims=True)
            weights = jnp.exp2((scores - highest) * factor)
            sums_kept[head, lines, :] = jnp.sum(weights, axis=1, keepdims=True)
            weights_kept[head, lines, :] = weights.astype(jnp.bfloat16)
        return carry

    lax.fori_loop(0, blocks, score_block, 0)
    own_value.wait()
    whole(value_recv, 1).wait_recv()
    unpack(value_recv, 0, rows, values)

    def one_block(step, carry):
        block, bit = 0, 1
        while bit < blocks:
            block = block + bit * ((me // group // bit + (blocks - 1 - step) // bit) % 2)
            bit *= 2
        lines = pl.ds(pl.multiple_of(block * group * rows, group * rows), group * rows)
        outcomes = []
        for head in range(heads):
            mixture = jnp.dot(
                weights_kept[head, lines, :], values[head], preferred_element_type=jnp.float32
            )
            outcomes.append((mixture / sums_kept[head, lines, :]).astype(jnp.bfloat16))
        joined = jnp.concatenate([piece.astype(jnp.float32) for piece in outcomes], axis=1)
        for part in range(group):
            peer = block * group + part
            mine = joined[part * rows : (part + 1) * rows]
            mixed_send[peer, :rows, :] = mine[:, :128].astype(jnp.bfloat16)
            tail = jnp.concatenate(
                [mine[:, 128:], jnp.zeros((rows, 256 - span), jnp.float32)], axis=1
            )
            mixed_send[peer, rows:, :] = tail.T[: span - 128].astype(jnp.bfloat16)

            @pl.when(peer != me)
            def _():
                remote(
                    mixed_send.at[peer],
                    mixed_recv.at[me],
                    back_send_sem.at[0],
                    back_recv_sem.at[0],
                    base + peer,
                ).start()

            @pl.when(peer == me)
            def _():
                pltpu.make_async_copy(
                    mixed_send.at[me], mixed_recv.at[me], local_sem.at[2]
                ).start()

        return carry

    lax.fori_loop(0, blocks, one_block, 0)
    pltpu.make_async_copy(mixed_send.at[me], mixed_recv.at[me], local_sem.at[2]).wait()
    returned = mixed_recv.at[pl.ds(0, peers - 1)]
    back = remote(
        returned,
        returned,
        back_send_sem.at[0],
        back_recv_sem.at[0],
        base + lax.rem(me + 1, peers),
    )
    back.wait_recv()
    back.wait_send()
    whole(pair_send, 0).wait_send()
    whole(value_send, 1).wait_send()
    for peer in range(peers):
        start = peer * span
        attention[:, start : start + 128] = mixed_recv[peer, :rows, :]
        tail = mixed_recv[peer, rows:, :].astype(jnp.float32).T
        attention[:, start + 128 : start + span] = tail.astype(jnp.bfloat16)
    weight_copy.wait()
    projected = (
        jnp.dot(attention[...], w_out_ref[...], preferred_element_type=jnp.float32)
        .astype(jnp.bfloat16)
        .astype(jnp.float32)
    )
    tiles = width // 128
    for tile in range(tiles):
        mixed[tile] = projected[:, tile * 128 : (tile + 1) * 128]
    pieces = [
        [mixed[tile, pl.ds(part, rows // 4, stride=4), :] for tile in range(tiles)]
        for part in range(4)
    ]
    total_width = 4 * width
    flat = [piece for row in pieces for piece in row]
    centre = jnp.sum(sum(flat), axis=1, keepdims=True) / total_width
    spread = (
        jnp.sum(sum((piece - centre) * (piece - centre) for piece in flat), axis=1, keepdims=True)
        / total_width
    )
    inverse = lax.rsqrt(spread + norm_eps)
    for index, piece in enumerate(flat):
        out_ref[:, index * 128 : (index + 1) * 128] = (
            (piece - centre) * inverse * gain_ref[index : index + 1, :]
            + bias_ref[index : index + 1, :]
        ).astype(jnp.bfloat16)


def language_part(
    far,
    near,
    run_vision,
    normed_ref,
    ids_ref,
    router_hbm,
    w_merge_hbm,
    w_gate_hbm,
    w_up_hbm,
    w_down_hbm,
    out_ref,
    router_ref,
    merge_rows,
    w_gate,
    w_up,
    w_down,
    norm_send,
    norm_recv,
    part_send,
    y_recv,
    z_send,
    z_recv,
    chosen_kept,
    gathered,
    expert_part,
    core_recv,
    core_sum,
    y2_recv,
    z2_send,
    z2_recv,
    local_sem,
    w_send_sem,
    w_recv_sem,
    n_send_sem,
    n_recv_sem,
    y_send_sem,
    y_recv_sem,
    z_send_sem,
    z_recv_sem,
    g_recv_sem,
    gz_send_sem,
    gy_send_sem,
    gc_send_sem,
    c_send_sem,
    c_recv_sem,
    y2_send_sem,
    y2_recv_sem,
    z2_send_sem,
    z2_recv_sem,
):
    place = lax.axis_index("wide")
    chips = far * near
    core = lax.rem(place, 2)
    chip = place // 2
    a = chip // near
    b = lax.rem(chip, near)
    other = place + 1 - 2 * core
    tokens_here = normed_ref.shape[0]
    depth = w_merge_hbm.shape[0]
    out_width = w_merge_hbm.shape[1]
    experts = chips
    f32 = jnp.float32
    half = jnp.bfloat16

    def at(a_index, b_index, c_index):
        return (a_index * near + b_index) * 2 + c_index

    other_chips = [lax.rem(chip + step, chips) for step in range(1, chips)]
    weight_copies = [
        pltpu.make_async_copy(w_gate_hbm.at[0], w_gate, local_sem.at[0]),
        pltpu.make_async_copy(w_up_hbm.at[0], w_up, local_sem.at[1]),
        pltpu.make_async_copy(w_down_hbm.at[0], w_down, local_sem.at[2]),
    ]
    own_rows = merge_rows.at[pl.ds(core * depth, depth)]
    merge_copy = pltpu.make_async_copy(w_merge_hbm, own_rows, local_sem.at[3])
    merge_swap = remote(w_merge_hbm, own_rows, w_send_sem.at[0], w_recv_sem.at[0], other)

    def start_rest():
        merge_swap.start()
        merge_copy.start()
        for copy in weight_copies:
            copy.start()
        named_rows = router_hbm[...].astype(f32)
        router_ref[...] = jnp.concatenate(
            [
                named_rows,
                named_rows,
                jnp.zeros((router_ref.shape[0] - 2 * experts, out_width), f32),
            ],
            axis=0,
        ).astype(half)

    run_vision(start_rest)
    tiles, rest = divmod(2 * depth, 128)
    folds = 128 // rest
    folded = tokens_here // folds
    for q in range(chips):
        low = 2 * depth * q
        for tile in range(tiles):
            norm_send[q, tile * tokens_here : (tile + 1) * tokens_here, :] = normed_ref[
                :, low + tile * 128 : low + (tile + 1) * 128
            ]
        end = normed_ref[:, low + tiles * 128 : low + 2 * depth]
        norm_send[q, tiles * tokens_here :, :] = jnp.concatenate(
            [end[fold * folded : (fold + 1) * folded] for fold in range(folds)], axis=1
        )
    own_norm = pltpu.make_async_copy(norm_send.at[chip], norm_recv.at[chip], local_sem.at[4])
    own_norm.start()
    for q in other_chips:
        remote(
            norm_send.at[q], norm_recv.at[chip], n_send_sem.at[0], n_recv_sem.at[0], q * 2 + core
        ).start()
    merge_copy.wait()
    merge_swap.wait_send()
    remote(
        w_merge_hbm,
        merge_rows.at[pl.ds((1 - core) * depth, depth)],
        w_send_sem.at[0],
        w_recv_sem.at[0],
        other,
    ).wait_recv()
    own_norm.wait()
    arrivals = norm_recv.at[pl.ds(0, chips - 1)]
    normed_copies = remote(arrivals, arrivals, n_send_sem.at[0], n_recv_sem.at[0], other)
    normed_copies.wait_recv()
    normed_copies.wait_send()
    column_block = min(512, out_width)
    end = norm_recv[:, tiles * tokens_here :, :]
    end = jnp.concatenate(
        [end[:, :, fold * rest : (fold + 1) * rest] for fold in range(folds)], axis=1
    )
    flat = jnp.concatenate(
        [
            norm_recv[:, tile * tokens_here : (tile + 1) * tokens_here, :].reshape(
                chips * tokens_here, 128
            )
            for tile in range(tiles)
        ]
        + [end.reshape(chips * tokens_here, rest)],
        axis=1,
    )

    def merge_columns(index, carry):
        columns = pl.ds(pl.multiple_of(index * column_block, column_block), column_block)
        part_send[:, :, columns] = (
            jnp.dot(flat, merge_rows[:, columns], preferred_element_type=f32)
            .astype(half)
            .reshape(chips, tokens_here, column_block)
        )
        return carry

    lax.fori_loop(0, out_width // column_block, merge_columns, 0)

    near_steps = range(1, near)
    pieces = out_width // column_block
    parts = column_parts
    part_width = out_width // parts

    def columns_of(piece):
        return pl.ds(piece * column_block, column_block)

    def part_of(part):
        return pl.ds(part * part_width, part_width)

    def paired(step):
        value, bit = 0, 1
        while bit < far:
            mine, theirs = a // bit % 2, step // bit % 2
            value = value + bit * (mine + theirs - 2 * mine * theirs)
            bit *= 2
        return value

    def y_copy(a_index, step, slot, part):
        target = lax.rem(b + step, near)
        columns = part_of(part)
        return remote(
            part_send.at[a_index * near + target, :, columns],
            y_recv.at[slot, a_index, :, columns],
            y_send_sem.at[0],
            y_recv_sem.at[slot, a_index, part],
            at(a, target, core),
        )

    def y_total(a_index, part):
        columns = part_of(part)
        value = part_send[a_index * near + b, :, columns].astype(f32)
        for step in near_steps:
            y_copy(a_index, step, step - 1, part).wait_recv()
            value = value + y_recv[step - 1, a_index, :, columns].astype(f32)
        return value

    def z_copy(a_index, slot, part):
        columns = part_of(part)
        return remote(
            z_send.at[a_index, :, columns],
            z_recv.at[slot, :, columns],
            z_send_sem.at[0],
            z_recv_sem.at[slot, part],
            at(a_index, b, core),
        )

    far_targets = [paired(step) for step in range(far - 1, 0, -1)]
    for part in range(parts):
        for a_index in far_targets + [a]:
            for step in near_steps:
                y_copy(a_index, step, near - step - 1, part).start()

    def merge_far(part):
        for a_index in far_targets:
            z_send[a_index, :, part_of(part)] = y_total(a_index, part).astype(half)
            z_copy(a_index, a, part).start()

    def merge_own(part):
        columns = part_of(part)
        value = y_total(a, part)
        for a_index in far_targets:
            z_copy(a_index, a_index, part).wait_recv()
            value = value + z_recv[a_index, :, columns].astype(f32)
        gathered[place, :, columns] = value.astype(half)

    lane_count = router_ref.shape[0]

    def span_of(part):
        extra = lane_count if part == parts - 1 else 0
        return pl.ds(part * part_width, part_width + extra)

    def share(slot, send_sem, target, part):
        block = gathered.at[slot, :, span_of(part)]
        return remote(block, block, send_sem, g_recv_sem.at[slot, part], target)

    def arrived(slot, part):
        share(slot, gc_send_sem.at[0], other, part).wait_recv()

    def to_far(a_index, part):
        return share(place, gz_send_sem.at[0], at(a_index, b, core), part)

    def to_near(a_index, step, part):
        return share(
            at(a_index, b, core),
            gy_send_sem.at[0],
            at(a, lax.rem(b + step, near), core),
            part,
        )

    def to_core(a_index, b_index, part):
        return share(at(a_index, b_index, core), gc_send_sem.at[0], other, part)

    def pass_on(a_index, part):
        for step in near_steps:
            to_near(a_index, step, part).start()
        to_core(a_index, b, part).start()

    def turn(step):
        value, bit = 0, 1
        while bit < far:
            wide_bit, next_bit = far // (2 * bit), far // bit
            value = value + bit * ((step // wide_bit + step // next_bit) % 2)
            bit *= 2
        return paired(value)

    def share_own(part):
        for step in range(1, far):
            to_far(turn(step), part).start()
        pass_on(a, part)

    def forward_far(a_index, part):
        arrived(at(a_index, b, core), part)
        pass_on(a_index, part)

    def forward_near(a_index, part):
        for step in near_steps:
            b_index = lax.rem(b + step, near)
            arrived(at(a_index, b_index, core), part)
            to_core(a_index, b_index, part).start()

    lane = lax.broadcasted_iota(jnp.int32, (tokens_here, lane_count), 1)
    line = lax.broadcasted_iota(jnp.int32, (lane_count, tokens_here), 0)
    line = jnp.where(line < experts, line, line - experts)
    marks = jnp.zeros((lane_count, tokens_here), f32)
    for k in range(ids_ref.shape[0]):
        marks = jnp.where(line == ids_ref[k : k + 1, :], 1.0, marks)
    same = (
        lax.broadcasted_iota(jnp.int32, (tokens_here, tokens_here), 0)
        == lax.broadcasted_iota(jnp.int32, (tokens_here, tokens_here), 1)
    )
    chosen = by_rows(jnp.where(same, 1.0, 0.0).astype(half), marks.astype(half))
    chosen_kept[...] = chosen
    for part in range(parts):
        merge_far(part)
    for part in range(parts - 1):
        merge_own(part)
        share_own(part)
    merge_own(parts - 1)
    tokens = gathered[place, :, :out_width]

    logits = by_rows(tokens, router_ref[...])
    gates = chosen_kept[...] / (1.0 + jnp.exp(-logits))
    gate_sum = jnp.sum(jnp.where(lane < experts, gates, 0.0), axis=1, keepdims=True)
    route = route_scale * gates / gate_sum
    route_high = route.astype(half)
    route_low = (route - route_high.astype(f32)).astype(half)
    gathered[place, :, out_width:] = jnp.where(lane < experts, route_high.astype(f32), route_low.astype(f32)).astype(half)

    share_own(parts - 1)
    for part in range(parts - 1):
        forward_far(turn(1), part)
        forward_near(a, part)
        for step in range(2, far):
            forward_far(turn(step), part)
    for copy in weight_copies:
        copy.wait()

    def core_copy(a_index, side, piece):
        columns = columns_of(piece)
        return remote(
            expert_part.at[a_index, side, :, :, columns],
            core_recv.at[a_index, :, :, columns],
            c_send_sem.at[0],
            c_recv_sem.at[a_index, piece],
            other,
        )

    def y2_copy(a_index, step, slot, piece):
        target = lax.rem(b + step, near)
        columns = columns_of(piece)
        return remote(
            core_sum.at[a_index, target, :, columns],
            y2_recv.at[slot, a_index, :, columns],
            y2_send_sem.at[0],
            y2_recv_sem.at[slot, a_index, piece],
            at(a, target, core),
        )

    def z2_copy(a_index, slot, piece):
        columns = columns_of(piece)
        return remote(
            z2_send.at[a_index, :, columns],
            z2_recv.at[slot, :, columns],
            z2_send_sem.at[0],
            z2_recv_sem.at[slot, piece],
            at(a_index, b, core),
        )

    chunk = near * 2
    expert = place // 2

    def y2_start(a_index, piece):
        for step in near_steps:
            y2_copy(a_index, step, near - step - 1, piece).start()

    def join_cores(a_index, piece):
        columns = columns_of(piece)
        core_copy(a_index, 1 - core, piece).wait_recv()
        core_sum[a_index, :, :, columns] = (
            expert_part[a_index, core, :, :, columns].astype(f32)
            + core_recv[a_index, :, :, columns].astype(f32)
        ).astype(half)

    def y2_total(a_index, piece):
        columns = columns_of(piece)
        value = core_sum[a_index, b, :, columns].astype(f32)
        for step in near_steps:
            y2_copy(a_index, step, step - 1, piece).wait_recv()
            value = value + y2_recv[step - 1, a_index, :, columns].astype(f32)
        return value

    def join_near(a_index):
        for piece in range(pieces):
            z2_send[a_index, :, columns_of(piece)] = y2_total(a_index, piece).astype(half)
            z2_copy(a_index, a, piece).start()

    def chunks(step, carry):
        a_index = turn(step)

        @pl.when(step < far - 1)
        def _():
            forward_far(turn(step + 1), parts - 1)

        forward_near(a_index, parts - 1)

        @pl.when(step < far - 1)
        def _():
            for part in range(parts - 1):
                forward_near(turn(step + 1), part)

        @pl.when(step == 1)
        def _():
            for piece in range(pieces):
                join_cores(a, piece)

        @pl.when(step > 1)
        def _():
            previous = turn(step - 1)
            for piece in range(pieces):
                join_cores(previous, piece)
                y2_start(previous, piece)

        for part in range(parts):
            for b_index in range(near):
                arrived(at(a_index, b_index, 1 - core), part)
        slots = pl.ds(a_index * chunk, chunk)
        rows = gathered[slots, :, :out_width].reshape(chunk * tokens_here, out_width)
        table = gathered[slots, :, out_width:].reshape(chunk * tokens_here, lane_count).astype(f32)
        table_lane = lax.broadcasted_iota(jnp.int32, table.shape, 1)
        mine = jnp.logical_or(table_lane == expert, table_lane == expert + experts)
        scale = jnp.sum(jnp.where(mine, table, 0.0), axis=1, keepdims=True)
        gate_part = by_rows(rows, w_gate[...])
        up_part = by_rows(rows, w_up[...])
        hidden = (gate_part / (1.0 + jnp.exp(-gate_part)) * up_part).astype(half)

        for piece in range(pieces):
            columns = columns_of(piece)
            product = jnp.dot(hidden, w_down[:, columns], preferred_element_type=f32).astype(half)
            scaled = (product.astype(f32) * scale).astype(half)
            for b_index in range(near):
                for side in range(2):
                    start = (b_index * 2 + side) * tokens_here
                    expert_part[a_index, side, b_index, :, columns] = scaled[
                        start : start + tokens_here
                    ]
            core_copy(a_index, 1 - core, piece).start()

        @pl.when(step > 2)
        def _():
            join_near(turn(step - 2))

        return carry

    lax.fori_loop(0, far, chunks, 0)
    final = turn(far - 1)
    for piece in range(pieces):
        join_cores(final, piece)
        y2_start(final, piece)
    for piece in range(pieces):
        y2_start(a, piece)
    for step in range(max(1, far - 2), far):
        join_near(turn(step))
    for piece in range(pieces):
        columns = columns_of(piece)
        value = y2_total(a, piece)
        for step in range(1, far):
            z2_copy(turn(step), turn(step), piece).wait_recv()
            value = value + z2_recv[turn(step), :, columns].astype(f32)
        out_ref[:, columns] = value.astype(half)

    def sent(block, sem):
        remote(block, block, sem, w_recv_sem.at[0], other).wait_send()

    sent(part_send.at[pl.ds(0, far * (near - 1))], y_send_sem.at[0])
    sent(z_send.at[pl.ds(0, far - 1)], z_send_sem.at[0])
    sent(gathered.at[pl.ds(0, far - 1)], gz_send_sem.at[0])
    sent(gathered.at[pl.ds(0, far * (near - 1))], gy_send_sem.at[0])
    sent(gathered.at[pl.ds(0, chips)], gc_send_sem.at[0])
    sent(core_sum, c_send_sem.at[0])
    sent(y2_recv, y2_send_sem.at[0])
    sent(z2_send.at[pl.ds(0, far - 1)], z2_send_sem.at[0])


def layer_kernel(far, near, peers, head_dim, *refs):
    operands, out_ref, normed = refs[:11], refs[11], refs[12]
    grid_ref, gain_ref, bias_ref, ids_ref, named_ref, small_sem = refs[13:19]
    grid_hbm, qkv_hbm, w_out_hbm, gain_hbm, bias_hbm, ids_hbm, named_hbm = operands[:7]
    scratch = refs[19:]
    vision_scratch, language_scratch = scratch[:20], scratch[20:]
    place = lax.axis_index("wide")
    devices = lax.axis_size("wide")
    barrier = greet([lax.rem(place + step, devices) for step in range(1, devices)])
    fetches = [
        pltpu.make_async_copy(source, target, small_sem.at[index])
        for index, (source, target) in enumerate(
            [
                (named_hbm, named_ref),
                (grid_hbm, grid_ref),
                (gain_hbm, gain_ref),
                (bias_hbm, bias_ref),
                (ids_hbm, ids_ref),
            ]
        )
    ]

    def run_vision(start_rest):
        vision_part(
            peers,
            head_dim,
            barrier,
            grid_ref,
            qkv_hbm,
            w_out_hbm,
            gain_ref,
            bias_ref,
            normed,
            *vision_scratch,
            start_rest,
            fetches,
        )

    language_part(
        far,
        near,
        run_vision,
        normed,
        ids_ref,
        named_ref,
        *operands[7:],
        out_ref,
        *language_scratch,
    )


def fast_local(
    qkv,
    grid,
    w_out,
    ln_gain,
    ln_bias,
    w_merge,
    w_router,
    expert_ids,
    slot_pos,
    w_gate,
    w_up,
    w_down,
):
    devices = lax.axis_size("wide")
    peers = devices // CLIPS
    patch_rows = qkv.shape[0]
    width = w_out.shape[0]
    head_dim = width // HEADS
    heads = HEADS // peers
    span = heads * head_dim
    chips = devices // 2
    near = 1
    while 4 * near * near <= chips:
        near *= 2
    far = chips // near
    rows = patch_rows // 4
    depth, out_width = w_merge.shape
    experts = w_router.shape[1]
    lanes = -(-2 * experts // 128) * 128
    hidden = w_gate.shape[2]
    whole = pl.BlockSpec(memory_space=pltpu.VMEM)
    away = pl.BlockSpec(memory_space=pltpu.MemorySpace.HBM)
    half = jnp.bfloat16
    block = (rows, out_width)
    dma = pltpu.SemaphoreType.DMA
    pieces = out_width // min(512, out_width)
    return pl.pallas_call(
        functools.partial(layer_kernel, far, near, peers, head_dim),
        out_shape=jax.ShapeDtypeStruct(block, half),
        in_specs=[away] * 11,
        out_specs=whole,
        scratch_shapes=[
            pltpu.VMEM((rows, 4 * width), half),
            pltpu.SMEM(grid.shape, jnp.int32),
            pltpu.VMEM((4 * width // 128, 128), jnp.float32),
            pltpu.VMEM((4 * width // 128, 128), jnp.float32),
            pltpu.VMEM(expert_ids.shape[::-1], jnp.int32),
            pltpu.VMEM((experts, out_width), half),
            dma((5,)),
            pltpu.VMEM((patch_rows, 3 * width), half),
            pltpu.VMEM((peers, 2 * (patch_rows + span - 128), 128), half),
            pltpu.VMEM((peers, 2 * (patch_rows + span - 128), 128), half),
            pltpu.VMEM((peers, patch_rows + span - 128, 128), half),
            pltpu.VMEM((peers, patch_rows + span - 128, 128), half),
            pltpu.VMEM((heads, peers * patch_rows, head_dim), half),
            pltpu.VMEM((heads, peers * patch_rows, head_dim), half),
            pltpu.VMEM((heads, peers * patch_rows, head_dim), half),
            pltpu.VMEM((heads, peers * patch_rows, peers * patch_rows), half),
            pltpu.VMEM((heads, peers * patch_rows, 1), jnp.float32),
            pltpu.VMEM((peers, patch_rows + span - 128, 128), half),
            pltpu.VMEM((peers, patch_rows + span - 128, 128), half),
            pltpu.VMEM((patch_rows, width), half),
            pltpu.VMEM((width // 128, patch_rows, 128), jnp.float32),
            pltpu.VMEM((width, width), half),
            dma((2,)),
            dma((2,)),
            dma((1,)),
            dma((1,)),
            dma((5,)),
            pltpu.VMEM((lanes, out_width), half),
            pltpu.VMEM((2 * depth, out_width), half),
            pltpu.VMEM((hidden, out_width), half),
            pltpu.VMEM((hidden, out_width), half),
            pltpu.VMEM((hidden, out_width), half),
            pltpu.VMEM((chips, rows * 2 * depth // 128, 128), half),
            pltpu.VMEM((chips, rows * 2 * depth // 128, 128), half),
            pltpu.VMEM((chips, *block), half),
            pltpu.VMEM((near - 1, far, *block), half),
            pltpu.VMEM((far, *block), half),
            pltpu.VMEM((far, *block), half),
            pltpu.VMEM((rows, lanes), jnp.float32),
            pltpu.VMEM((devices, rows, out_width + lanes), half),
            pltpu.VMEM((far, 2, near, *block), half),
            pltpu.VMEM((far, near, *block), half),
            pltpu.VMEM((far, near, *block), half),
            pltpu.VMEM((near - 1, far, *block), half),
            pltpu.VMEM((far, *block), half),
            pltpu.VMEM((far, *block), half),
            dma((5,)),
            dma((1,)),
            dma((1,)),
            dma((1,)),
            dma((1,)),
            dma((1,)),
            dma((near - 1, far, column_parts)),
            dma((1,)),
            dma((far, column_parts)),
            dma((devices, column_parts)),
            dma((1,)),
            dma((1,)),
            dma((1,)),
            dma((1,)),
            dma((far, pieces)),
            dma((1,)),
            dma((near - 1, far, pieces)),
            dma((1,)),
            dma((far, pieces)),
        ],
        compiler_params=pltpu.CompilerParams(
            collective_id=0, has_side_effects=True, vmem_limit_bytes=50 * 2**20
        ),
        name="layer",
    )(
        *[
            pltpu.with_memory_space_constraint(operand, pltpu.MemorySpace.HBM)
            for operand in (
                grid,
                qkv,
                w_out,
                ln_gain.reshape(-1, 128),
                ln_bias.reshape(-1, 128),
                expert_ids.T,
                w_router.T,
                w_merge,
                w_gate.swapaxes(1, 2),
                w_up.swapaxes(1, 2),
                w_down,
            )
        ]
    )


def either(*operands):
    devices = lax.axis_size("wide")
    qkv, w_router, expert_ids = operands[0], operands[6], operands[7]
    token_count = qkv.shape[0] // 4
    experts = w_router.shape[1]
    dense = 2 * token_count * expert_ids.shape[1] >= experts * token_count
    whole_heads = HEADS % (devices // CLIPS) == 0 and devices == 2 * experts
    if not (dense and whole_heads):
        return local(*operands)
    span = HEADS // (devices // CLIPS) * (operands[2].shape[0] // HEADS)
    packs = qkv.shape[0] == 128 and 128 < span < 256 and span % 16 == 0
    rest = 2 * operands[5].shape[0] % 128
    packs = packs and rest > 0 and 128 % rest == 0 and token_count * rest % 2048 == 0
    return fast_local(*operands) if packs else local(*operands)


def solution(mesh):
    placed = (
        P(("grp", "wide"), None),
        P("grp", None),
        P(),
        P(),
        P(),
        P("wide", None),
        P(),
        P(("grp", "wide"), None),
        P(("grp", "wide"), None),
        P("wide", None, None),
        P("wide", None, None),
        P("wide", None, None),
    )
    return jax.shard_map(
        either, mesh=mesh, in_specs=placed, out_specs=P(("grp", "wide"), None), check_vma=False
    )
```

```python
import functools

import jax
import jax.numpy as jnp
from jax import lax
from jax.experimental import pallas as pl
from jax.experimental.pallas import tpu as pltpu
from jax.sharding import PartitionSpec as P

HEADS = 16
CLIPS = 2


route_scale = 2.446
norm_eps = 1e-05
column_parts = 2


def swapped(value, axis, stride):
    mask = 2**stride
    pairs = [(source, source ^ mask) for source in range(lax.axis_size(axis))]
    return lax.ppermute(value, axis, pairs)


def ordered_pair(own_part, partner, upper_bit):
    return jnp.where(
        upper_bit == 1,
        jnp.concatenate([partner, own_part], 0),
        jnp.concatenate([own_part, partner], 0),
    )


def local(
    qkv,
    grid,
    w_out,
    ln_gain,
    ln_bias,
    w_merge,
    w_router,
    expert_ids,
    slot_pos,
    w_gate,
    w_up,
    w_down,
):
    devices = lax.axis_size("wide")
    position_self = lax.axis_index("wide")
    vit_width = w_out.shape[0]
    head_dim = vit_width // HEADS
    groups = devices // HEADS
    local_rows = qkv.shape[0]
    sub_rows = local_rows // groups
    per_clip = devices // CLIPS
    query_send = (
        qkv[:, :vit_width]
        .reshape(groups, sub_rows, HEADS, head_dim)
        .transpose(2, 0, 1, 3)
        .reshape(devices, sub_rows, head_dim)
    )
    key_value = jnp.concatenate(
        [
            qkv[:, vit_width : 2 * vit_width].reshape(local_rows, HEADS, head_dim),
            qkv[:, 2 * vit_width :].reshape(local_rows, HEADS, head_dim),
        ],
        axis=2,
    )
    spread_send = jnp.broadcast_to(
        key_value.transpose(1, 0, 2)[:, None], (HEADS, groups, local_rows, 2 * head_dim)
    ).reshape(devices, local_rows, 2 * head_dim)
    queries, key_rows = (
        lax.all_to_all(query_send, "wide", split_axis=0, concat_axis=0, tiled=True),
        lax.all_to_all(spread_send, "wide", split_axis=0, concat_axis=0, tiled=True),
    )
    key_rows = key_rows[None]
    key_groups = key_rows.shape[0]
    key_count = key_rows.shape[2]
    key_place = (
        jnp.arange(per_clip, dtype=jnp.int32)[None, :, None] * local_rows
        + jnp.arange(key_groups, dtype=jnp.int32)[:, None, None] * local_rows
        + jnp.arange(key_count, dtype=jnp.int32)[None, None, :]
    ).reshape(-1)
    patch_counts = grid[:, 0] * grid[:, 1]
    clip_queries = queries.reshape(CLIPS, per_clip * sub_rows, head_dim)
    query_block_rows = min(512, per_clip * sub_rows)
    score_scale = head_dim ** (-0.5)

    def attend(clip_index):
        key_block = lax.dynamic_slice_in_dim(key_rows, clip_index * per_clip, per_clip, 1).reshape(
            -1, 2 * head_dim
        )
        visible = key_place < lax.dynamic_index_in_dim(patch_counts, clip_index, 0, keepdims=False)
        query_all = lax.dynamic_index_in_dim(clip_queries, clip_index, 0, keepdims=False)

        def one_block(query_block):
            scores = (
                lax.dot_general(
                    query_block,
                    key_block[:, :head_dim],
                    (((1,), (1,)), ((), ())),
                    preferred_element_type=jnp.float32,
                )
                * score_scale
            )
            scores = jnp.where(visible[None, :], scores, -jnp.inf)
            highest = jnp.max(scores, axis=1, keepdims=True)
            weights = jnp.exp(scores - highest)
            running = jnp.sum(weights, axis=1, keepdims=True)
            mixture = jnp.dot(
                weights.astype(jnp.bfloat16),
                key_block[:, head_dim:],
                preferred_element_type=jnp.float32,
            )
            return (mixture / running).astype(jnp.bfloat16)

        return lax.map(one_block, query_all.reshape(-1, query_block_rows, head_dim)).reshape(
            -1, head_dim
        )

    attended = lax.map(attend, jnp.arange(CLIPS, dtype=jnp.int32))
    returned = lax.all_to_all(
        attended.reshape(devices, sub_rows, head_dim),
        "wide",
        split_axis=0,
        concat_axis=0,
        tiled=True,
    )
    attention = (
        returned.reshape(HEADS, groups, sub_rows, head_dim)
        .transpose(1, 2, 0, 3)
        .reshape(local_rows, vit_width)
    )
    projected = jnp.dot(attention, w_out, preferred_element_type=jnp.float32).astype(jnp.bfloat16)
    merged = projected.reshape(local_rows // 4, 4 * vit_width).astype(jnp.float32)
    centre = jnp.mean(merged, axis=1, keepdims=True)
    centered = merged - centre
    spread = jnp.mean(centered * centered, axis=1, keepdims=True)
    normed = (centered * lax.rsqrt(spread + norm_eps) * ln_gain + ln_bias).astype(jnp.bfloat16)
    tok_groups = min(8, devices)
    feat_groups = devices // tok_groups
    merge_rows = w_merge
    for bit_index in range(tok_groups.bit_length() - 1):
        partner = swapped(merge_rows, "wide", bit_index)
        upper_bit = position_self // (1 << bit_index) % 2
        merge_rows = ordered_pair(merge_rows, partner, upper_bit)
    token_count = normed.shape[0]
    part_rows = token_count // tok_groups
    feat_width = normed.shape[1] // feat_groups
    out_width = w_merge.shape[1]
    merge_send = (
        normed.reshape(tok_groups, part_rows, feat_groups, feat_width)
        .transpose(2, 0, 1, 3)
        .reshape(devices, part_rows, feat_width)
    )
    flat_rows = lax.all_to_all(merge_send, "wide", split_axis=0, concat_axis=0, tiled=True).reshape(
        -1, feat_width
    )
    partial_value = jnp.dot(flat_rows, merge_rows, preferred_element_type=jnp.float32).reshape(
        devices, -1, out_width
    )
    summed = lax.all_to_all(partial_value, "wide", split_axis=0, concat_axis=0, tiled=True)
    tokens = (
        jnp.sum(summed.reshape(feat_groups, tok_groups, part_rows, out_width), axis=0)
        .reshape(token_count, out_width)
        .astype(jnp.bfloat16)
    )
    logits = jnp.dot(tokens, w_router, preferred_element_type=jnp.float32)
    experts = w_router.shape[1]
    top_count = expert_ids.shape[1]
    matches = expert_ids[:, :, None] == jnp.arange(experts, dtype=jnp.int32)[None, None, :]
    chosen = jnp.sum(jnp.where(matches, logits[:, None, :], 0.0), axis=2)
    gate_values = jax.nn.sigmoid(chosen)
    route_weight = route_scale * gate_values / jnp.sum(gate_values, axis=1, keepdims=True)
    capacity = min(token_count, 2 * token_count * top_count // experts)
    slot_count = experts * capacity
    target = expert_ids * capacity + slot_pos
    one_hot = jnp.any(
        target[None, :, :] == jnp.arange(slot_count, dtype=jnp.int32)[:, None, None], axis=2
    ).astype(jnp.bfloat16)
    buffer = jnp.dot(one_hot, tokens, preferred_element_type=jnp.float32).astype(jnp.bfloat16)
    gate_half = w_gate[0]
    up_half = w_up[0]
    down_half = w_down[0]
    half_cap = capacity // 2
    dispatch = buffer.reshape(devices, half_cap, out_width)
    portion = lax.all_to_all(dispatch, "wide", split_axis=0, concat_axis=0, tiled=True)
    item_count = portion.shape[1]
    partner_rows = swapped(portion, "wide", 0)
    both_rows = jnp.concatenate([portion, partner_rows], axis=1)
    flat_rows = both_rows.reshape(-1, out_width)
    gate_part = jnp.dot(flat_rows, gate_half, preferred_element_type=jnp.float32)
    up_part = jnp.dot(flat_rows, up_half, preferred_element_type=jnp.float32)
    hidden = (jax.nn.silu(gate_part) * up_part).astype(jnp.bfloat16)
    product = (
        jnp.dot(hidden, down_half, preferred_element_type=jnp.float32)
        .astype(jnp.bfloat16)
        .reshape(devices, 2 * item_count, out_width)
    )
    from_partner = swapped(product[:, item_count:], "wide", 0)
    joined = (
        product[:, :item_count].astype(jnp.float32) + from_partner.astype(jnp.float32)
    ).astype(jnp.bfloat16)
    answers = lax.all_to_all(joined, "wide", split_axis=0, concat_axis=0, tiled=True)
    slot_result = answers.reshape(slot_count, out_width)
    slot_result = lax.optimization_barrier(slot_result)
    picked = jnp.take(slot_result, target.reshape(-1), axis=0).reshape(
        token_count, top_count, out_width
    )
    return jnp.sum(picked.astype(jnp.float32) * route_weight[:, :, None], axis=1).astype(
        jnp.bfloat16
    )


def remote(source, target, send_sem, recv_sem, place):
    return pltpu.make_async_remote_copy(
        src_ref=source,
        dst_ref=target,
        send_sem=send_sem,
        recv_sem=recv_sem,
        device_id={"wide": place},
        device_id_type=pl.DeviceIdType.MESH,
    )


def by_rows(left, right):
    return lax.dot_general(
        left, right, (((1,), (1,)), ((), ())), preferred_element_type=jnp.float32
    )


def greet(places):
    barrier = pltpu.get_barrier_semaphore()
    for place in places:
        pl.semaphore_signal(
            barrier, inc=1, device_id={"wide": place}, device_id_type=pl.DeviceIdType.MESH
        )
    return barrier


def vision_part(
    peers,
    head_dim,
    barrier,
    grid_ref,
    qkv_hbm,
    w_out_hbm,
    gain_ref,
    bias_ref,
    out_ref,
    qkv_ref,
    pair_send,
    pair_recv,
    value_send,
    value_recv,
    queries,
    keys,
    values,
    weights_kept,
    sums_kept,
    mixed_send,
    mixed_recv,
    attention,
    mixed,
    w_out_ref,
    send_sem,
    recv_sem,
    back_send_sem,
    back_recv_sem,
    local_sem,
    start_rest,
    fetches,
):
    place = lax.axis_index("wide")
    base = place // peers * peers
    me = place - base
    rows = qkv_ref.shape[0]
    width = w_out_hbm.shape[0]
    heads = HEADS // peers
    span = heads * head_dim
    devices = lax.axis_size("wide")
    qkv_copy = pltpu.make_async_copy(qkv_hbm, qkv_ref, local_sem.at[3])
    qkv_copy.start()
    weight_copy = pltpu.make_async_copy(w_out_hbm, w_out_ref, local_sem.at[0])
    weight_copy.start()
    for fetch in fetches:
        fetch.start()
    qkv_copy.wait()
    tail = span - 128
    for part, (packed, first, last) in enumerate(
        [
            (pair_send, 0, 2 * rows),
            (pair_send, rows, 2 * rows + tail),
            (value_send, 0, rows),
        ]
    ):
        ends = [part * width + (peer + 1) * span for peer in range(peers)]
        tails = jnp.concatenate([qkv_ref[:, end - tail : end] for end in ends], axis=1)
        turned = tails.astype(jnp.float32).T
        for peer, end in enumerate(ends):
            packed[peer, first : first + rows, :] = qkv_ref[:, end - span : end - tail]
            packed[peer, last : last + tail, :] = turned[
                peer * tail : (peer + 1) * tail
            ].astype(jnp.bfloat16)
    pl.semaphore_wait(barrier, devices - 1)
    own_pair = pltpu.make_async_copy(pair_send.at[me], pair_recv.at[me], local_sem.at[1])
    own_value = pltpu.make_async_copy(value_send.at[me], value_recv.at[me], local_sem.at[4])
    own_pair.start()
    own_value.start()
    for kind, (source, target) in enumerate(
        [(pair_send, pair_recv), (value_send, value_recv)]
    ):
        for step in range(1, peers):
            peer = lax.rem(me + step, peers)
            remote(
                source.at[peer], target.at[me], send_sem.at[kind], recv_sem.at[kind], base + peer
            ).start()
    for fetch in fetches:
        fetch.wait()
    start_rest()

    def whole(block, kind):
        block = block.at[pl.ds(0, peers - 1)]
        return remote(
            block, block, send_sem.at[kind], recv_sem.at[kind], base + lax.rem(me + 1, peers)
        )

    own_pair.wait()
    whole(pair_recv, 0).wait_recv()

    def unpack(packed, first, last, target):
        turned = (
            packed[:, last : last + tail, :].astype(jnp.float32).reshape(peers * tail, rows).T
        )
        for peer in range(peers):
            joined = jnp.concatenate(
                [
                    packed[peer, first : first + rows, :],
                    turned[:, peer * tail : (peer + 1) * tail].astype(jnp.bfloat16),
                ],
                axis=1,
            )
            for head in range(heads):
                target[head, peer * rows : (peer + 1) * rows, :] = joined[
                    :, head * head_dim : (head + 1) * head_dim
                ]

    unpack(pair_recv, 0, 2 * rows, queries)
    unpack(pair_recv, rows, 2 * rows + tail, keys)
    factor = head_dim ** (-0.5) * 1.4426950408889634
    clip = place // peers
    count = grid_ref[clip, 0] * grid_ref[clip, 1]
    visible = lax.broadcasted_iota(jnp.int32, (1, peers * rows), 1) < count
    hide = jnp.where(visible, 0.0, -jnp.inf)
    group = 2 if peers % 2 == 0 else 1
    blocks = peers // group

    def score_block(block, carry):
        lines = pl.ds(pl.multiple_of(block * group * rows, group * rows), group * rows)
        for head in range(heads):
            scores = lax.dot_general(
                queries[head, lines, :], keys[head], (((1,), (1,)), ((), ())), preferred_element_type=jnp.float32
            )
            scores = scores + hide
            highest = jnp.max(scores, axis=1, keepdims=True)
            weights = jnp.exp2((scores - highest) * factor)
            sums_kept[head, lines, :] = jnp.sum(weights, axis=1, keepdims=True)
            weights_kept[head, lines, :] = weights.astype(jnp.bfloat16)
        return carry

    lax.fori_loop(0, blocks, score_block, 0)
    own_value.wait()
    whole(value_recv, 1).wait_recv()
    unpack(value_recv, 0, rows, values)

    def one_block(step, carry):
        block, bit = 0, 1
        while bit < blocks:
            block = block + bit * ((me // group // bit + (blocks - 1 - step) // bit) % 2)
            bit *= 2
        lines = pl.ds(pl.multiple_of(block * group * rows, group * rows), group * rows)
        outcomes = []
        for head in range(heads):
            mixture = jnp.dot(
                weights_kept[head, lines, :], values[head], preferred_element_type=jnp.float32
            )
            outcomes.append((mixture / sums_kept[head, lines, :]).astype(jnp.bfloat16))
        joined = jnp.concatenate([piece.astype(jnp.float32) for piece in outcomes], axis=1)
        for part in range(group):
            peer = block * group + part
            mine = joined[part * rows : (part + 1) * rows]
            mixed_send[peer, :rows, :] = mine[:, :128].astype(jnp.bfloat16)
            tail = jnp.concatenate(
                [mine[:, 128:], jnp.zeros((rows, 256 - span), jnp.float32)], axis=1
            )
            mixed_send[peer, rows:, :] = tail.T[: span - 128].astype(jnp.bfloat16)

            @pl.when(peer != me)
            def _():
                remote(
                    mixed_send.at[peer],
                    mixed_recv.at[me],
                    back_send_sem.at[0],
                    back_recv_sem.at[0],
                    base + peer,
                ).start()

            @pl.when(peer == me)
            def _():
                pltpu.make_async_copy(
                    mixed_send.at[me], mixed_recv.at[me], local_sem.at[2]
                ).start()

        return carry

    lax.fori_loop(0, blocks, one_block, 0)
    pltpu.make_async_copy(mixed_send.at[me], mixed_recv.at[me], local_sem.at[2]).wait()
    returned = mixed_recv.at[pl.ds(0, peers - 1)]
    back = remote(
        returned,
        returned,
        back_send_sem.at[0],
        back_recv_sem.at[0],
        base + lax.rem(me + 1, peers),
    )
    back.wait_recv()
    back.wait_send()
    whole(pair_send, 0).wait_send()
    whole(value_send, 1).wait_send()
    for peer in range(peers):
        start = peer * span
        attention[:, start : start + 128] = mixed_recv[peer, :rows, :]
        tail = mixed_recv[peer, rows:, :].astype(jnp.float32).T
        attention[:, start + 128 : start + span] = tail.astype(jnp.bfloat16)
    weight_copy.wait()
    projected = (
        jnp.dot(attention[...], w_out_ref[...], preferred_element_type=jnp.float32)
        .astype(jnp.bfloat16)
        .astype(jnp.float32)
    )
    tiles = width // 128
    for tile in range(tiles):
        mixed[tile] = projected[:, tile * 128 : (tile + 1) * 128]
    pieces = [
        [mixed[tile, pl.ds(part, rows // 4, stride=4), :] for tile in range(tiles)]
        for part in range(4)
    ]
    total_width = 4 * width
    flat = [piece for row in pieces for piece in row]
    centre = jnp.sum(sum(flat), axis=1, keepdims=True) / total_width
    spread = (
        jnp.sum(sum((piece - centre) * (piece - centre) for piece in flat), axis=1, keepdims=True)
        / total_width
    )
    inverse = lax.rsqrt(spread + norm_eps)
    for index, piece in enumerate(flat):
        out_ref[:, index * 128 : (index + 1) * 128] = (
            (piece - centre) * inverse * gain_ref[index : index + 1, :]
            + bias_ref[index : index + 1, :]
        ).astype(jnp.bfloat16)


def language_part(
    far,
    near,
    run_vision,
    normed_ref,
    ids_ref,
    router_hbm,
    w_merge_hbm,
    w_gate_hbm,
    w_up_hbm,
    w_down_hbm,
    out_ref,
    router_ref,
    merge_rows,
    w_gate,
    w_up,
    w_down,
    norm_send,
    norm_recv,
    part_send,
    y_recv,
    z_send,
    z_recv,
    chosen_kept,
    gathered,
    expert_part,
    core_recv,
    core_sum,
    y2_recv,
    z2_send,
    z2_recv,
    local_sem,
    w_send_sem,
    w_recv_sem,
    n_send_sem,
    n_recv_sem,
    y_send_sem,
    y_recv_sem,
    z_send_sem,
    z_recv_sem,
    g_recv_sem,
    gz_send_sem,
    gy_send_sem,
    gc_send_sem,
    c_send_sem,
    c_recv_sem,
    y2_send_sem,
    y2_recv_sem,
    z2_send_sem,
    z2_recv_sem,
):
    place = lax.axis_index("wide")
    chips = far * near
    core = lax.rem(place, 2)
    chip = place // 2
    a = chip // near
    b = lax.rem(chip, near)
    other = place + 1 - 2 * core
    tokens_here = normed_ref.shape[0]
    depth = w_merge_hbm.shape[0]
    out_width = w_merge_hbm.shape[1]
    experts = chips
    f32 = jnp.float32
    half = jnp.bfloat16

    def at(a_index, b_index, c_index):
        return (a_index * near + b_index) * 2 + c_index

    other_chips = [lax.rem(chip + step, chips) for step in range(1, chips)]
    weight_copies = [
        pltpu.make_async_copy(w_gate_hbm.at[0], w_gate, local_sem.at[0]),
        pltpu.make_async_copy(w_up_hbm.at[0], w_up, local_sem.at[1]),
        pltpu.make_async_copy(w_down_hbm.at[0], w_down, local_sem.at[2]),
    ]
    own_rows = merge_rows.at[pl.ds(core * depth, depth)]
    merge_copy = pltpu.make_async_copy(w_merge_hbm, own_rows, local_sem.at[3])
    merge_swap = remote(w_merge_hbm, own_rows, w_send_sem.at[0], w_recv_sem.at[0], other)

    def start_rest():
        merge_swap.start()
        merge_copy.start()
        for copy in weight_copies:
            copy.start()
        named_rows = router_hbm[...].astype(f32)
        router_ref[...] = jnp.concatenate(
            [
                named_rows,
                named_rows,
                jnp.zeros((router_ref.shape[0] - 2 * experts, out_width), f32),
            ],
            axis=0,
        ).astype(half)

    run_vision(start_rest)
    tiles, rest = divmod(2 * depth, 128)
    folds = 128 // rest
    folded = tokens_here // folds
    for q in range(chips):
        low = 2 * depth * q
        for tile in range(tiles):
            norm_send[q, tile * tokens_here : (tile + 1) * tokens_here, :] = normed_ref[
                :, low + tile * 128 : low + (tile + 1) * 128
            ]
        end = normed_ref[:, low + tiles * 128 : low + 2 * depth]
        norm_send[q, tiles * tokens_here :, :] = jnp.concatenate(
            [end[fold * folded : (fold + 1) * folded] for fold in range(folds)], axis=1
        )
    own_norm = pltpu.make_async_copy(norm_send.at[chip], norm_recv.at[chip], local_sem.at[4])
    own_norm.start()
    for q in other_chips:
        remote(
            norm_send.at[q], norm_recv.at[chip], n_send_sem.at[0], n_recv_sem.at[0], q * 2 + core
        ).start()
    merge_copy.wait()
    merge_swap.wait_send()
    remote(
        w_merge_hbm,
        merge_rows.at[pl.ds((1 - core) * depth, depth)],
        w_send_sem.at[0],
        w_recv_sem.at[0],
        other,
    ).wait_recv()
    own_norm.wait()
    arrivals = norm_recv.at[pl.ds(0, chips - 1)]
    normed_copies = remote(arrivals, arrivals, n_send_sem.at[0], n_recv_sem.at[0], other)
    normed_copies.wait_recv()
    normed_copies.wait_send()
    column_block = min(1024, out_width)
    end = norm_recv[:, tiles * tokens_here :, :]
    end = jnp.concatenate(
        [end[:, :, fold * rest : (fold + 1) * rest] for fold in range(folds)], axis=1
    )
    flat = jnp.concatenate(
        [
            norm_recv[:, tile * tokens_here : (tile + 1) * tokens_here, :].reshape(
                chips * tokens_here, 128
            )
            for tile in range(tiles)
        ]
        + [end.reshape(chips * tokens_here, rest)],
        axis=1,
    )

    def merge_columns(index, carry):
        columns = pl.ds(pl.multiple_of(index * column_block, column_block), column_block)
        part_send[:, :, columns] = (
            jnp.dot(flat, merge_rows[:, columns], preferred_element_type=f32)
            .astype(half)
            .reshape(chips, tokens_here, column_block)
        )
        return carry

    lax.fori_loop(0, out_width // column_block, merge_columns, 0)

    near_steps = range(1, near)
    pieces = out_width // column_block
    parts = column_parts
    part_width = out_width // parts

    def columns_of(piece):
        return pl.ds(piece * column_block, column_block)

    def part_of(part):
        return pl.ds(part * part_width, part_width)

    def paired(step):
        value, bit = 0, 1
        while bit < far:
            mine, theirs = a // bit % 2, step // bit % 2
            value = value + bit * (mine + theirs - 2 * mine * theirs)
            bit *= 2
        return value

    def y_copy(a_index, step, slot, part):
        target = lax.rem(b + step, near)
        columns = part_of(part)
        return remote(
            part_send.at[a_index * near + target, :, columns],
            y_recv.at[slot, a_index, :, columns],
            y_send_sem.at[0],
            y_recv_sem.at[slot, a_index, part],
            at(a, target, core),
        )

    def y_total(a_index, part):
        columns = part_of(part)
        value = part_send[a_index * near + b, :, columns].astype(f32)
        for step in near_steps:
            y_copy(a_index, step, step - 1, part).wait_recv()
            value = value + y_recv[step - 1, a_index, :, columns].astype(f32)
        return value

    def z_copy(a_index, slot, part):
        columns = part_of(part)
        return remote(
            z_send.at[a_index, :, columns],
            z_recv.at[slot, :, columns],
            z_send_sem.at[0],
            z_recv_sem.at[slot, part],
            at(a_index, b, core),
        )

    far_targets = [paired(step) for step in range(far - 1, 0, -1)]
    for part in range(parts):
        for a_index in far_targets + [a]:
            for step in near_steps:
                y_copy(a_index, step, near - step - 1, part).start()

    def merge_far(part):
        for a_index in far_targets:
            z_send[a_index, :, part_of(part)] = y_total(a_index, part).astype(half)
            z_copy(a_index, a, part).start()

    def merge_own(part):
        columns = part_of(part)
        value = y_total(a, part)
        for a_index in far_targets:
            z_copy(a_index, a_index, part).wait_recv()
            value = value + z_recv[a_index, :, columns].astype(f32)
        gathered[place, :, columns] = value.astype(half)

    lane_count = router_ref.shape[0]

    def span_of(part):
        extra = lane_count if part == parts - 1 else 0
        return pl.ds(part * part_width, part_width + extra)

    def share(slot, send_sem, target, part):
        block = gathered.at[slot, :, span_of(part)]
        return remote(block, block, send_sem, g_recv_sem.at[slot, part], target)

    def arrived(slot, part):
        share(slot, gc_send_sem.at[0], other, part).wait_recv()

    def to_far(a_index, part):
        return share(place, gz_send_sem.at[0], at(a_index, b, core), part)

    def to_near(a_index, step, part):
        return share(
            at(a_index, b, core),
            gy_send_sem.at[0],
            at(a, lax.rem(b + step, near), core),
            part,
        )

    def to_core(a_index, b_index, part):
        return share(at(a_index, b_index, core), gc_send_sem.at[0], other, part)

    def pass_on(a_index, part):
        for step in near_steps:
            to_near(a_index, step, part).start()
        to_core(a_index, b, part).start()

    def turn(step):
        value, bit = 0, 1
        while bit < far:
            wide_bit, next_bit = far // (2 * bit), far // bit
            value = value + bit * ((step // wide_bit + step // next_bit) % 2)
            bit *= 2
        return paired(value)

    def share_own(part):
        for step in range(1, far):
            to_far(turn(step), part).start()
        pass_on(a, part)

    def forward_far(a_index, part):
        arrived(at(a_index, b, core), part)
        pass_on(a_index, part)

    def forward_near(a_index, part):
        for step in near_steps:
            b_index = lax.rem(b + step, near)
            arrived(at(a_index, b_index, core), part)
            to_core(a_index, b_index, part).start()

    lane = lax.broadcasted_iota(jnp.int32, (tokens_here, lane_count), 1)
    line = lax.broadcasted_iota(jnp.int32, (lane_count, tokens_here), 0)
    line = jnp.where(line < experts, line, line - experts)
    marks = jnp.zeros((lane_count, tokens_here), f32)
    for k in range(ids_ref.shape[0]):
        marks = jnp.where(line == ids_ref[k : k + 1, :], 1.0, marks)
    same = (
        lax.broadcasted_iota(jnp.int32, (tokens_here, tokens_here), 0)
        == lax.broadcasted_iota(jnp.int32, (tokens_here, tokens_here), 1)
    )
    chosen = by_rows(jnp.where(same, 1.0, 0.0).astype(half), marks.astype(half))
    chosen_kept[...] = chosen
    for part in range(parts):
        merge_far(part)
    for part in range(parts - 1):
        merge_own(part)
        share_own(part)
    merge_own(parts - 1)
    tokens = gathered[place, :, :out_width]

    logits = by_rows(tokens, router_ref[...])
    gates = chosen_kept[...] / (1.0 + jnp.exp(-logits))
    gate_sum = jnp.sum(jnp.where(lane < experts, gates, 0.0), axis=1, keepdims=True)
    route = route_scale * gates / gate_sum
    route_high = route.astype(half)
    route_low = (route - route_high.astype(f32)).astype(half)
    gathered[place, :, out_width:] = jnp.where(lane < experts, route_high.astype(f32), route_low.astype(f32)).astype(half)

    share_own(parts - 1)
    for part in range(parts - 1):
        forward_far(turn(1), part)
        forward_near(a, part)
        for step in range(2, far):
            forward_far(turn(step), part)
    for copy in weight_copies:
        copy.wait()

    def core_copy(a_index, side, piece):
        columns = columns_of(piece)
        return remote(
            expert_part.at[a_index, side, :, :, columns],
            core_recv.at[a_index, :, :, columns],
            c_send_sem.at[0],
            c_recv_sem.at[a_index, piece],
            other,
        )

    def y2_copy(a_index, step, slot, piece):
        target = lax.rem(b + step, near)
        columns = columns_of(piece)
        return remote(
            core_sum.at[a_index, target, :, columns],
            y2_recv.at[slot, a_index, :, columns],
            y2_send_sem.at[0],
            y2_recv_sem.at[slot, a_index, piece],
            at(a, target, core),
        )

    def z2_copy(a_index, slot, piece):
        columns = columns_of(piece)
        return remote(
            z2_send.at[a_index, :, columns],
            z2_recv.at[slot, :, columns],
            z2_send_sem.at[0],
            z2_recv_sem.at[slot, piece],
            at(a_index, b, core),
        )

    chunk = near * 2
    expert = place // 2

    def y2_start(a_index, piece):
        for step in near_steps:
            y2_copy(a_index, step, near - step - 1, piece).start()

    def join_cores(a_index, piece):
        columns = columns_of(piece)
        core_copy(a_index, 1 - core, piece).wait_recv()
        core_sum[a_index, :, :, columns] = (
            expert_part[a_index, core, :, :, columns].astype(f32)
            + core_recv[a_index, :, :, columns].astype(f32)
        ).astype(half)

    def y2_total(a_index, piece):
        columns = columns_of(piece)
        value = core_sum[a_index, b, :, columns].astype(f32)
        for step in near_steps:
            y2_copy(a_index, step, step - 1, piece).wait_recv()
            value = value + y2_recv[step - 1, a_index, :, columns].astype(f32)
        return value

    def join_near(a_index):
        for piece in range(pieces):
            z2_send[a_index, :, columns_of(piece)] = y2_total(a_index, piece).astype(half)
            z2_copy(a_index, a, piece).start()

    def chunks(step, carry):
        a_index = turn(step)

        @pl.when(step < far - 1)
        def _():
            forward_far(turn(step + 1), parts - 1)

        forward_near(a_index, parts - 1)

        @pl.when(step < far - 1)
        def _():
            for part in range(parts - 1):
                forward_near(turn(step + 1), part)

        @pl.when(step == 1)
        def _():
            for piece in range(pieces):
                join_cores(a, piece)

        @pl.when(step > 1)
        def _():
            previous = turn(step - 1)
            for piece in range(pieces):
                join_cores(previous, piece)
                y2_start(previous, piece)

        for part in range(parts):
            for b_index in range(near):
                arrived(at(a_index, b_index, 1 - core), part)
        slots = pl.ds(a_index * chunk, chunk)
        rows = gathered[slots, :, :out_width].reshape(chunk * tokens_here, out_width)
        table = gathered[slots, :, out_width:].reshape(chunk * tokens_here, lane_count).astype(f32)
        table_lane = lax.broadcasted_iota(jnp.int32, table.shape, 1)
        mine = jnp.logical_or(table_lane == expert, table_lane == expert + experts)
        scale = jnp.sum(jnp.where(mine, table, 0.0), axis=1, keepdims=True)
        gate_part = by_rows(rows, w_gate[...])
        up_part = by_rows(rows, w_up[...])
        hidden = (gate_part / (1.0 + jnp.exp(-gate_part)) * up_part).astype(half)

        for piece in range(pieces):
            columns = columns_of(piece)
            product = jnp.dot(hidden, w_down[:, columns], preferred_element_type=f32).astype(half)
            scaled = (product.astype(f32) * scale).astype(half)
            for b_index in range(near):
                for side in range(2):
                    start = (b_index * 2 + side) * tokens_here
                    expert_part[a_index, side, b_index, :, columns] = scaled[
                        start : start + tokens_here
                    ]
            core_copy(a_index, 1 - core, piece).start()

        @pl.when(step > 2)
        def _():
            join_near(turn(step - 2))

        return carry

    lax.fori_loop(0, far, chunks, 0)
    final = turn(far - 1)
    for piece in range(pieces):
        join_cores(final, piece)
        y2_start(final, piece)
    for piece in range(pieces):
        y2_start(a, piece)
    for step in range(max(1, far - 2), far):
        join_near(turn(step))
    for piece in range(pieces):
        columns = columns_of(piece)
        value = y2_total(a, piece)
        for step in range(1, far):
            z2_copy(turn(step), turn(step), piece).wait_recv()
            value = value + z2_recv[turn(step), :, columns].astype(f32)
        out_ref[:, columns] = value.astype(half)

    def sent(block, sem):
        remote(block, block, sem, w_recv_sem.at[0], other).wait_send()

    sent(part_send.at[pl.ds(0, far * (near - 1))], y_send_sem.at[0])
    sent(z_send.at[pl.ds(0, far - 1)], z_send_sem.at[0])
    sent(gathered.at[pl.ds(0, far - 1)], gz_send_sem.at[0])
    sent(gathered.at[pl.ds(0, far * (near - 1))], gy_send_sem.at[0])
    sent(gathered.at[pl.ds(0, chips)], gc_send_sem.at[0])
    sent(core_sum, c_send_sem.at[0])
    sent(y2_recv, y2_send_sem.at[0])
    sent(z2_send.at[pl.ds(0, far - 1)], z2_send_sem.at[0])


def layer_kernel(far, near, peers, head_dim, *refs):
    operands, out_ref, normed = refs[:11], refs[11], refs[12]
    grid_ref, gain_ref, bias_ref, ids_ref, named_ref, small_sem = refs[13:19]
    grid_hbm, qkv_hbm, w_out_hbm, gain_hbm, bias_hbm, ids_hbm, named_hbm = operands[:7]
    scratch = refs[19:]
    vision_scratch, language_scratch = scratch[:20], scratch[20:]
    place = lax.axis_index("wide")
    devices = lax.axis_size("wide")
    barrier = greet([lax.rem(place + step, devices) for step in range(1, devices)])
    fetches = [
        pltpu.make_async_copy(source, target, small_sem.at[index])
        for index, (source, target) in enumerate(
            [
                (named_hbm, named_ref),
                (grid_hbm, grid_ref),
                (gain_hbm, gain_ref),
                (bias_hbm, bias_ref),
                (ids_hbm, ids_ref),
            ]
        )
    ]

    def run_vision(start_rest):
        vision_part(
            peers,
            head_dim,
            barrier,
            grid_ref,
            qkv_hbm,
            w_out_hbm,
            gain_ref,
            bias_ref,
            normed,
            *vision_scratch,
            start_rest,
            fetches,
        )

    language_part(
        far,
        near,
        run_vision,
        normed,
        ids_ref,
        named_ref,
        *operands[7:],
        out_ref,
        *language_scratch,
    )


def fast_local(
    qkv,
    grid,
    w_out,
    ln_gain,
    ln_bias,
    w_merge,
    w_router,
    expert_ids,
    slot_pos,
    w_gate,
    w_up,
    w_down,
):
    devices = lax.axis_size("wide")
    peers = devices // CLIPS
    patch_rows = qkv.shape[0]
    width = w_out.shape[0]
    head_dim = width // HEADS
    heads = HEADS // peers
    span = heads * head_dim
    chips = devices // 2
    near = 1
    while 4 * near * near <= chips:
        near *= 2
    far = chips // near
    rows = patch_rows // 4
    depth, out_width = w_merge.shape
    experts = w_router.shape[1]
    lanes = -(-2 * experts // 128) * 128
    hidden = w_gate.shape[2]
    whole = pl.BlockSpec(memory_space=pltpu.VMEM)
    away = pl.BlockSpec(memory_space=pltpu.MemorySpace.HBM)
    half = jnp.bfloat16
    block = (rows, out_width)
    dma = pltpu.SemaphoreType.DMA
    pieces = out_width // min(1024, out_width)
    return pl.pallas_call(
        functools.partial(layer_kernel, far, near, peers, head_dim),
        out_shape=jax.ShapeDtypeStruct(block, half),
        in_specs=[away] * 11,
        out_specs=whole,
        scratch_shapes=[
            pltpu.VMEM((rows, 4 * width), half),
            pltpu.SMEM(grid.shape, jnp.int32),
            pltpu.VMEM((4 * width // 128, 128), jnp.float32),
            pltpu.VMEM((4 * width // 128, 128), jnp.float32),
            pltpu.VMEM(expert_ids.shape[::-1], jnp.int32),
            pltpu.VMEM((experts, out_width), half),
            dma((5,)),
            pltpu.VMEM((patch_rows, 3 * width), half),
            pltpu.VMEM((peers, 2 * (patch_rows + span - 128), 128), half),
            pltpu.VMEM((peers, 2 * (patch_rows + span - 128), 128), half),
            pltpu.VMEM((peers, patch_rows + span - 128, 128), half),
            pltpu.VMEM((peers, patch_rows + span - 128, 128), half),
            pltpu.VMEM((heads, peers * patch_rows, head_dim), half),
            pltpu.VMEM((heads, peers * patch_rows, head_dim), half),
            pltpu.VMEM((heads, peers * patch_rows, head_dim), half),
            pltpu.VMEM((heads, peers * patch_rows, peers * patch_rows), half),
            pltpu.VMEM((heads, peers * patch_rows, 1), jnp.float32),
            pltpu.VMEM((peers, patch_rows + span - 128, 128), half),
            pltpu.VMEM((peers, patch_rows + span - 128, 128), half),
            pltpu.VMEM((patch_rows, width), half),
            pltpu.VMEM((width // 128, patch_rows, 128), jnp.float32),
            pltpu.VMEM((width, width), half),
            dma((2,)),
            dma((2,)),
            dma((1,)),
            dma((1,)),
            dma((5,)),
            pltpu.VMEM((lanes, out_width), half),
            pltpu.VMEM((2 * depth, out_width), half),
            pltpu.VMEM((hidden, out_width), half),
            pltpu.VMEM((hidden, out_width), half),
            pltpu.VMEM((hidden, out_width), half),
            pltpu.VMEM((chips, rows * 2 * depth // 128, 128), half),
            pltpu.VMEM((chips, rows * 2 * depth // 128, 128), half),
            pltpu.VMEM((chips, *block), half),
            pltpu.VMEM((near - 1, far, *block), half),
            pltpu.VMEM((far, *block), half),
            pltpu.VMEM((far, *block), half),
            pltpu.VMEM((rows, lanes), jnp.float32),
            pltpu.VMEM((devices, rows, out_width + lanes), half),
            pltpu.VMEM((far, 2, near, *block), half),
            pltpu.VMEM((far, near, *block), half),
            pltpu.VMEM((far, near, *block), half),
            pltpu.VMEM((near - 1, far, *block), half),
            pltpu.VMEM((far, *block), half),
            pltpu.VMEM((far, *block), half),
            dma((5,)),
            dma((1,)),
            dma((1,)),
            dma((1,)),
            dma((1,)),
            dma((1,)),
            dma((near - 1, far, column_parts)),
            dma((1,)),
            dma((far, column_parts)),
            dma((devices, column_parts)),
            dma((1,)),
            dma((1,)),
            dma((1,)),
            dma((1,)),
            dma((far, pieces)),
            dma((1,)),
            dma((near - 1, far, pieces)),
            dma((1,)),
            dma((far, pieces)),
        ],
        compiler_params=pltpu.CompilerParams(
            collective_id=0, has_side_effects=True, vmem_limit_bytes=50 * 2**20
        ),
        name="layer",
    )(
        *[
            pltpu.with_memory_space_constraint(operand, pltpu.MemorySpace.HBM)
            for operand in (
                grid,
                qkv,
                w_out,
                ln_gain.reshape(-1, 128),
                ln_bias.reshape(-1, 128),
                expert_ids.T,
                w_router.T,
                w_merge,
                w_gate.swapaxes(1, 2),
                w_up.swapaxes(1, 2),
                w_down,
            )
        ]
    )


def either(*operands):
    devices = lax.axis_size("wide")
    qkv, w_router, expert_ids = operands[0], operands[6], operands[7]
    token_count = qkv.shape[0] // 4
    experts = w_router.shape[1]
    dense = 2 * token_count * expert_ids.shape[1] >= experts * token_count
    whole_heads = HEADS % (devices // CLIPS) == 0 and devices == 2 * experts
    if not (dense and whole_heads):
        return local(*operands)
    span = HEADS // (devices // CLIPS) * (operands[2].shape[0] // HEADS)
    packs = qkv.shape[0] == 128 and 128 < span < 256 and span % 16 == 0
    rest = 2 * operands[5].shape[0] % 128
    packs = packs and rest > 0 and 128 % rest == 0 and token_count * rest % 2048 == 0
    return fast_local(*operands) if packs else local(*operands)


def solution(mesh):
    placed = (
        P(("grp", "wide"), None),
        P("grp", None),
        P(),
        P(),
        P(),
        P("wide", None),
        P(),
        P(("grp", "wide"), None),
        P(("grp", "wide"), None),
        P("wide", None, None),
        P("wide", None, None),
        P("wide", None, None),
    )
    return jax.shard_map(
        either, mesh=mesh, in_specs=placed, out_specs=P(("grp", "wide"), None), check_vma=False
    )
```

```python
import functools

import jax
import jax.numpy as jnp
from jax import lax
from jax.experimental import pallas as pl
from jax.experimental.pallas import tpu as pltpu
from jax.sharding import PartitionSpec as P

HEADS = 16
CLIPS = 2


route_scale = 2.446
norm_eps = 1e-05
column_parts = 2


def swapped(value, axis, stride):
    mask = 2**stride
    pairs = [(source, source ^ mask) for source in range(lax.axis_size(axis))]
    return lax.ppermute(value, axis, pairs)


def ordered_pair(own_part, partner, upper_bit):
    return jnp.where(
        upper_bit == 1,
        jnp.concatenate([partner, own_part], 0),
        jnp.concatenate([own_part, partner], 0),
    )


def local(
    qkv,
    grid,
    w_out,
    ln_gain,
    ln_bias,
    w_merge,
    w_router,
    expert_ids,
    slot_pos,
    w_gate,
    w_up,
    w_down,
):
    devices = lax.axis_size("wide")
    position_self = lax.axis_index("wide")
    vit_width = w_out.shape[0]
    head_dim = vit_width // HEADS
    groups = devices // HEADS
    local_rows = qkv.shape[0]
    sub_rows = local_rows // groups
    per_clip = devices // CLIPS
    query_send = (
        qkv[:, :vit_width]
        .reshape(groups, sub_rows, HEADS, head_dim)
        .transpose(2, 0, 1, 3)
        .reshape(devices, sub_rows, head_dim)
    )
    key_value = jnp.concatenate(
        [
            qkv[:, vit_width : 2 * vit_width].reshape(local_rows, HEADS, head_dim),
            qkv[:, 2 * vit_width :].reshape(local_rows, HEADS, head_dim),
        ],
        axis=2,
    )
    spread_send = jnp.broadcast_to(
        key_value.transpose(1, 0, 2)[:, None], (HEADS, groups, local_rows, 2 * head_dim)
    ).reshape(devices, local_rows, 2 * head_dim)
    queries, key_rows = (
        lax.all_to_all(query_send, "wide", split_axis=0, concat_axis=0, tiled=True),
        lax.all_to_all(spread_send, "wide", split_axis=0, concat_axis=0, tiled=True),
    )
    key_rows = key_rows[None]
    key_groups = key_rows.shape[0]
    key_count = key_rows.shape[2]
    key_place = (
        jnp.arange(per_clip, dtype=jnp.int32)[None, :, None] * local_rows
        + jnp.arange(key_groups, dtype=jnp.int32)[:, None, None] * local_rows
        + jnp.arange(key_count, dtype=jnp.int32)[None, None, :]
    ).reshape(-1)
    patch_counts = grid[:, 0] * grid[:, 1]
    clip_queries = queries.reshape(CLIPS, per_clip * sub_rows, head_dim)
    query_block_rows = min(512, per_clip * sub_rows)
    score_scale = head_dim ** (-0.5)

    def attend(clip_index):
        key_block = lax.dynamic_slice_in_dim(key_rows, clip_index * per_clip, per_clip, 1).reshape(
            -1, 2 * head_dim
        )
        visible = key_place < lax.dynamic_index_in_dim(patch_counts, clip_index, 0, keepdims=False)
        query_all = lax.dynamic_index_in_dim(clip_queries, clip_index, 0, keepdims=False)

        def one_block(query_block):
            scores = (
                lax.dot_general(
                    query_block,
                    key_block[:, :head_dim],
                    (((1,), (1,)), ((), ())),
                    preferred_element_type=jnp.float32,
                )
                * score_scale
            )
            scores = jnp.where(visible[None, :], scores, -jnp.inf)
            highest = jnp.max(scores, axis=1, keepdims=True)
            weights = jnp.exp(scores - highest)
            running = jnp.sum(weights, axis=1, keepdims=True)
            mixture = jnp.dot(
                weights.astype(jnp.bfloat16),
                key_block[:, head_dim:],
                preferred_element_type=jnp.float32,
            )
            return (mixture / running).astype(jnp.bfloat16)

        return lax.map(one_block, query_all.reshape(-1, query_block_rows, head_dim)).reshape(
            -1, head_dim
        )

    attended = lax.map(attend, jnp.arange(CLIPS, dtype=jnp.int32))
    returned = lax.all_to_all(
        attended.reshape(devices, sub_rows, head_dim),
        "wide",
        split_axis=0,
        concat_axis=0,
        tiled=True,
    )
    attention = (
        returned.reshape(HEADS, groups, sub_rows, head_dim)
        .transpose(1, 2, 0, 3)
        .reshape(local_rows, vit_width)
    )
    projected = jnp.dot(attention, w_out, preferred_element_type=jnp.float32).astype(jnp.bfloat16)
    merged = projected.reshape(local_rows // 4, 4 * vit_width).astype(jnp.float32)
    centre = jnp.mean(merged, axis=1, keepdims=True)
    centered = merged - centre
    spread = jnp.mean(centered * centered, axis=1, keepdims=True)
    normed = (centered * lax.rsqrt(spread + norm_eps) * ln_gain + ln_bias).astype(jnp.bfloat16)
    tok_groups = min(8, devices)
    feat_groups = devices // tok_groups
    merge_rows = w_merge
    for bit_index in range(tok_groups.bit_length() - 1):
        partner = swapped(merge_rows, "wide", bit_index)
        upper_bit = position_self // (1 << bit_index) % 2
        merge_rows = ordered_pair(merge_rows, partner, upper_bit)
    token_count = normed.shape[0]
    part_rows = token_count // tok_groups
    feat_width = normed.shape[1] // feat_groups
    out_width = w_merge.shape[1]
    merge_send = (
        normed.reshape(tok_groups, part_rows, feat_groups, feat_width)
        .transpose(2, 0, 1, 3)
        .reshape(devices, part_rows, feat_width)
    )
    flat_rows = lax.all_to_all(merge_send, "wide", split_axis=0, concat_axis=0, tiled=True).reshape(
        -1, feat_width
    )
    partial_value = jnp.dot(flat_rows, merge_rows, preferred_element_type=jnp.float32).reshape(
        devices, -1, out_width
    )
    summed = lax.all_to_all(partial_value, "wide", split_axis=0, concat_axis=0, tiled=True)
    tokens = (
        jnp.sum(summed.reshape(feat_groups, tok_groups, part_rows, out_width), axis=0)
        .reshape(token_count, out_width)
        .astype(jnp.bfloat16)
    )
    logits = jnp.dot(tokens, w_router, preferred_element_type=jnp.float32)
    experts = w_router.shape[1]
    top_count = expert_ids.shape[1]
    matches = expert_ids[:, :, None] == jnp.arange(experts, dtype=jnp.int32)[None, None, :]
    chosen = jnp.sum(jnp.where(matches, logits[:, None, :], 0.0), axis=2)
    gate_values = jax.nn.sigmoid(chosen)
    route_weight = route_scale * gate_values / jnp.sum(gate_values, axis=1, keepdims=True)
    capacity = min(token_count, 2 * token_count * top_count // experts)
    slot_count = experts * capacity
    target = expert_ids * capacity + slot_pos
    one_hot = jnp.any(
        target[None, :, :] == jnp.arange(slot_count, dtype=jnp.int32)[:, None, None], axis=2
    ).astype(jnp.bfloat16)
    buffer = jnp.dot(one_hot, tokens, preferred_element_type=jnp.float32).astype(jnp.bfloat16)
    gate_half = w_gate[0]
    up_half = w_up[0]
    down_half = w_down[0]
    half_cap = capacity // 2
    dispatch = buffer.reshape(devices, half_cap, out_width)
    portion = lax.all_to_all(dispatch, "wide", split_axis=0, concat_axis=0, tiled=True)
    item_count = portion.shape[1]
    partner_rows = swapped(portion, "wide", 0)
    both_rows = jnp.concatenate([portion, partner_rows], axis=1)
    flat_rows = both_rows.reshape(-1, out_width)
    gate_part = jnp.dot(flat_rows, gate_half, preferred_element_type=jnp.float32)
    up_part = jnp.dot(flat_rows, up_half, preferred_element_type=jnp.float32)
    hidden = (jax.nn.silu(gate_part) * up_part).astype(jnp.bfloat16)
    product = (
        jnp.dot(hidden, down_half, preferred_element_type=jnp.float32)
        .astype(jnp.bfloat16)
        .reshape(devices, 2 * item_count, out_width)
    )
    from_partner = swapped(product[:, item_count:], "wide", 0)
    joined = (
        product[:, :item_count].astype(jnp.float32) + from_partner.astype(jnp.float32)
    ).astype(jnp.bfloat16)
    answers = lax.all_to_all(joined, "wide", split_axis=0, concat_axis=0, tiled=True)
    slot_result = answers.reshape(slot_count, out_width)
    slot_result = lax.optimization_barrier(slot_result)
    picked = jnp.take(slot_result, target.reshape(-1), axis=0).reshape(
        token_count, top_count, out_width
    )
    return jnp.sum(picked.astype(jnp.float32) * route_weight[:, :, None], axis=1).astype(
        jnp.bfloat16
    )


def remote(source, target, send_sem, recv_sem, place):
    return pltpu.make_async_remote_copy(
        src_ref=source,
        dst_ref=target,
        send_sem=send_sem,
        recv_sem=recv_sem,
        device_id={"wide": place},
        device_id_type=pl.DeviceIdType.MESH,
    )


def by_rows(left, right):
    return lax.dot_general(
        left, right, (((1,), (1,)), ((), ())), preferred_element_type=jnp.float32
    )


def greet(places):
    barrier = pltpu.get_barrier_semaphore()
    for place in places:
        pl.semaphore_signal(
            barrier, inc=1, device_id={"wide": place}, device_id_type=pl.DeviceIdType.MESH
        )
    return barrier


def vision_part(
    peers,
    head_dim,
    barrier,
    grid_ref,
    qkv_hbm,
    w_out_hbm,
    gain_ref,
    bias_ref,
    out_ref,
    qkv_ref,
    pair_send,
    pair_recv,
    value_send,
    value_recv,
    queries,
    keys,
    values,
    weights_kept,
    sums_kept,
    mixed_send,
    mixed_recv,
    attention,
    mixed,
    w_out_ref,
    send_sem,
    recv_sem,
    back_send_sem,
    back_recv_sem,
    local_sem,
    start_rest,
    fetches,
):
    place = lax.axis_index("wide")
    base = place // peers * peers
    me = place - base
    rows = qkv_ref.shape[0]
    width = w_out_hbm.shape[0]
    heads = HEADS // peers
    span = heads * head_dim
    devices = lax.axis_size("wide")
    qkv_copy = pltpu.make_async_copy(qkv_hbm, qkv_ref, local_sem.at[3])
    qkv_copy.start()
    weight_copy = pltpu.make_async_copy(w_out_hbm, w_out_ref, local_sem.at[0])
    weight_copy.start()
    for fetch in fetches:
        fetch.start()
    qkv_copy.wait()
    tail = span - 128
    for part, (packed, first, last) in enumerate(
        [
            (pair_send, 0, 2 * rows),
            (pair_send, rows, 2 * rows + tail),
            (value_send, 0, rows),
        ]
    ):
        ends = [part * width + (peer + 1) * span for peer in range(peers)]
        tails = jnp.concatenate([qkv_ref[:, end - tail : end] for end in ends], axis=1)
        turned = tails.astype(jnp.float32).T
        for peer, end in enumerate(ends):
            packed[peer, first : first + rows, :] = qkv_ref[:, end - span : end - tail]
            packed[peer, last : last + tail, :] = turned[
                peer * tail : (peer + 1) * tail
            ].astype(jnp.bfloat16)
    pl.semaphore_wait(barrier, peers)
    own_pair = pltpu.make_async_copy(pair_send.at[me], pair_recv.at[me], local_sem.at[1])
    own_value = pltpu.make_async_copy(value_send.at[me], value_recv.at[me], local_sem.at[4])
    own_pair.start()
    own_value.start()
    for kind, (source, target) in enumerate(
        [(pair_send, pair_recv), (value_send, value_recv)]
    ):
        for step in range(1, peers):
            peer = lax.rem(me + step, peers)
            remote(
                source.at[peer], target.at[me], send_sem.at[kind], recv_sem.at[kind], base + peer
            ).start()
    for fetch in fetches:
        fetch.wait()
    start_rest()

    def whole(block, kind):
        block = block.at[pl.ds(0, peers - 1)]
        return remote(
            block, block, send_sem.at[kind], recv_sem.at[kind], base + lax.rem(me + 1, peers)
        )

    own_pair.wait()
    whole(pair_recv, 0).wait_recv()

    def unpack(packed, first, last, target):
        turned = (
            packed[:, last : last + tail, :].astype(jnp.float32).reshape(peers * tail, rows).T
        )
        for peer in range(peers):
            joined = jnp.concatenate(
                [
                    packed[peer, first : first + rows, :],
                    turned[:, peer * tail : (peer + 1) * tail].astype(jnp.bfloat16),
                ],
                axis=1,
            )
            for head in range(heads):
                target[head, peer * rows : (peer + 1) * rows, :] = joined[
                    :, head * head_dim : (head + 1) * head_dim
                ]

    unpack(pair_recv, 0, 2 * rows, queries)
    unpack(pair_recv, rows, 2 * rows + tail, keys)
    factor = head_dim ** (-0.5) * 1.4426950408889634
    clip = place // peers
    count = grid_ref[clip, 0] * grid_ref[clip, 1]
    visible = lax.broadcasted_iota(jnp.int32, (1, peers * rows), 1) < count
    hide = jnp.where(visible, 0.0, -jnp.inf)
    group = 2 if peers % 2 == 0 else 1
    blocks = peers // group

    def score_block(block, carry):
        lines = pl.ds(pl.multiple_of(block * group * rows, group * rows), group * rows)
        for head in range(heads):
            scores = lax.dot_general(
                queries[head, lines, :], keys[head], (((1,), (1,)), ((), ())), preferred_element_type=jnp.float32
            )
            scores = scores + hide
            highest = jnp.max(scores, axis=1, keepdims=True)
            weights = jnp.exp2((scores - highest) * factor)
            sums_kept[head, lines, :] = jnp.sum(weights, axis=1, keepdims=True)
            weights_kept[head, lines, :] = weights.astype(jnp.bfloat16)
        return carry

    lax.fori_loop(0, blocks, score_block, 0)
    own_value.wait()
    whole(value_recv, 1).wait_recv()
    unpack(value_recv, 0, rows, values)

    def one_block(step, carry):
        block, bit = 0, 1
        while bit < blocks:
            block = block + bit * ((me // group // bit + (blocks - 1 - step) // bit) % 2)
            bit *= 2
        lines = pl.ds(pl.multiple_of(block * group * rows, group * rows), group * rows)
        outcomes = []
        for head in range(heads):
            mixture = jnp.dot(
                weights_kept[head, lines, :], values[head], preferred_element_type=jnp.float32
            )
            outcomes.append((mixture / sums_kept[head, lines, :]).astype(jnp.bfloat16))
        joined = jnp.concatenate([piece.astype(jnp.float32) for piece in outcomes], axis=1)
        for part in range(group):
            peer = block * group + part
            mine = joined[part * rows : (part + 1) * rows]
            mixed_send[peer, :rows, :] = mine[:, :128].astype(jnp.bfloat16)
            tail = jnp.concatenate(
                [mine[:, 128:], jnp.zeros((rows, 256 - span), jnp.float32)], axis=1
            )
            mixed_send[peer, rows:, :] = tail.T[: span - 128].astype(jnp.bfloat16)

            @pl.when(peer != me)
            def _():
                remote(
                    mixed_send.at[peer],
                    mixed_recv.at[me],
                    back_send_sem.at[0],
                    back_recv_sem.at[0],
                    base + peer,
                ).start()

            @pl.when(peer == me)
            def _():
                pltpu.make_async_copy(
                    mixed_send.at[me], mixed_recv.at[me], local_sem.at[2]
                ).start()

        return carry

    lax.fori_loop(0, blocks, one_block, 0)
    pltpu.make_async_copy(mixed_send.at[me], mixed_recv.at[me], local_sem.at[2]).wait()
    returned = mixed_recv.at[pl.ds(0, peers - 1)]
    back = remote(
        returned,
        returned,
        back_send_sem.at[0],
        back_recv_sem.at[0],
        base + lax.rem(me + 1, peers),
    )
    back.wait_recv()
    back.wait_send()
    whole(pair_send, 0).wait_send()
    whole(value_send, 1).wait_send()
    for peer in range(peers):
        start = peer * span
        attention[:, start : start + 128] = mixed_recv[peer, :rows, :]
        tail = mixed_recv[peer, rows:, :].astype(jnp.float32).T
        attention[:, start + 128 : start + span] = tail.astype(jnp.bfloat16)
    weight_copy.wait()
    projected = (
        jnp.dot(attention[...], w_out_ref[...], preferred_element_type=jnp.float32)
        .astype(jnp.bfloat16)
        .astype(jnp.float32)
    )
    tiles = width // 128
    for tile in range(tiles):
        mixed[tile] = projected[:, tile * 128 : (tile + 1) * 128]
    pieces = [
        [mixed[tile, pl.ds(part, rows // 4, stride=4), :] for tile in range(tiles)]
        for part in range(4)
    ]
    total_width = 4 * width
    flat = [piece for row in pieces for piece in row]
    centre = jnp.sum(sum(flat), axis=1, keepdims=True) / total_width
    spread = (
        jnp.sum(sum((piece - centre) * (piece - centre) for piece in flat), axis=1, keepdims=True)
        / total_width
    )
    inverse = lax.rsqrt(spread + norm_eps)
    for index, piece in enumerate(flat):
        out_ref[:, index * 128 : (index + 1) * 128] = (
            (piece - centre) * inverse * gain_ref[index : index + 1, :]
            + bias_ref[index : index + 1, :]
        ).astype(jnp.bfloat16)


def language_part(
    far,
    near,
    run_vision,
    normed_ref,
    ids_ref,
    router_hbm,
    w_merge_hbm,
    w_gate_hbm,
    w_up_hbm,
    w_down_hbm,
    out_ref,
    router_ref,
    merge_rows,
    w_gate,
    w_up,
    w_down,
    norm_send,
    norm_recv,
    part_send,
    y_recv,
    z_send,
    z_recv,
    chosen_kept,
    gathered,
    expert_part,
    core_recv,
    core_sum,
    y2_recv,
    z2_send,
    z2_recv,
    local_sem,
    w_send_sem,
    w_recv_sem,
    n_send_sem,
    n_recv_sem,
    y_send_sem,
    y_recv_sem,
    z_send_sem,
    z_recv_sem,
    g_recv_sem,
    gz_send_sem,
    gy_send_sem,
    gc_send_sem,
    c_send_sem,
    c_recv_sem,
    y2_send_sem,
    y2_recv_sem,
    z2_send_sem,
    z2_recv_sem,
):
    place = lax.axis_index("wide")
    chips = far * near
    core = lax.rem(place, 2)
    chip = place // 2
    a = chip // near
    b = lax.rem(chip, near)
    other = place + 1 - 2 * core
    tokens_here = normed_ref.shape[0]
    depth = w_merge_hbm.shape[0]
    out_width = w_merge_hbm.shape[1]
    experts = chips
    f32 = jnp.float32
    half = jnp.bfloat16

    def at(a_index, b_index, c_index):
        return (a_index * near + b_index) * 2 + c_index

    other_chips = [lax.rem(chip + step, chips) for step in range(1, chips)]
    weight_copies = [
        pltpu.make_async_copy(w_gate_hbm.at[0], w_gate, local_sem.at[0]),
        pltpu.make_async_copy(w_up_hbm.at[0], w_up, local_sem.at[1]),
        pltpu.make_async_copy(w_down_hbm.at[0], w_down, local_sem.at[2]),
    ]
    own_rows = merge_rows.at[pl.ds(core * depth, depth)]
    merge_copy = pltpu.make_async_copy(w_merge_hbm, own_rows, local_sem.at[3])
    merge_swap = remote(w_merge_hbm, own_rows, w_send_sem.at[0], w_recv_sem.at[0], other)

    def start_rest():
        merge_swap.start()
        merge_copy.start()
        for copy in weight_copies:
            copy.start()
        named_rows = router_hbm[...].astype(f32)
        router_ref[...] = jnp.concatenate(
            [
                named_rows,
                named_rows,
                jnp.zeros((router_ref.shape[0] - 2 * experts, out_width), f32),
            ],
            axis=0,
        ).astype(half)

    run_vision(start_rest)
    tiles, rest = divmod(2 * depth, 128)
    folds = 128 // rest
    folded = tokens_here // folds
    for q in range(chips):
        low = 2 * depth * q
        for tile in range(tiles):
            norm_send[q, tile * tokens_here : (tile + 1) * tokens_here, :] = normed_ref[
                :, low + tile * 128 : low + (tile + 1) * 128
            ]
        end = normed_ref[:, low + tiles * 128 : low + 2 * depth]
        norm_send[q, tiles * tokens_here :, :] = jnp.concatenate(
            [end[fold * folded : (fold + 1) * folded] for fold in range(folds)], axis=1
        )
    own_norm = pltpu.make_async_copy(norm_send.at[chip], norm_recv.at[chip], local_sem.at[4])
    own_norm.start()
    for q in other_chips:
        remote(
            norm_send.at[q], norm_recv.at[chip], n_send_sem.at[0], n_recv_sem.at[0], q * 2 + core
        ).start()
    merge_copy.wait()
    merge_swap.wait_send()
    remote(
        w_merge_hbm,
        merge_rows.at[pl.ds((1 - core) * depth, depth)],
        w_send_sem.at[0],
        w_recv_sem.at[0],
        other,
    ).wait_recv()
    own_norm.wait()
    arrivals = norm_recv.at[pl.ds(0, chips - 1)]
    normed_copies = remote(arrivals, arrivals, n_send_sem.at[0], n_recv_sem.at[0], other)
    normed_copies.wait_recv()
    normed_copies.wait_send()
    column_block = min(1024, out_width)
    end = norm_recv[:, tiles * tokens_here :, :]
    end = jnp.concatenate(
        [end[:, :, fold * rest : (fold + 1) * rest] for fold in range(folds)], axis=1
    )
    flat = jnp.concatenate(
        [
            norm_recv[:, tile * tokens_here : (tile + 1) * tokens_here, :].reshape(
                chips * tokens_here, 128
            )
            for tile in range(tiles)
        ]
        + [end.reshape(chips * tokens_here, rest)],
        axis=1,
    )

    def merge_columns(index, carry):
        columns = pl.ds(pl.multiple_of(index * column_block, column_block), column_block)
        part_send[:, :, columns] = (
            jnp.dot(flat, merge_rows[:, columns], preferred_element_type=f32)
            .astype(half)
            .reshape(chips, tokens_here, column_block)
        )
        return carry

    lax.fori_loop(0, out_width // column_block, merge_columns, 0)

    near_steps = range(1, near)
    pieces = out_width // column_block
    parts = column_parts
    part_width = out_width // parts

    def columns_of(piece):
        return pl.ds(piece * column_block, column_block)

    def part_of(part):
        return pl.ds(part * part_width, part_width)

    def paired(step):
        value, bit = 0, 1
        while bit < far:
            mine, theirs = a // bit % 2, step // bit % 2
            value = value + bit * (mine + theirs - 2 * mine * theirs)
            bit *= 2
        return value

    def y_copy(a_index, step, slot, part):
        target = lax.rem(b + step, near)
        columns = part_of(part)
        return remote(
            part_send.at[a_index * near + target, :, columns],
            y_recv.at[slot, a_index, :, columns],
            y_send_sem.at[0],
            y_recv_sem.at[slot, a_index, part],
            at(a, target, core),
        )

    def y_total(a_index, part):
        columns = part_of(part)
        value = part_send[a_index * near + b, :, columns].astype(f32)
        for step in near_steps:
            y_copy(a_index, step, step - 1, part).wait_recv()
            value = value + y_recv[step - 1, a_index, :, columns].astype(f32)
        return value

    def z_copy(a_index, slot, part):
        columns = part_of(part)
        return remote(
            z_send.at[a_index, :, columns],
            z_recv.at[slot, :, columns],
            z_send_sem.at[0],
            z_recv_sem.at[slot, part],
            at(a_index, b, core),
        )

    far_targets = [paired(step) for step in range(far - 1, 0, -1)]
    for part in range(parts):
        for a_index in far_targets + [a]:
            for step in near_steps:
                y_copy(a_index, step, near - step - 1, part).start()

    def merge_far(part):
        for a_index in far_targets:
            z_send[a_index, :, part_of(part)] = y_total(a_index, part).astype(half)
            z_copy(a_index, a, part).start()

    def merge_own(part):
        columns = part_of(part)
        value = y_total(a, part)
        for a_index in far_targets:
            z_copy(a_index, a_index, part).wait_recv()
            value = value + z_recv[a_index, :, columns].astype(f32)
        gathered[place, :, columns] = value.astype(half)

    lane_count = router_ref.shape[0]

    def span_of(part):
        extra = lane_count if part == parts - 1 else 0
        return pl.ds(part * part_width, part_width + extra)

    def share(slot, send_sem, target, part):
        block = gathered.at[slot, :, span_of(part)]
        return remote(block, block, send_sem, g_recv_sem.at[slot, part], target)

    def arrived(slot, part):
        share(slot, gc_send_sem.at[0], other, part).wait_recv()

    def to_far(a_index, part):
        return share(place, gz_send_sem.at[0], at(a_index, b, core), part)

    def to_near(a_index, step, part):
        return share(
            at(a_index, b, core),
            gy_send_sem.at[0],
            at(a, lax.rem(b + step, near), core),
            part,
        )

    def to_core(a_index, b_index, part):
        return share(at(a_index, b_index, core), gc_send_sem.at[0], other, part)

    def pass_on(a_index, part):
        for step in near_steps:
            to_near(a_index, step, part).start()
        to_core(a_index, b, part).start()

    def turn(step):
        value, bit = 0, 1
        while bit < far:
            wide_bit, next_bit = far // (2 * bit), far // bit
            value = value + bit * ((step // wide_bit + step // next_bit) % 2)
            bit *= 2
        return paired(value)

    def share_own(part):
        for step in range(1, far):
            to_far(turn(step), part).start()
        pass_on(a, part)

    def forward_far(a_index, part):
        arrived(at(a_index, b, core), part)
        pass_on(a_index, part)

    def forward_near(a_index, part):
        for step in near_steps:
            b_index = lax.rem(b + step, near)
            arrived(at(a_index, b_index, core), part)
            to_core(a_index, b_index, part).start()

    lane = lax.broadcasted_iota(jnp.int32, (tokens_here, lane_count), 1)
    line = lax.broadcasted_iota(jnp.int32, (lane_count, tokens_here), 0)
    line = jnp.where(line < experts, line, line - experts)
    marks = jnp.zeros((lane_count, tokens_here), f32)
    for k in range(ids_ref.shape[0]):
        marks = jnp.where(line == ids_ref[k : k + 1, :], 1.0, marks)
    same = (
        lax.broadcasted_iota(jnp.int32, (tokens_here, tokens_here), 0)
        == lax.broadcasted_iota(jnp.int32, (tokens_here, tokens_here), 1)
    )
    chosen = by_rows(jnp.where(same, 1.0, 0.0).astype(half), marks.astype(half))
    chosen_kept[...] = chosen
    for part in range(parts):
        merge_far(part)
    for part in range(parts - 1):
        merge_own(part)
        share_own(part)
    merge_own(parts - 1)
    tokens = gathered[place, :, :out_width]

    logits = by_rows(tokens, router_ref[...])
    gates = chosen_kept[...] / (1.0 + jnp.exp(-logits))
    gate_sum = jnp.sum(jnp.where(lane < experts, gates, 0.0), axis=1, keepdims=True)
    route = route_scale * gates / gate_sum
    route_high = route.astype(half)
    route_low = (route - route_high.astype(f32)).astype(half)
    gathered[place, :, out_width:] = jnp.where(lane < experts, route_high.astype(f32), route_low.astype(f32)).astype(half)

    share_own(parts - 1)
    for part in range(parts - 1):
        forward_far(turn(1), part)
        forward_near(a, part)
        for step in range(2, far):
            forward_far(turn(step), part)
    for copy in weight_copies:
        copy.wait()

    def core_copy(a_index, side, piece):
        columns = columns_of(piece)
        return remote(
            expert_part.at[a_index, side, :, :, columns],
            core_recv.at[a_index, :, :, columns],
            c_send_sem.at[0],
            c_recv_sem.at[a_index, piece],
            other,
        )

    def y2_copy(a_index, step, slot, piece):
        target = lax.rem(b + step, near)
        columns = columns_of(piece)
        return remote(
            core_sum.at[a_index, target, :, columns],
            y2_recv.at[slot, a_index, :, columns],
            y2_send_sem.at[0],
            y2_recv_sem.at[slot, a_index, piece],
            at(a, target, core),
        )

    def z2_copy(a_index, slot, piece):
        columns = columns_of(piece)
        return remote(
            z2_send.at[a_index, :, columns],
            z2_recv.at[slot, :, columns],
            z2_send_sem.at[0],
            z2_recv_sem.at[slot, piece],
            at(a_index, b, core),
        )

    chunk = near * 2
    expert = place // 2

    def y2_start(a_index, piece):
        for step in near_steps:
            y2_copy(a_index, step, near - step - 1, piece).start()

    def join_cores(a_index, piece):
        columns = columns_of(piece)
        core_copy(a_index, 1 - core, piece).wait_recv()
        core_sum[a_index, :, :, columns] = (
            expert_part[a_index, core, :, :, columns].astype(f32)
            + core_recv[a_index, :, :, columns].astype(f32)
        ).astype(half)

    def y2_total(a_index, piece):
        columns = columns_of(piece)
        value = core_sum[a_index, b, :, columns].astype(f32)
        for step in near_steps:
            y2_copy(a_index, step, step - 1, piece).wait_recv()
            value = value + y2_recv[step - 1, a_index, :, columns].astype(f32)
        return value

    def join_near(a_index):
        for piece in range(pieces):
            z2_send[a_index, :, columns_of(piece)] = y2_total(a_index, piece).astype(half)
            z2_copy(a_index, a, piece).start()

    def chunks(step, carry):
        a_index = turn(step)

        @pl.when(step < far - 1)
        def _():
            forward_far(turn(step + 1), parts - 1)

        forward_near(a_index, parts - 1)

        @pl.when(step < far - 1)
        def _():
            for part in range(parts - 1):
                forward_near(turn(step + 1), part)

        @pl.when(step == 1)
        def _():
            for piece in range(pieces):
                join_cores(a, piece)

        @pl.when(step > 1)
        def _():
            previous = turn(step - 1)
            for piece in range(pieces):
                join_cores(previous, piece)
                y2_start(previous, piece)

        for part in range(parts):
            for b_index in range(near):
                arrived(at(a_index, b_index, 1 - core), part)
        slots = pl.ds(a_index * chunk, chunk)
        rows = gathered[slots, :, :out_width].reshape(chunk * tokens_here, out_width)
        table = gathered[slots, :, out_width:].reshape(chunk * tokens_here, lane_count).astype(f32)
        table_lane = lax.broadcasted_iota(jnp.int32, table.shape, 1)
        mine = jnp.logical_or(table_lane == expert, table_lane == expert + experts)
        scale = jnp.sum(jnp.where(mine, table, 0.0), axis=1, keepdims=True)
        gate_part = by_rows(rows, w_gate[...])
        up_part = by_rows(rows, w_up[...])
        hidden = (gate_part / (1.0 + jnp.exp(-gate_part)) * up_part).astype(half)

        for piece in range(pieces):
            columns = columns_of(piece)
            product = jnp.dot(hidden, w_down[:, columns], preferred_element_type=f32).astype(half)
            scaled = (product.astype(f32) * scale).astype(half)
            for b_index in range(near):
                for side in range(2):
                    start = (b_index * 2 + side) * tokens_here
                    expert_part[a_index, side, b_index, :, columns] = scaled[
                        start : start + tokens_here
                    ]
            core_copy(a_index, 1 - core, piece).start()

        @pl.when(step > 2)
        def _():
            join_near(turn(step - 2))

        return carry

    lax.fori_loop(0, far, chunks, 0)
    final = turn(far - 1)
    for piece in range(pieces):
        join_cores(final, piece)
        y2_start(final, piece)
    for piece in range(pieces):
        y2_start(a, piece)
    for step in range(max(1, far - 2), far):
        join_near(turn(step))
    for piece in range(pieces):
        columns = columns_of(piece)
        value = y2_total(a, piece)
        for step in range(1, far):
            z2_copy(turn(step), turn(step), piece).wait_recv()
            value = value + z2_recv[turn(step), :, columns].astype(f32)
        out_ref[:, columns] = value.astype(half)

    def sent(block, sem):
        remote(block, block, sem, w_recv_sem.at[0], other).wait_send()

    sent(part_send.at[pl.ds(0, far * (near - 1))], y_send_sem.at[0])
    sent(z_send.at[pl.ds(0, far - 1)], z_send_sem.at[0])
    sent(gathered.at[pl.ds(0, far - 1)], gz_send_sem.at[0])
    sent(gathered.at[pl.ds(0, far * (near - 1))], gy_send_sem.at[0])
    sent(gathered.at[pl.ds(0, chips)], gc_send_sem.at[0])
    sent(core_sum, c_send_sem.at[0])
    sent(y2_recv, y2_send_sem.at[0])
    sent(z2_send.at[pl.ds(0, far - 1)], z2_send_sem.at[0])


def layer_kernel(far, near, peers, head_dim, *refs):
    operands, out_ref, normed = refs[:11], refs[11], refs[12]
    grid_ref, gain_ref, bias_ref, ids_ref, named_ref, small_sem = refs[13:19]
    grid_hbm, qkv_hbm, w_out_hbm, gain_hbm, bias_hbm, ids_hbm, named_hbm = operands[:7]
    scratch = refs[19:]
    vision_scratch, language_scratch = scratch[:20], scratch[20:]
    place = lax.axis_index("wide")
    devices = lax.axis_size("wide")
    start = place // peers * peers
    clip_mates = [start + lax.rem(place - start + step, peers) for step in range(1, peers)]
    barrier = greet(clip_mates + [lax.rem(place + peers, devices)])
    fetches = [
        pltpu.make_async_copy(source, target, small_sem.at[index])
        for index, (source, target) in enumerate(
            [
                (named_hbm, named_ref),
                (grid_hbm, grid_ref),
                (gain_hbm, gain_ref),
                (bias_hbm, bias_ref),
                (ids_hbm, ids_ref),
            ]
        )
    ]

    def run_vision(start_rest):
        vision_part(
            peers,
            head_dim,
            barrier,
            grid_ref,
            qkv_hbm,
            w_out_hbm,
            gain_ref,
            bias_ref,
            normed,
            *vision_scratch,
            start_rest,
            fetches,
        )

    language_part(
        far,
        near,
        run_vision,
        normed,
        ids_ref,
        named_ref,
        *operands[7:],
        out_ref,
        *language_scratch,
    )


def fast_local(
    qkv,
    grid,
    w_out,
    ln_gain,
    ln_bias,
    w_merge,
    w_router,
    expert_ids,
    slot_pos,
    w_gate,
    w_up,
    w_down,
):
    devices = lax.axis_size("wide")
    peers = devices // CLIPS
    patch_rows = qkv.shape[0]
    width = w_out.shape[0]
    head_dim = width // HEADS
    heads = HEADS // peers
    span = heads * head_dim
    chips = devices // 2
    near = 1
    while 4 * near * near <= chips:
        near *= 2
    far = chips // near
    rows = patch_rows // 4
    depth, out_width = w_merge.shape
    experts = w_router.shape[1]
    lanes = -(-2 * experts // 128) * 128
    hidden = w_gate.shape[2]
    whole = pl.BlockSpec(memory_space=pltpu.VMEM)
    away = pl.BlockSpec(memory_space=pltpu.MemorySpace.HBM)
    half = jnp.bfloat16
    block = (rows, out_width)
    dma = pltpu.SemaphoreType.DMA
    pieces = out_width // min(1024, out_width)
    return pl.pallas_call(
        functools.partial(layer_kernel, far, near, peers, head_dim),
        out_shape=jax.ShapeDtypeStruct(block, half),
        in_specs=[away] * 11,
        out_specs=whole,
        scratch_shapes=[
            pltpu.VMEM((rows, 4 * width), half),
            pltpu.SMEM(grid.shape, jnp.int32),
            pltpu.VMEM((4 * width // 128, 128), jnp.float32),
            pltpu.VMEM((4 * width // 128, 128), jnp.float32),
            pltpu.VMEM(expert_ids.shape[::-1], jnp.int32),
            pltpu.VMEM((experts, out_width), half),
            dma((5,)),
            pltpu.VMEM((patch_rows, 3 * width), half),
            pltpu.VMEM((peers, 2 * (patch_rows + span - 128), 128), half),
            pltpu.VMEM((peers, 2 * (patch_rows + span - 128), 128), half),
            pltpu.VMEM((peers, patch_rows + span - 128, 128), half),
            pltpu.VMEM((peers, patch_rows + span - 128, 128), half),
            pltpu.VMEM((heads, peers * patch_rows, head_dim), half),
            pltpu.VMEM((heads, peers * patch_rows, head_dim), half),
            pltpu.VMEM((heads, peers * patch_rows, head_dim), half),
            pltpu.VMEM((heads, peers * patch_rows, peers * patch_rows), half),
            pltpu.VMEM((heads, peers * patch_rows, 1), jnp.float32),
            pltpu.VMEM((peers, patch_rows + span - 128, 128), half),
            pltpu.VMEM((peers, patch_rows + span - 128, 128), half),
            pltpu.VMEM((patch_rows, width), half),
            pltpu.VMEM((width // 128, patch_rows, 128), jnp.float32),
            pltpu.VMEM((width, width), half),
            dma((2,)),
            dma((2,)),
            dma((1,)),
            dma((1,)),
            dma((5,)),
            pltpu.VMEM((lanes, out_width), half),
            pltpu.VMEM((2 * depth, out_width), half),
            pltpu.VMEM((hidden, out_width), half),
            pltpu.VMEM((hidden, out_width), half),
            pltpu.VMEM((hidden, out_width), half),
            pltpu.VMEM((chips, rows * 2 * depth // 128, 128), half),
            pltpu.VMEM((chips, rows * 2 * depth // 128, 128), half),
            pltpu.VMEM((chips, *block), half),
            pltpu.VMEM((near - 1, far, *block), half),
            pltpu.VMEM((far, *block), half),
            pltpu.VMEM((far, *block), half),
            pltpu.VMEM((rows, lanes), jnp.float32),
            pltpu.VMEM((devices, rows, out_width + lanes), half),
            pltpu.VMEM((far, 2, near, *block), half),
            pltpu.VMEM((far, near, *block), half),
            pltpu.VMEM((far, near, *block), half),
            pltpu.VMEM((near - 1, far, *block), half),
            pltpu.VMEM((far, *block), half),
            pltpu.VMEM((far, *block), half),
            dma((5,)),
            dma((1,)),
            dma((1,)),
            dma((1,)),
            dma((1,)),
            dma((1,)),
            dma((near - 1, far, column_parts)),
            dma((1,)),
            dma((far, column_parts)),
            dma((devices, column_parts)),
            dma((1,)),
            dma((1,)),
            dma((1,)),
            dma((1,)),
            dma((far, pieces)),
            dma((1,)),
            dma((near - 1, far, pieces)),
            dma((1,)),
            dma((far, pieces)),
        ],
        compiler_params=pltpu.CompilerParams(
            collective_id=0, has_side_effects=True, vmem_limit_bytes=50 * 2**20
        ),
        name="layer",
    )(
        *[
            pltpu.with_memory_space_constraint(operand, pltpu.MemorySpace.HBM)
            for operand in (
                grid,
                qkv,
                w_out,
                ln_gain.reshape(-1, 128),
                ln_bias.reshape(-1, 128),
                expert_ids.T,
                w_router.T,
                w_merge,
                w_gate.swapaxes(1, 2),
                w_up.swapaxes(1, 2),
                w_down,
            )
        ]
    )


def either(*operands):
    devices = lax.axis_size("wide")
    qkv, w_router, expert_ids = operands[0], operands[6], operands[7]
    token_count = qkv.shape[0] // 4
    experts = w_router.shape[1]
    dense = 2 * token_count * expert_ids.shape[1] >= experts * token_count
    whole_heads = HEADS % (devices // CLIPS) == 0 and devices == 2 * experts
    if not (dense and whole_heads):
        return local(*operands)
    span = HEADS // (devices // CLIPS) * (operands[2].shape[0] // HEADS)
    packs = qkv.shape[0] == 128 and 128 < span < 256 and span % 16 == 0
    rest = 2 * operands[5].shape[0] % 128
    packs = packs and rest > 0 and 128 % rest == 0 and token_count * rest % 2048 == 0
    return fast_local(*operands) if packs else local(*operands)


def solution(mesh):
    placed = (
        P(("grp", "wide"), None),
        P("grp", None),
        P(),
        P(),
        P(),
        P("wide", None),
        P(),
        P(("grp", "wide"), None),
        P(("grp", "wide"), None),
        P("wide", None, None),
        P("wide", None, None),
        P("wide", None, None),
    )
    return jax.shard_map(
        either, mesh=mesh, in_specs=placed, out_specs=P(("grp", "wide"), None), check_vma=False
    )
```
